32 devices in a mesh: doc: 8 (over z, core), clu: 4 (over y, x).
Axes of the slice: x: 2, y: 2, z: 4, core: 2. Of those that a mesh axis runs over, the one named last changes fastest.
Arguments:
- embeddings: bfloat16 [4096, 256], P(('doc', 'clu')), may hold values from -16 to 16
- centroids: bfloat16 [4096, 256], P('clu'), may hold values from -1 to 1
Outputs:
- new_centroids: float32 [256, 4096], P('doc', 'clu')
- cluster_mass: float32 [4096], P('clu')
The draws below stay inside these ranges and needn't reach their ends.
All inputs are finite; a program needn't handle non-finite values.
Results may differ from the reference program's by a relative error of at most 0.0011.
Values may be sent and summed in bfloat16 or wider, within the bound.
A program may use at most 64 MiB of HBM per device.

```python
import math
import jax
import jax.numpy as jnp
from jax import lax

D = 256
K = 4096
ITERS = 2
DOCS = 4096


def shared_draw(key):
    normal_draw = jax.random.normal(jax.random.fold_in(key, 11), (K, D), jnp.float32)
    centers = jnp.clip(normal_draw, -4.0, 4.0) / jnp.sqrt(jnp.float32(D))
    features_raw = jnp.clip(jax.random.normal(jax.random.fold_in(key, 12), (DOCS, D), jnp.float32), -4.0, 4.0)
    column_scale = 10.0 ** (jnp.arange(D, dtype=jnp.float32) / D) * 0.2157
    embeds = features_raw * column_scale[None, :]
    return (embeds, centers)


def draw_embeddings(key, part):
    return shared_draw(key)[0].astype(jnp.bfloat16)


def draw_centroids(key, part):
    return shared_draw(key)[1].astype(jnp.bfloat16)


def setup_inputs(seed: int = 0) -> dict:
    seeds = jax.random.split(jax.random.key(seed), 3)
    return {
        "embeddings": draw_embeddings(jax.random.fold_in(seeds[2], 71), 0),
        "centroids": draw_centroids(jax.random.fold_in(seeds[2], 71), 0),
    }


entropic_smoothing = 0.05

def reference(embeddings, centroids):
    doc_total = embeddings.shape[0]
    features = embeddings.shape[1]
    cluster_labels = centroids.shape[0]
    block_size = math.gcd(doc_total, 4096)
    block_count = doc_total // block_size
    blocks = embeddings.reshape(block_count, block_size, features)
    log_docs = jnp.log(jnp.float32(doc_total))
    log_clusters = jnp.log(jnp.float32(cluster_labels))

    def scores_of(row_block):
        similarity_energy = lax.dot_general(row_block, centroids, (((1,), (1,)), ((), ())), preferred_element_type=jnp.float32)
        return similarity_energy / entropic_smoothing
    potential = jnp.zeros((block_count, block_size), jnp.float32)
    col_pot = jnp.zeros((cluster_labels,), jnp.float32)
    for iteration in range(ITERS):

        def column_step(state, inputs):
            similarity_energy = scores_of(inputs[0]) + inputs[1][:, None]
            highest = jnp.maximum(state[0], lax.optimization_barrier(jnp.max(similarity_energy, axis=0)))
            expsum = state[1] * jnp.exp(state[0] - highest) + lax.optimization_barrier(jnp.sum(jnp.exp(similarity_energy - highest[None, :]), axis=0))
            return ((highest, expsum), None)
        start_state = (jnp.full((cluster_labels,), -jnp.inf, jnp.float32), jnp.zeros((cluster_labels,), jnp.float32))
        final_state, unused = lax.scan(column_step, start_state, (blocks, potential))
        col_pot = -log_clusters - (final_state[0] + jnp.log(final_state[1]))

        def row_step(row_block):
            similarity_energy = scores_of(row_block) + col_pot[None, :]
            highest = lax.optimization_barrier(jnp.max(similarity_energy, axis=1))
            return -log_docs - (highest + jnp.log(lax.optimization_barrier(jnp.sum(jnp.exp(similarity_energy - highest[:, None]), axis=1))))
        potential = lax.map(row_step, blocks)

    def plan_step(state, inputs):
        plan = jnp.exp(scores_of(inputs[0]) + inputs[1][:, None] + col_pot[None, :] + log_docs)
        mass_part = state[1] + lax.optimization_barrier(jnp.sum(plan, axis=0))
        partial_sum = state[0] + lax.dot_general(inputs[0], plan.astype(jnp.bfloat16), (((0,), (0,)), ((), ())), preferred_element_type=jnp.float32)
        return ((partial_sum, mass_part), None)
    start_state = (jnp.zeros((features, cluster_labels), jnp.float32), jnp.zeros((cluster_labels,), jnp.float32))
    final_state, unused = lax.scan(plan_step, start_state, (blocks, potential))
    summed = final_state[0]
    mean_sq = lax.optimization_barrier(jnp.mean(summed * summed, axis=0))
    new_centroids = summed * lax.rsqrt(mean_sq + 1e-06)
    cluster_mass = final_state[1] * (jnp.float32(cluster_labels) / jnp.float32(doc_total))
    return (new_centroids, cluster_mass)
```

```python
import functools
import math

import jax
import jax.numpy as jnp
from jax import lax
from jax.experimental import pallas as pl
from jax.experimental.pallas import tpu as pltpu
from jax.sharding import PartitionSpec as P

ITERS = 2
SMOOTHING = 0.05
LOG2E = math.log2(math.e)
MESH = pl.DeviceIdType.MESH
F32 = jnp.float32


def scattered_kernel(
    nd, nc,
    emb_ref, cent_ref, out_ref, mass_ref,
    emb_all, centers, scores, plan, rpot, colbuf, rowbuf, massbuf, sqbuf, sums, rsbuf, tot, pairbuf,
    own_sem, cent_sem, emb_ss, emb_rs, fwd_ss, col_ss, col_rs, row_ss, row_rs,
    mass_ss, mass_rs, sq_ss, sq_rs, sum_ss, sum_rs, pair_ss, pair_rs,
):
    nz = nd // 2
    nb = 2 * nc
    rows, features = emb_ref.shape
    half = cent_ref.shape[0] // 2
    own_f = features // nd
    log_docs = math.log2(rows * nd * nc)
    log_clusters = math.log2(2 * half * nc)
    d = lax.axis_index("doc")
    c = lax.axis_index("clu")
    core = lax.rem(d, 2)
    z = lax.div(d, 2)
    partner = d + 1 - 2 * core
    me = core * nc + c

    def block_peer(k):
        peer = lax.rem(me + k, nb)
        return peer, (2 * z + lax.div(peer, nc), lax.rem(peer, nc))

    def z_peer(k):
        peer = lax.rem(z + k, nz)
        return peer, (2 * peer + core, c)

    def doc_peer(k):
        peer = lax.rem(d + k, nd)
        return peer, (peer, c)

    def remote(src, dst, ss, rs, device):
        return pltpu.make_async_remote_copy(
            src_ref=src, dst_ref=dst, send_sem=ss, recv_sem=rs,
            device_id=device, device_id_type=MESH,
        )

    sends = []

    def send(*args):
        copy = remote(*args)
        copy.start()
        sends.append(copy)

    own_copy = pltpu.make_async_copy(emb_ref, emb_all.at[me], own_sem)
    own_copy.start()
    cent_copy = pltpu.make_async_copy(
        cent_ref.at[pl.ds(pl.multiple_of(core * half, half), half), :], centers, cent_sem
    )
    cent_copy.start()
    barrier = pltpu.get_barrier_semaphore()
    for k in range(1, nb):
        pl.semaphore_signal(barrier, inc=1, device_id=block_peer(k)[1], device_id_type=MESH)
    for k in range(1, nd):
        pl.semaphore_signal(barrier, inc=1, device_id=doc_peer(k)[1], device_id_type=MESH)

    def col_update(state, t):
        high, total = state
        t = t.reshape(rows // 8, 8, half)
        new = jnp.maximum(high, jnp.max(t, axis=0))
        total = total * jnp.exp2(high - new) + jnp.sum(jnp.exp2(t - new[None]), axis=0)
        return new, total

    state = (jnp.full((8, half), -jnp.inf, F32), jnp.zeros((8, half), F32))

    def first_block(state, slot):
        s = lax.dot_general(
            emb_all[slot], centers[...], (((1,), (1,)), ((), ())), preferred_element_type=F32
        ) * (LOG2E / SMOOTHING)
        scores[slot] = s
        return col_update(state, s)

    def arrive(slot):
        remote(
            emb_all.at[slot], emb_all.at[slot], emb_ss.at[0], emb_rs.at[slot], (partner, c)
        ).wait_recv()

    def clu_peer(k):
        if nc & (nc - 1):
            return lax.rem(c + k, nc)
        bits = [1 << i for i in range(nc.bit_length() - 1)]
        return sum(lax.rem(lax.div(c, b) + k // b, 2) * b for b in bits)

    own_copy.wait()
    cent_copy.wait()
    state = first_block(state, me)
    pl.semaphore_wait(barrier, nb - 1 + nd - 1)

    own = emb_all.at[me]
    for k in reversed(range(1, nc)):
        send(own, own, emb_ss.at[k], emb_rs.at[me], (d, clu_peer(k)))
    send(own, own, emb_ss.at[0], emb_rs.at[me], (partner, c))
    other = 1 - core
    for k in range(1, nc):
        slot = core * nc + clu_peer(k)
        arrive(slot)
        send(emb_all.at[slot], emb_all.at[slot], fwd_ss.at[k], emb_rs.at[slot], (partner, c))
        state = first_block(state, slot)
    for k in range(nc):
        slot = other * nc + clu_peer(k)
        arrive(slot)
        state = first_block(state, slot)

    diagonal = lax.broadcasted_iota(jnp.int32, (rows, rows), 0) == lax.broadcasted_iota(
        jnp.int32, (rows, rows), 1
    )

    def to_lanes(x):
        return jnp.sum(jnp.where(diagonal, x, 0.0), axis=0, keepdims=True)

    def to_sublanes(x):
        return jnp.sum(jnp.where(diagonal, x, 0.0), axis=1, keepdims=True)

    def column_potential(it, state):
        high, total = state
        top = jnp.max(high, axis=0, keepdims=True)
        total = jnp.sum(total * jnp.exp2(high - top), axis=0, keepdims=True)
        colbuf[it, z] = top + jnp.log2(total)
        mine = colbuf.at[it, z]
        for k in range(1, nz):
            send(mine, mine, col_ss.at[it, k], col_rs.at[it, z], z_peer(k)[1])
        for k in range(1, nz):
            peer, device = z_peer(k)
            theirs = colbuf.at[it, peer]
            remote(theirs, theirs, col_ss.at[it, k], col_rs.at[it, peer], device).wait_recv()
        logs = [colbuf[it, s] for s in range(nz)]
        top = functools.reduce(jnp.maximum, logs)
        return -log_clusters - (top + jnp.log2(sum(jnp.exp2(x - top) for x in logs)))

    part = nb // 2

    def row_send(it, h, col_pot):
        def block(b, carry):
            t = scores[h * part + b] + col_pot
            high = jnp.max(t, axis=1, keepdims=True)
            total = jnp.sum(jnp.exp2(t - high), axis=1, keepdims=True)
            rowbuf[it, h, me, pl.ds(b, 1), :] = to_lanes(high + jnp.log2(total))
            return carry

        lax.fori_loop(0, part, block, 0, unroll=4)
        mine = rowbuf.at[it, h, me]
        for k in range(1, nb):
            send(mine, mine, row_ss.at[it, h, k], row_rs.at[it, h, me], block_peer(k)[1])

    def row_receive(it, h):
        for k in range(1, nb):
            peer, device = block_peer(k)
            theirs = rowbuf.at[it, h, peer]
            remote(
                theirs, theirs, row_ss.at[it, h, k], row_rs.at[it, h, peer], device
            ).wait_recv()
        logs = rowbuf[it, h]
        top = jnp.max(logs, axis=0)
        total = jnp.sum(jnp.exp2(logs - top[None]), axis=0)
        rpot[h] = -log_docs - (top + jnp.log2(total))

    for it in range(ITERS):
        if it > 0:
            state = (jnp.full((8, half), -jnp.inf, F32), jnp.zeros((8, half), F32))
            for h in range(2):
                def again(b, state):
                    t = scores[h * part + b] + to_sublanes(rpot[h, pl.ds(b, 1), :])
                    return col_update(state, t)

                row_receive(it - 1, h)
                state = lax.fori_loop(0, part, again, state, unroll=4)
        col_pot = column_potential(it, state)
        for h in range(2):
            row_send(it, h, col_pot)

    mass = jnp.zeros((8, half), F32)
    for h in range(2):
        def plan_block(b, mass):
            t = scores[h * part + b] + to_sublanes(rpot[h, pl.ds(b, 1), :]) + col_pot + log_docs
            p = jnp.exp2(t)
            plan[h, pl.ds(pl.multiple_of(b * rows, rows), rows), :] = p.astype(jnp.bfloat16)
            return mass + jnp.sum(p.reshape(rows // 8, 8, half), axis=0)

        row_receive(ITERS - 1, h)
        mass = lax.fori_loop(0, part, plan_block, mass, unroll=4)
        product = lax.dot_general(
            emb_all[h * part:(h + 1) * part].reshape(part * rows, features), plan[h],
            (((0,), (0,)), ((), ())), preferred_element_type=F32,
        )
        sums[...] = product if h == 0 else sums[...] + product
    massbuf[d] = jnp.sum(mass, axis=0, keepdims=True)
    far = sorted(range(1, nz), key=lambda k: -min(k, nz - k))

    def share(peer):
        return sums.at[pl.ds(pl.multiple_of(peer * 2 * own_f, 2 * own_f), 2 * own_f), :]

    for k in far:
        peer, device = z_peer(k)
        send(share(peer), rsbuf.at[z], sum_ss.at[k], sum_rs.at[z], device)
    for k in range(1, nd):
        send(massbuf.at[d], massbuf.at[d], mass_ss.at[k], mass_rs.at[d], doc_peer(k)[1])
    total = share(z)[...]
    for k in reversed(far):
        peer, device = z_peer(k)
        remote(share(z), rsbuf.at[peer], sum_ss.at[k], sum_rs.at[peer], device).wait_recv()
        total = total + rsbuf[peer]
    tot[...] = total
    sqbuf[d] = jnp.sum(total * total, axis=0, keepdims=True)

    def features_of(which):
        return tot.at[pl.ds(pl.multiple_of(which * own_f, own_f), own_f), :]

    for k in range(1, nd):
        send(sqbuf.at[d], sqbuf.at[d], sq_ss.at[k], sq_rs.at[d], doc_peer(k)[1])
    send(features_of(other), pairbuf, pair_ss, pair_rs, (partner, c))
    for k in range(1, nd):
        peer, device = doc_peer(k)
        theirs = massbuf.at[peer]
        remote(theirs, theirs, mass_ss.at[k], mass_rs.at[peer], device).wait_recv()
        theirs = sqbuf.at[peer]
        remote(theirs, theirs, sq_ss.at[k], sq_rs.at[peer], device).wait_recv()
    remote(features_of(core), pairbuf, pair_ss, pair_rs, (partner, c)).wait_recv()

    def finish(which, block):
        columns = pl.ds(pl.multiple_of(which * half, half), half)
        squares = sum(sqbuf[2 * s + which] for s in range(nz))
        out_ref[:, columns] = block * lax.rsqrt(squares / features + 1e-06)
        mass_ref[:, columns] = sum(massbuf[2 * s + which] for s in range(nz)) * (
            2 * half * nc / (rows * nd * nc)
        )

    finish(core, features_of(core)[...])
    finish(other, pairbuf[...])
    for copy in sends:
        copy.wait_send()


def scattered(nd, nc, embeddings, centroids):
    rows, features = embeddings.shape
    own_cols = centroids.shape[0]
    half, nz, nb = own_cols // 2, nd // 2, 2 * nc
    own_f = features // nd
    dma = pltpu.SemaphoreType.DMA
    out, mass = pl.pallas_call(
        functools.partial(scattered_kernel, nd, nc),
        out_shape=(
            jax.ShapeDtypeStruct((own_f, own_cols), F32),
            jax.ShapeDtypeStruct((1, own_cols), F32),
        ),
        in_specs=[pl.BlockSpec(memory_space=pltpu.HBM)] * 2,
        out_specs=(pl.BlockSpec(memory_space=pltpu.VMEM),) * 2,
        scratch_shapes=[
            pltpu.VMEM((nb, rows, features), jnp.bfloat16),
            pltpu.VMEM((half, features), jnp.bfloat16),
            pltpu.VMEM((nb, rows, half), F32),
            pltpu.VMEM((2, nc * rows, half), jnp.bfloat16),
            pltpu.VMEM((2, nc, rows), F32),
            pltpu.VMEM((ITERS, nz, 1, half), F32),
            pltpu.VMEM((ITERS, 2, nb, nc, rows), F32),
            pltpu.VMEM((nd, 1, half), F32),
            pltpu.VMEM((nd, 1, half), F32),
            pltpu.VMEM((features, half), F32),
            pltpu.VMEM((nz, 2 * own_f, half), F32),
            pltpu.VMEM((2 * own_f, half), F32),
            pltpu.VMEM((own_f, half), F32),
            dma, dma, dma((nc,)), dma((nb,)), dma((nc,)),
            dma((ITERS, nz)), dma((ITERS, nz)), dma((ITERS, 2, nb)), dma((ITERS, 2, nb)),
            dma((nd,)), dma((nd,)), dma((nd,)), dma((nd,)),
            dma((nz,)), dma((nz,)), dma, dma,
        ],
        compiler_params=pltpu.CompilerParams(
            collective_id=0, has_side_effects=True
        ),
    )(embeddings, centroids)
    return out, mass.reshape(own_cols)


def replicated_kernel(
    nd, nc,
    emb_ref, cent_ref, out_ref, mass_ref,
    emb_all, centers, scores, plan, high, total, wide, rpot, zpot, colbuf, rowbuf, sums, finished, pairbuf, pairmass,
    own_sem, cent_sem, own_ss, emb_rs, core_ss, plane_ss, col_ss, col_rs, row_ss, row_rs,
    zp_ss, zp_rs, pair_ss, pair_rs,
):
    nz = nd // 2
    nb = 2 * nc
    rows, features = emb_ref.shape
    half = cent_ref.shape[0] // 2
    own_f = features // nd
    docs, clusters = rows * nd * nc, 2 * half * nc
    log_docs, log_clusters = math.log2(docs), math.log2(clusters)
    d = lax.axis_index("doc")
    c = lax.axis_index("clu")
    core = lax.rem(d, 2)
    other = 1 - core
    z = lax.div(d, 2)
    partner = d + other - core
    me = core * nc + c
    step = min(half, 64)
    tiles = step // 8

    def paired(i, k, n):
        if n & (n - 1):
            return lax.rem(i + k, n)
        bits = [1 << b for b in range(n.bit_length() - 1)]
        return sum(lax.rem(lax.div(i, b) + k // b, 2) * b for b in bits)

    def block_peer(k):
        peer = paired(me, k, nb)
        return peer, (2 * z + lax.div(peer, nc), lax.rem(peer, nc))

    def clu_peer(k):
        return paired(c, k, nc)

    def z_peer(k):
        return paired(z, k, nz)

    def slot_of(plane, side, cluster):
        return plane * nb + side * nc + cluster

    def remote(src, dst, ss, rs, device):
        return pltpu.make_async_remote_copy(
            src_ref=src, dst_ref=dst, send_sem=ss, recv_sem=rs,
            device_id=device, device_id_type=MESH,
        )

    sends = []

    def send(*args):
        copy = remote(*args)
        copy.start()
        sends.append(copy)

    mine = slot_of(z, core, c)
    own = emb_all.at[mine]
    own_copy = pltpu.make_async_copy(emb_ref, own, own_sem)
    own_copy.start()
    cent_copy = pltpu.make_async_copy(
        cent_ref.at[pl.ds(pl.multiple_of(core * half, half), half), :], centers, cent_sem
    )
    cent_copy.start()
    barrier = pltpu.get_barrier_semaphore()
    for k in range(1, nb):
        pl.semaphore_signal(barrier, inc=1, device_id=block_peer(k)[1], device_id_type=MESH)
    for k in range(1, nz):
        pl.semaphore_signal(
            barrier, inc=1, device_id=(2 * z_peer(k) + core, c), device_id_type=MESH
        )

    def score(slot):
        return lax.dot_general(
            centers[...], emb_all[slot], (((1,), (1,)), ((), ())), preferred_element_type=F32
        ) * (LOG2E / SMOOTHING)

    def arrive(slot):
        remote(
            emb_all.at[slot], emb_all.at[slot], own_ss.at[0], emb_rs.at[slot], (partner, c)
        ).wait_recv()

    def to_partner(slot, k):
        send(emb_all.at[slot], emb_all.at[slot], core_ss.at[k], emb_rs.at[slot], (partner, c))

    def to_plane(slot, k):
        for j in reversed(range(1, nc)):
            send(
                emb_all.at[slot], emb_all.at[slot], plane_ss.at[k, j], emb_rs.at[slot],
                (d, clu_peer(j)),
            )

    def plane_scores(k):
        def body(b, carry):
            slot = z_peer(k) * nb + b
            scores[slot] = score(slot) + wide[...]
            return carry

        for j in range(nc):
            arrive(slot_of(z_peer(k), other, clu_peer(j)))
        lax.fori_loop(0, nb, body, 0, unroll=2)

    def piece(g):
        return pl.ds(pl.multiple_of(g * step, step), step)

    def column_update(slots, first):
        def body(g, carry):
            at = piece(g)
            ts = [scores[s, at, :] for s in slots]
            old = None if first else high[at, :]
            new = functools.reduce(jnp.maximum, ts if first else ts + [old])
            part = sum(jnp.exp2(t - new) for t in ts)
            total[at, :] = part if first else part + total[at, :] * jnp.exp2(old - new)
            high[at, :] = new
            return carry

        lax.fori_loop(0, half // step, body, 0, unroll=2)

    own_copy.wait()
    cent_copy.wait()
    scores[mine] = score(mine)
    pl.semaphore_wait(barrier, nb - 1 + nz - 1)

    to_plane(mine, 0)
    to_partner(mine, 0)
    for k in range(1, nz):
        send(own, own, own_ss.at[k], emb_rs.at[mine], (2 * z_peer(k) + core, c))
    column_update([mine], True)
    for k in range(1, nc):
        slot = slot_of(z, core, clu_peer(k))
        arrive(slot)
        to_partner(slot, k)
        scores[slot] = score(slot)
    column_update([slot_of(z, core, clu_peer(k)) for k in range(1, nc)], False)

    def from_plane(k):
        slot = slot_of(z_peer(k), core, c)
        arrive(slot)
        to_plane(slot, k)
        to_partner(slot, k * nc)

    def across(k):
        for j in range(1, nc):
            slot = slot_of(z_peer(k), core, clu_peer(j))
            arrive(slot)
            to_partner(slot, k * nc + j)

    early = list(range(1, nz))[:-1]
    late = list(range(1, nz))[-1:]
    for k in early[:1]:
        from_plane(k)
    for k in range(nc):
        slot = slot_of(z, other, clu_peer(k))
        arrive(slot)
        scores[slot] = score(slot)
        if k % 2:
            column_update([slot_of(z, other, clu_peer(k - 1)), slot], False)
    if nc % 2:
        column_update([slot_of(z, other, clu_peer(nc - 1))], False)

    def spread(x):
        wide[...] = jnp.transpose(jnp.broadcast_to(x, (rows, half)))

    def column_send(it, x):
        colbuf[it, z] = x
        ref = colbuf.at[it, z]
        for k in range(1, nz):
            send(ref, ref, col_ss.at[it, k], col_rs.at[it, z], (2 * z_peer(k) + core, c))

    def column_receive(it):
        for k in range(1, nz):
            theirs = colbuf.at[it, z_peer(k)]
            remote(
                theirs, theirs, col_ss.at[it, k], col_rs.at[it, z_peer(k)], (partner, c)
            ).wait_recv()
        return [colbuf[it, s] for s in range(nz)]

    def row_send(it):
        ref = rowbuf.at[it, me]
        for k in range(1, nb):
            send(ref, ref, row_ss.at[it, k], row_rs.at[it, me], block_peer(k)[1])

    def row_receive(it):
        for k in range(1, nb):
            peer, device = block_peer(k)
            theirs = rowbuf.at[it, peer]
            remote(theirs, theirs, row_ss.at[it, k], row_rs.at[it, peer], device).wait_recv()
        return [rowbuf[it, s] for s in range(nb)]

    def folded(x, op):
        return functools.reduce(op, [x[8 * i:8 * i + 8] for i in range(tiles)])

    def row_first(b, carry):
        slot = z * nb + b
        top = jnp.full((8, rows), -jnp.inf, F32)
        for g in range(half // step):
            at = pl.ds(g * step, step)
            t = scores[slot, at, :] + wide[at, :]
            scores[slot, at, :] = t
            top = jnp.maximum(top, folded(t, jnp.maximum))
        top = jnp.max(top, axis=0, keepdims=True)
        acc = jnp.zeros((8, rows), F32)
        for g in range(half // step):
            at = pl.ds(g * step, step)
            acc = acc + folded(jnp.exp2(scores[slot, at, :] - top), jnp.add)
        rowbuf[0, me, pl.ds(b, 1), :] = top + jnp.log2(jnp.sum(acc, axis=0, keepdims=True))
        return carry

    def row_next(it, b, carry):
        slot = z * nb + b
        r = rpot[pl.ds(b, 1), :]
        acc = jnp.zeros((8, rows), F32)
        for g in range(half // step):
            at = pl.ds(g * step, step)
            t = scores[slot, at, :] + wide[at, :]
            scores[slot, at, :] = t
            acc = acc + folded(jnp.exp2(t + r), jnp.add)
        rowbuf[it, me, pl.ds(b, 1), :] = jnp.sum(acc, axis=0, keepdims=True)
        return carry

    def column_next(g, carry):
        at = piece(g)
        acc = jnp.zeros((step, rows), F32)
        for b in range(nb):
            acc = acc + jnp.exp2(scores[z * nb + b, at, :] + rpot[pl.ds(b, 1), :])
        total[at, :] = acc
        return carry

    tops = jnp.transpose(high[...])
    top = jnp.max(tops, axis=0, keepdims=True)
    column_send(
        0,
        top + jnp.log2(
            jnp.sum(jnp.transpose(total[...]) * jnp.exp2(tops - top), axis=0, keepdims=True)
        ),
    )
    for k in early[1:]:
        from_plane(k)
    logs = column_receive(0)
    top = functools.reduce(jnp.maximum, logs)
    col_pot = -log_clusters - (top + jnp.log2(sum(jnp.exp2(x - top) for x in logs)))
    spread(col_pot)
    lax.fori_loop(0, nb, row_first, 0, unroll=2)
    row_send(0)
    for k in early:
        across(k)
    logs = row_receive(0)
    top = functools.reduce(jnp.maximum, logs)
    rpot[...] = -log_docs - (top + jnp.log2(sum(jnp.exp2(x - top) for x in logs)))

    for it in range(1, ITERS):
        lax.fori_loop(0, half // step, column_next, 0, unroll=2)
        column_send(it, jnp.sum(jnp.transpose(total[...]), axis=0, keepdims=True))
        if it == 1:
            for k in late:
                from_plane(k)
        change = -log_clusters - jnp.log2(sum(column_receive(it)))
        col_pot = col_pot + change
        spread(change)
        lax.fori_loop(0, nb, functools.partial(row_next, it), 0, unroll=2)
        row_send(it)
        if it == 1:
            for k in late:
                across(k)
        if it == ITERS - 1:
            spread(col_pot)
        for k in early if it == ITERS - 1 else ():
            plane_scores(k)
        rpot[...] = rpot[...] - log_docs - jnp.log2(sum(row_receive(it)))

    zpot[z] = rpot[...] + log_docs
    ref = zpot.at[z]
    for k in range(1, nz):
        send(ref, ref, zp_ss.at[k], zp_rs.at[z], (2 * z_peer(k) + core, c))

    def plane_plan(plane, first):
        def body(g, carry):
            at = piece(g)
            acc = jnp.zeros((step, rows), F32)
            for b in range(nb):
                p = jnp.exp2(scores[plane * nb + b, at, :] + zpot[plane, pl.ds(b, 1), :])
                plan[at, b * rows:(b + 1) * rows] = p.astype(jnp.bfloat16)
                acc = acc + p
            total[at, :] = acc if first else acc + total[at, :]
            return carry

        lax.fori_loop(0, half // step, body, 0, unroll=2)
        product = lax.dot_general(
            plan[...], emb_all[pl.ds(plane * nb, nb)].reshape(nb * rows, features),
            (((1,), (0,)), ((), ())), preferred_element_type=F32,
        )
        sums[...] = product if first else sums[...] + product

    plane_plan(z, True)
    for k in late:
        plane_scores(k)
    for k in range(1, nz):
        plane = z_peer(k)
        theirs = zpot.at[plane]
        remote(theirs, theirs, zp_ss.at[k], zp_rs.at[plane], (partner, c)).wait_recv()
        plane_plan(plane, False)

    everything = jnp.transpose(sums[...])
    scale = lax.rsqrt(jnp.sum(everything * everything, axis=0, keepdims=True) / features + 1e-06)
    finished[...] = everything * scale
    pairmass[0] = jnp.sum(jnp.transpose(total[...]), axis=0, keepdims=True) * (clusters / docs)

    def features_of(which):
        return finished.at[pl.ds(pl.multiple_of((2 * z + which) * own_f, own_f), own_f), :]

    send(features_of(other), pairbuf, pair_ss.at[0], pair_rs.at[0], (partner, c))
    send(pairmass.at[0], pairmass.at[1], pair_ss.at[1], pair_rs.at[1], (partner, c))
    columns = pl.ds(pl.multiple_of(core * half, half), half)
    out_ref[:, columns] = features_of(core)[...]
    mass_ref[:, columns] = pairmass[0]
    columns = pl.ds(pl.multiple_of(other * half, half), half)
    remote(pairbuf, pairbuf, pair_ss.at[0], pair_rs.at[0], (partner, c)).wait_recv()
    out_ref[:, columns] = pairbuf[...]
    remote(
        pairmass.at[1], pairmass.at[1], pair_ss.at[1], pair_rs.at[1], (partner, c)
    ).wait_recv()
    mass_ref[:, columns] = pairmass[1]
    for copy in sends:
        copy.wait_send()


def replicated(nd, nc, embeddings, centroids):
    rows, features = embeddings.shape
    own_cols = centroids.shape[0]
    half, nz, nb = own_cols // 2, nd // 2, 2 * nc
    own_f = features // nd
    dma = pltpu.SemaphoreType.DMA
    out, mass = pl.pallas_call(
        functools.partial(replicated_kernel, nd, nc),
        out_shape=(
            jax.ShapeDtypeStruct((own_f, own_cols), F32),
            jax.ShapeDtypeStruct((1, own_cols), F32),
        ),
        in_specs=[pl.BlockSpec(memory_space=pltpu.HBM)] * 2,
        out_specs=(pl.BlockSpec(memory_space=pltpu.VMEM),) * 2,
        scratch_shapes=[
            pltpu.VMEM((nz * nb, rows, features), jnp.bfloat16),
            pltpu.VMEM((half, features), jnp.bfloat16),
            pltpu.VMEM((nz * nb, half, rows), F32),
            pltpu.VMEM((half, nb * rows), jnp.bfloat16),
            pltpu.VMEM((half, rows), F32),
            pltpu.VMEM((half, rows), F32),
            pltpu.VMEM((half, rows), F32),
            pltpu.VMEM((nb, rows), F32),
            pltpu.VMEM((nz, nb, rows), F32),
            pltpu.VMEM((ITERS, nz, 1, half), F32),
            pltpu.VMEM((ITERS, nb, nb, rows), F32),
            pltpu.VMEM((half, features), F32),
            pltpu.VMEM((features, half), F32),
            pltpu.VMEM((own_f, half), F32),
            pltpu.VMEM((2, 1, half), F32),
            dma, dma, dma((nz,)), dma((nz * nb,)), dma((nz * nc,)), dma((nz, nc)),
            dma((ITERS, nz)), dma((ITERS, nz)), dma((ITERS, nb)), dma((ITERS, nb)),
            dma((nz,)), dma((nz,)), dma((2,)), dma((2,)),
        ],
        compiler_params=pltpu.CompilerParams(
            collective_id=0, has_side_effects=True, vmem_limit_bytes=VMEM_BYTES
        ),
    )(embeddings, centroids)
    return out, mass.reshape(own_cols)


VMEM_BYTES = 48 << 20


def local(nd, nc, embeddings, centroids):
    rows, features = embeddings.shape
    docs = rows * nd * nc
    half = centroids.shape[0] // 2
    held = docs * (2 * features + 4 * half)
    form = replicated if 2 * held <= VMEM_BYTES else scattered
    return form(nd, nc, embeddings, centroids)


def solution(mesh):
    placed = (P(("doc", "clu"), None), P("clu", None))
    body = functools.partial(local, mesh.shape["doc"], mesh.shape["clu"])
    return jax.shard_map(
        body, mesh=mesh, in_specs=placed, out_specs=(P("doc", "clu"), P("clu")), check_vma=False
    )
```

```python
import functools
import math

import jax
import jax.numpy as jnp
from jax import lax
from jax.experimental import pallas as pl
from jax.experimental.pallas import tpu as pltpu
from jax.sharding import PartitionSpec as P

ITERS = 2
SMOOTHING = 0.05
LOG2E = math.log2(math.e)
MESH = pl.DeviceIdType.MESH
F32 = jnp.float32


def scattered_kernel(
    nd, nc,
    emb_ref, cent_ref, out_ref, mass_ref,
    emb_all, centers, scores, plan, rpot, colbuf, rowbuf, massbuf, sqbuf, sums, rsbuf, tot, pairbuf,
    own_sem, cent_sem, emb_ss, emb_rs, fwd_ss, col_ss, col_rs, row_ss, row_rs,
    mass_ss, mass_rs, sq_ss, sq_rs, sum_ss, sum_rs, pair_ss, pair_rs,
):
    nz = nd // 2
    nb = 2 * nc
    rows, features = emb_ref.shape
    half = cent_ref.shape[0] // 2
    own_f = features // nd
    log_docs = math.log2(rows * nd * nc)
    log_clusters = math.log2(2 * half * nc)
    d = lax.axis_index("doc")
    c = lax.axis_index("clu")
    core = lax.rem(d, 2)
    z = lax.div(d, 2)
    partner = d + 1 - 2 * core
    me = core * nc + c

    def block_peer(k):
        peer = lax.rem(me + k, nb)
        return peer, (2 * z + lax.div(peer, nc), lax.rem(peer, nc))

    def z_peer(k):
        peer = lax.rem(z + k, nz)
        return peer, (2 * peer + core, c)

    def doc_peer(k):
        peer = lax.rem(d + k, nd)
        return peer, (peer, c)

    def remote(src, dst, ss, rs, device):
        return pltpu.make_async_remote_copy(
            src_ref=src, dst_ref=dst, send_sem=ss, recv_sem=rs,
            device_id=device, device_id_type=MESH,
        )

    sends = []

    def send(*args):
        copy = remote(*args)
        copy.start()
        sends.append(copy)

    own_copy = pltpu.make_async_copy(emb_ref, emb_all.at[me], own_sem)
    own_copy.start()
    cent_copy = pltpu.make_async_copy(
        cent_ref.at[pl.ds(pl.multiple_of(core * half, half), half), :], centers, cent_sem
    )
    cent_copy.start()
    barrier = pltpu.get_barrier_semaphore()
    for k in range(1, nb):
        pl.semaphore_signal(barrier, inc=1, device_id=block_peer(k)[1], device_id_type=MESH)
    for k in range(1, nd):
        pl.semaphore_signal(barrier, inc=1, device_id=doc_peer(k)[1], device_id_type=MESH)

    def col_update(state, t):
        high, total = state
        t = t.reshape(rows // 8, 8, half)
        new = jnp.maximum(high, jnp.max(t, axis=0))
        total = total * jnp.exp2(high - new) + jnp.sum(jnp.exp2(t - new[None]), axis=0)
        return new, total

    state = (jnp.full((8, half), -jnp.inf, F32), jnp.zeros((8, half), F32))

    def first_block(state, slot):
        s = lax.dot_general(
            emb_all[slot], centers[...], (((1,), (1,)), ((), ())), preferred_element_type=F32
        ) * (LOG2E / SMOOTHING)
        scores[slot] = s
        return col_update(state, s)

    def arrive(slot):
        remote(
            emb_all.at[slot], emb_all.at[slot], emb_ss.at[0], emb_rs.at[slot], (partner, c)
        ).wait_recv()

    def clu_peer(k):
        if nc & (nc - 1):
            return lax.rem(c + k, nc)
        bits = [1 << i for i in range(nc.bit_length() - 1)]
        return sum(lax.rem(lax.div(c, b) + k // b, 2) * b for b in bits)

    own_copy.wait()
    cent_copy.wait()
    state = first_block(state, me)
    pl.semaphore_wait(barrier, nb - 1 + nd - 1)

    own = emb_all.at[me]
    for k in reversed(range(1, nc)):
        send(own, own, emb_ss.at[k], emb_rs.at[me], (d, clu_peer(k)))
    send(own, own, emb_ss.at[0], emb_rs.at[me], (partner, c))
    other = 1 - core
    for k in range(1, nc):
        slot = core * nc + clu_peer(k)
        arrive(slot)
        send(emb_all.at[slot], emb_all.at[slot], fwd_ss.at[k], emb_rs.at[slot], (partner, c))
        state = first_block(state, slot)
    for k in range(nc):
        slot = other * nc + clu_peer(k)
        arrive(slot)
        state = first_block(state, slot)

    diagonal = lax.broadcasted_iota(jnp.int32, (rows, rows), 0) == lax.broadcasted_iota(
        jnp.int32, (rows, rows), 1
    )

    def to_lanes(x):
        return jnp.sum(jnp.where(diagonal, x, 0.0), axis=0, keepdims=True)

    def to_sublanes(x):
        return jnp.sum(jnp.where(diagonal, x, 0.0), axis=1, keepdims=True)

    def column_potential(it, state):
        high, total = state
        top = jnp.max(high, axis=0, keepdims=True)
        total = jnp.sum(total * jnp.exp2(high - top), axis=0, keepdims=True)
        colbuf[it, z] = top + jnp.log2(total)
        mine = colbuf.at[it, z]
        for k in range(1, nz):
            send(mine, mine, col_ss.at[it, k], col_rs.at[it, z], z_peer(k)[1])
        for k in range(1, nz):
            peer, device = z_peer(k)
            theirs = colbuf.at[it, peer]
            remote(theirs, theirs, col_ss.at[it, k], col_rs.at[it, peer], device).wait_recv()
        logs = [colbuf[it, s] for s in range(nz)]
        top = functools.reduce(jnp.maximum, logs)
        return -log_clusters - (top + jnp.log2(sum(jnp.exp2(x - top) for x in logs)))

    part = nb // 2

    def row_send(it, h, col_pot):
        def block(b, carry):
            t = scores[h * part + b] + col_pot
            high = jnp.max(t, axis=1, keepdims=True)
            total = jnp.sum(jnp.exp2(t - high), axis=1, keepdims=True)
            rowbuf[it, h, me, pl.ds(b, 1), :] = to_lanes(high + jnp.log2(total))
            return carry

        lax.fori_loop(0, part, block, 0, unroll=4)
        mine = rowbuf.at[it, h, me]
        for k in range(1, nb):
            send(mine, mine, row_ss.at[it, h, k], row_rs.at[it, h, me], block_peer(k)[1])

    def row_receive(it, h):
        for k in range(1, nb):
            peer, device = block_peer(k)
            theirs = rowbuf.at[it, h, peer]
            remote(
                theirs, theirs, row_ss.at[it, h, k], row_rs.at[it, h, peer], device
            ).wait_recv()
        logs = rowbuf[it, h]
        top = jnp.max(logs, axis=0)
        total = jnp.sum(jnp.exp2(logs - top[None]), axis=0)
        rpot[h] = -log_docs - (top + jnp.log2(total))

    for it in range(ITERS):
        if it > 0:
            state = (jnp.full((8, half), -jnp.inf, F32), jnp.zeros((8, half), F32))
            for h in range(2):
                def again(b, state):
                    t = scores[h * part + b] + to_sublanes(rpot[h, pl.ds(b, 1), :])
                    return col_update(state, t)

                row_receive(it - 1, h)
                state = lax.fori_loop(0, part, again, state, unroll=4)
        col_pot = column_potential(it, state)
        for h in range(2):
            row_send(it, h, col_pot)

    mass = jnp.zeros((8, half), F32)
    for h in range(2):
        def plan_block(b, mass):
            t = scores[h * part + b] + to_sublanes(rpot[h, pl.ds(b, 1), :]) + col_pot + log_docs
            p = jnp.exp2(t)
            plan[h, pl.ds(pl.multiple_of(b * rows, rows), rows), :] = p.astype(jnp.bfloat16)
            return mass + jnp.sum(p.reshape(rows // 8, 8, half), axis=0)

        row_receive(ITERS - 1, h)
        mass = lax.fori_loop(0, part, plan_block, mass, unroll=4)
        product = lax.dot_general(
            emb_all[h * part:(h + 1) * part].reshape(part * rows, features), plan[h],
            (((0,), (0,)), ((), ())), preferred_element_type=F32,
        )
        sums[...] = product if h == 0 else sums[...] + product
    massbuf[d] = jnp.sum(mass, axis=0, keepdims=True)
    far = sorted(range(1, nz), key=lambda k: -min(k, nz - k))

    def share(peer):
        return sums.at[pl.ds(pl.multiple_of(peer * 2 * own_f, 2 * own_f), 2 * own_f), :]

    for k in far:
        peer, device = z_peer(k)
        send(share(peer), rsbuf.at[z], sum_ss.at[k], sum_rs.at[z], device)
    for k in range(1, nd):
        send(massbuf.at[d], massbuf.at[d], mass_ss.at[k], mass_rs.at[d], doc_peer(k)[1])
    total = share(z)[...]
    for k in reversed(far):
        peer, device = z_peer(k)
        remote(share(z), rsbuf.at[peer], sum_ss.at[k], sum_rs.at[peer], device).wait_recv()
        total = total + rsbuf[peer]
    tot[...] = total
    sqbuf[d] = jnp.sum(total * total, axis=0, keepdims=True)

    def features_of(which):
        return tot.at[pl.ds(pl.multiple_of(which * own_f, own_f), own_f), :]

    for k in range(1, nd):
        send(sqbuf.at[d], sqbuf.at[d], sq_ss.at[k], sq_rs.at[d], doc_peer(k)[1])
    send(features_of(other), pairbuf, pair_ss, pair_rs, (partner, c))
    for k in range(1, nd):
        peer, device = doc_peer(k)
        theirs = massbuf.at[peer]
        remote(theirs, theirs, mass_ss.at[k], mass_rs.at[peer], device).wait_recv()
        theirs = sqbuf.at[peer]
        remote(theirs, theirs, sq_ss.at[k], sq_rs.at[peer], device).wait_recv()
    remote(features_of(core), pairbuf, pair_ss, pair_rs, (partner, c)).wait_recv()

    def finish(which, block):
        columns = pl.ds(pl.multiple_of(which * half, half), half)
        squares = sum(sqbuf[2 * s + which] for s in range(nz))
        out_ref[:, columns] = block * lax.rsqrt(squares / features + 1e-06)
        mass_ref[:, columns] = sum(massbuf[2 * s + which] for s in range(nz)) * (
            2 * half * nc / (rows * nd * nc)
        )

    finish(core, features_of(core)[...])
    finish(other, pairbuf[...])
    for copy in sends:
        copy.wait_send()


def scattered(nd, nc, embeddings, centroids):
    rows, features = embeddings.shape
    own_cols = centroids.shape[0]
    half, nz, nb = own_cols // 2, nd // 2, 2 * nc
    own_f = features // nd
    dma = pltpu.SemaphoreType.DMA
    out, mass = pl.pallas_call(
        functools.partial(scattered_kernel, nd, nc),
        out_shape=(
            jax.ShapeDtypeStruct((own_f, own_cols), F32),
            jax.ShapeDtypeStruct((1, own_cols), F32),
        ),
        in_specs=[pl.BlockSpec(memory_space=pltpu.HBM)] * 2,
        out_specs=(pl.BlockSpec(memory_space=pltpu.VMEM),) * 2,
        scratch_shapes=[
            pltpu.VMEM((nb, rows, features), jnp.bfloat16),
            pltpu.VMEM((half, features), jnp.bfloat16),
            pltpu.VMEM((nb, rows, half), F32),
            pltpu.VMEM((2, nc * rows, half), jnp.bfloat16),
            pltpu.VMEM((2, nc, rows), F32),
            pltpu.VMEM((ITERS, nz, 1, half), F32),
            pltpu.VMEM((ITERS, 2, nb, nc, rows), F32),
            pltpu.VMEM((nd, 1, half), F32),
            pltpu.VMEM((nd, 1, half), F32),
            pltpu.VMEM((features, half), F32),
            pltpu.VMEM((nz, 2 * own_f, half), F32),
            pltpu.VMEM((2 * own_f, half), F32),
            pltpu.VMEM((own_f, half), F32),
            dma, dma, dma((nc,)), dma((nb,)), dma((nc,)),
            dma((ITERS, nz)), dma((ITERS, nz)), dma((ITERS, 2, nb)), dma((ITERS, 2, nb)),
            dma((nd,)), dma((nd,)), dma((nd,)), dma((nd,)),
            dma((nz,)), dma((nz,)), dma, dma,
        ],
        compiler_params=pltpu.CompilerParams(
            collective_id=0, has_side_effects=True
        ),
    )(embeddings, centroids)
    return out, mass.reshape(own_cols)


def replicated_kernel(
    nd, nc,
    emb_ref, cent_ref, out_ref, mass_ref,
    emb_all, centers, scores, plan, high, total, wide, rpot, zpot, colbuf, rowbuf, sums, finished, pairbuf, pairmass,
    own_sem, cent_sem, own_ss, emb_rs, core_ss, plane_ss, col_ss, col_rs, row_ss, row_rs,
    zp_ss, zp_rs, pair_ss, pair_rs,
):
    nz = nd // 2
    nb = 2 * nc
    rows, features = emb_ref.shape
    half = cent_ref.shape[0] // 2
    own_f = features // nd
    docs, clusters = rows * nd * nc, 2 * half * nc
    log_docs, log_clusters = math.log2(docs), math.log2(clusters)
    d = lax.axis_index("doc")
    c = lax.axis_index("clu")
    core = lax.rem(d, 2)
    other = 1 - core
    z = lax.div(d, 2)
    partner = d + other - core
    me = core * nc + c
    step = min(half, 64)
    tiles = step // 8

    def paired(i, k, n):
        if n & (n - 1):
            return lax.rem(i + k, n)
        bits = [1 << b for b in range(n.bit_length() - 1)]
        return sum(lax.rem(lax.div(i, b) + k // b, 2) * b for b in bits)

    def block_peer(k):
        peer = paired(me, k, nb)
        return peer, (2 * z + lax.div(peer, nc), lax.rem(peer, nc))

    def clu_peer(k):
        return paired(c, k, nc)

    def z_peer(k):
        return paired(z, k, nz)

    def slot_of(plane, side, cluster):
        return plane * nb + side * nc + cluster

    def remote(src, dst, ss, rs, device):
        return pltpu.make_async_remote_copy(
            src_ref=src, dst_ref=dst, send_sem=ss, recv_sem=rs,
            device_id=device, device_id_type=MESH,
        )

    sends = []

    def send(*args):
        copy = remote(*args)
        copy.start()
        sends.append(copy)

    mine = slot_of(z, core, c)
    own = emb_all.at[mine]
    own_copy = pltpu.make_async_copy(emb_ref, own, own_sem)
    own_copy.start()
    cent_copy = pltpu.make_async_copy(
        cent_ref.at[pl.ds(pl.multiple_of(core * half, half), half), :], centers, cent_sem
    )
    cent_copy.start()
    barrier = pltpu.get_barrier_semaphore()
    for k in range(1, nb):
        pl.semaphore_signal(barrier, inc=1, device_id=block_peer(k)[1], device_id_type=MESH)
    for k in range(1, nz):
        pl.semaphore_signal(
            barrier, inc=1, device_id=(2 * z_peer(k) + core, c), device_id_type=MESH
        )

    def score(slot):
        return lax.dot_general(
            centers[...], emb_all[slot], (((1,), (1,)), ((), ())), preferred_element_type=F32
        ) * (LOG2E / SMOOTHING)

    def arrive(slot):
        remote(
            emb_all.at[slot], emb_all.at[slot], own_ss.at[0], emb_rs.at[slot], (partner, c)
        ).wait_recv()

    def to_partner(slot, k):
        send(emb_all.at[slot], emb_all.at[slot], core_ss.at[k], emb_rs.at[slot], (partner, c))

    def to_plane(slot, k):
        for j in reversed(range(1, nc)):
            send(
                emb_all.at[slot], emb_all.at[slot], plane_ss.at[k, j], emb_rs.at[slot],
                (d, clu_peer(j)),
            )

    def plane_scores(k):
        def body(b, carry):
            slot = z_peer(k) * nb + 2 * b
            both = lax.dot_general(
                centers[...], emb_all[pl.ds(slot, 2)].reshape(2 * rows, features),
                (((1,), (1,)), ((), ())), preferred_element_type=F32,
            ) * (LOG2E / SMOOTHING)
            scores[slot] = both[:, :rows] + wide[...]
            scores[slot + 1] = both[:, rows:] + wide[...]
            return carry

        for j in range(nc):
            arrive(slot_of(z_peer(k), other, clu_peer(j)))
        lax.fori_loop(0, nb // 2, body, 0, unroll=2)

    def piece(g):
        return pl.ds(pl.multiple_of(g * step, step), step)

    def column_update(slots, first):
        def body(g, carry):
            at = piece(g)
            ts = [scores[s, at, :] for s in slots]
            old = None if first else high[at, :]
            new = functools.reduce(jnp.maximum, ts if first else ts + [old])
            part = sum(jnp.exp2(t - new) for t in ts)
            total[at, :] = part if first else part + total[at, :] * jnp.exp2(old - new)
            high[at, :] = new
            return carry

        lax.fori_loop(0, half // step, body, 0, unroll=2)

    own_copy.wait()
    cent_copy.wait()
    scores[mine] = score(mine)
    pl.semaphore_wait(barrier, nb - 1 + nz - 1)

    to_plane(mine, 0)
    to_partner(mine, 0)
    for k in range(1, nz):
        send(own, own, own_ss.at[k], emb_rs.at[mine], (2 * z_peer(k) + core, c))
    column_update([mine], True)
    for k in range(1, nc):
        slot = slot_of(z, core, clu_peer(k))
        arrive(slot)
        to_partner(slot, k)
        scores[slot] = score(slot)
    column_update([slot_of(z, core, clu_peer(k)) for k in range(1, nc)], False)

    def from_plane(k):
        slot = slot_of(z_peer(k), core, c)
        arrive(slot)
        to_plane(slot, k)
        to_partner(slot, k * nc)

    def across(k):
        for j in range(1, nc):
            slot = slot_of(z_peer(k), core, clu_peer(j))
            arrive(slot)
            to_partner(slot, k * nc + j)

    early = list(range(1, nz))[:-1]
    late = list(range(1, nz))[-1:]
    for k in early[:1]:
        from_plane(k)
    for k in range(nc):
        slot = slot_of(z, other, clu_peer(k))
        arrive(slot)
        scores[slot] = score(slot)
        if k % 2:
            column_update([slot_of(z, other, clu_peer(k - 1)), slot], False)
    if nc % 2:
        column_update([slot_of(z, other, clu_peer(nc - 1))], False)

    def spread(x):
        wide[...] = jnp.transpose(jnp.broadcast_to(x, (rows, half)))

    def column_send(it, x):
        colbuf[it, z] = x
        ref = colbuf.at[it, z]
        for k in range(1, nz):
            send(ref, ref, col_ss.at[it, k], col_rs.at[it, z], (2 * z_peer(k) + core, c))

    def column_receive(it):
        for k in range(1, nz):
            theirs = colbuf.at[it, z_peer(k)]
            remote(
                theirs, theirs, col_ss.at[it, k], col_rs.at[it, z_peer(k)], (partner, c)
            ).wait_recv()
        return [colbuf[it, s] for s in range(nz)]

    def row_send(it):
        ref = rowbuf.at[it, me]
        for k in range(1, nb):
            send(ref, ref, row_ss.at[it, k], row_rs.at[it, me], block_peer(k)[1])

    def row_receive(it):
        for k in range(1, nb):
            peer, device = block_peer(k)
            theirs = rowbuf.at[it, peer]
            remote(theirs, theirs, row_ss.at[it, k], row_rs.at[it, peer], device).wait_recv()
        return [rowbuf[it, s] for s in range(nb)]

    def folded(x, op):
        return functools.reduce(op, [x[8 * i:8 * i + 8] for i in range(tiles)])

    def row_first(b, carry):
        slot = z * nb + b
        top = jnp.full((8, rows), -jnp.inf, F32)
        for g in range(half // step):
            at = pl.ds(g * step, step)
            t = scores[slot, at, :] + wide[at, :]
            scores[slot, at, :] = t
            top = jnp.maximum(top, folded(t, jnp.maximum))
        top = jnp.max(top, axis=0, keepdims=True)
        acc = jnp.zeros((8, rows), F32)
        for g in range(half // step):
            at = pl.ds(g * step, step)
            acc = acc + folded(jnp.exp2(scores[slot, at, :] - top), jnp.add)
        rowbuf[0, me, pl.ds(b, 1), :] = top + jnp.log2(jnp.sum(acc, axis=0, keepdims=True))
        return carry

    def row_next(it, b, carry):
        slot = z * nb + b
        r = rpot[pl.ds(b, 1), :]
        acc = jnp.zeros((8, rows), F32)
        for g in range(half // step):
            at = pl.ds(g * step, step)
            t = scores[slot, at, :] + wide[at, :]
            scores[slot, at, :] = t
            acc = acc + folded(jnp.exp2(t + r), jnp.add)
        rowbuf[it, me, pl.ds(b, 1), :] = jnp.sum(acc, axis=0, keepdims=True)
        return carry

    def column_next(g, carry):
        at = piece(g)
        acc = jnp.zeros((step, rows), F32)
        for b in range(nb):
            acc = acc + jnp.exp2(scores[z * nb + b, at, :] + rpot[pl.ds(b, 1), :])
        total[at, :] = acc
        return carry

    tops = jnp.transpose(high[...])
    top = jnp.max(tops, axis=0, keepdims=True)
    column_send(
        0,
        top + jnp.log2(
            jnp.sum(jnp.transpose(total[...]) * jnp.exp2(tops - top), axis=0, keepdims=True)
        ),
    )
    for k in early[1:]:
        from_plane(k)
    logs = column_receive(0)
    top = functools.reduce(jnp.maximum, logs)
    col_pot = -log_clusters - (top + jnp.log2(sum(jnp.exp2(x - top) for x in logs)))
    spread(col_pot)
    lax.fori_loop(0, nb, row_first, 0, unroll=4)
    row_send(0)
    for k in early:
        across(k)
    logs = row_receive(0)
    top = functools.reduce(jnp.maximum, logs)
    rpot[...] = -log_docs - (top + jnp.log2(sum(jnp.exp2(x - top) for x in logs)))

    for it in range(1, ITERS):
        lax.fori_loop(0, half // step, column_next, 0, unroll=4)
        column_send(it, jnp.sum(jnp.transpose(total[...]), axis=0, keepdims=True))
        if it == 1:
            for k in late:
                from_plane(k)
        change = -log_clusters - jnp.log2(sum(column_receive(it)))
        col_pot = col_pot + change
        spread(change)
        lax.fori_loop(0, nb, functools.partial(row_next, it), 0, unroll=4)
        row_send(it)
        if it == 1:
            for k in late:
                across(k)
        if it == ITERS - 1:
            spread(col_pot)
        for k in early if it == ITERS - 1 else ():
            plane_scores(k)
        rpot[...] = rpot[...] - log_docs - jnp.log2(sum(row_receive(it)))

    zpot[z] = rpot[...] + log_docs
    ref = zpot.at[z]
    for k in range(1, nz):
        send(ref, ref, zp_ss.at[k], zp_rs.at[z], (2 * z_peer(k) + core, c))

    def plane_plan(plane, first):
        def body(g, carry):
            at = piece(g)
            acc = jnp.zeros((step, rows), F32)
            for b in range(nb):
                p = jnp.exp2(scores[plane * nb + b, at, :] + zpot[plane, pl.ds(b, 1), :])
                plan[at, b * rows:(b + 1) * rows] = p.astype(jnp.bfloat16)
                acc = acc + p
            total[at, :] = acc if first else acc + total[at, :]
            return carry

        lax.fori_loop(0, half // step, body, 0, unroll=4)
        product = lax.dot_general(
            plan[...], emb_all[pl.ds(plane * nb, nb)].reshape(nb * rows, features),
            (((1,), (0,)), ((), ())), preferred_element_type=F32,
        )
        sums[...] = product if first else sums[...] + product

    plane_plan(z, True)
    for k in late:
        plane_scores(k)
    for k in range(1, nz):
        plane = z_peer(k)
        theirs = zpot.at[plane]
        remote(theirs, theirs, zp_ss.at[k], zp_rs.at[plane], (partner, c)).wait_recv()
        plane_plan(plane, False)

    everything = jnp.transpose(sums[...])
    scale = lax.rsqrt(jnp.sum(everything * everything, axis=0, keepdims=True) / features + 1e-06)
    finished[...] = everything * scale
    pairmass[0] = jnp.sum(jnp.transpose(total[...]), axis=0, keepdims=True) * (clusters / docs)

    def features_of(which):
        return finished.at[pl.ds(pl.multiple_of((2 * z + which) * own_f, own_f), own_f), :]

    send(features_of(other), pairbuf, pair_ss.at[0], pair_rs.at[0], (partner, c))
    send(pairmass.at[0], pairmass.at[1], pair_ss.at[1], pair_rs.at[1], (partner, c))
    columns = pl.ds(pl.multiple_of(core * half, half), half)
    out_ref[:, columns] = features_of(core)[...]
    mass_ref[:, columns] = pairmass[0]
    columns = pl.ds(pl.multiple_of(other * half, half), half)
    remote(pairbuf, pairbuf, pair_ss.at[0], pair_rs.at[0], (partner, c)).wait_recv()
    out_ref[:, columns] = pairbuf[...]
    remote(
        pairmass.at[1], pairmass.at[1], pair_ss.at[1], pair_rs.at[1], (partner, c)
    ).wait_recv()
    mass_ref[:, columns] = pairmass[1]
    for copy in sends:
        copy.wait_send()


def replicated(nd, nc, embeddings, centroids):
    rows, features = embeddings.shape
    own_cols = centroids.shape[0]
    half, nz, nb = own_cols // 2, nd // 2, 2 * nc
    own_f = features // nd
    dma = pltpu.SemaphoreType.DMA
    out, mass = pl.pallas_call(
        functools.partial(replicated_kernel, nd, nc),
        out_shape=(
            jax.ShapeDtypeStruct((own_f, own_cols), F32),
            jax.ShapeDtypeStruct((1, own_cols), F32),
        ),
        in_specs=[pl.BlockSpec(memory_space=pltpu.HBM)] * 2,
        out_specs=(pl.BlockSpec(memory_space=pltpu.VMEM),) * 2,
        scratch_shapes=[
            pltpu.VMEM((nz * nb, rows, features), jnp.bfloat16),
            pltpu.VMEM((half, features), jnp.bfloat16),
            pltpu.VMEM((nz * nb, half, rows), F32),
            pltpu.VMEM((half, nb * rows), jnp.bfloat16),
            pltpu.VMEM((half, rows), F32),
            pltpu.VMEM((half, rows), F32),
            pltpu.VMEM((half, rows), F32),
            pltpu.VMEM((nb, rows), F32),
            pltpu.VMEM((nz, nb, rows), F32),
            pltpu.VMEM((ITERS, nz, 1, half), F32),
            pltpu.VMEM((ITERS, nb, nb, rows), F32),
            pltpu.VMEM((half, features), F32),
            pltpu.VMEM((features, half), F32),
            pltpu.VMEM((own_f, half), F32),
            pltpu.VMEM((2, 1, half), F32),
            dma, dma, dma((nz,)), dma((nz * nb,)), dma((nz * nc,)), dma((nz, nc)),
            dma((ITERS, nz)), dma((ITERS, nz)), dma((ITERS, nb)), dma((ITERS, nb)),
            dma((nz,)), dma((nz,)), dma((2,)), dma((2,)),
        ],
        compiler_params=pltpu.CompilerParams(
            collective_id=0, has_side_effects=True, vmem_limit_bytes=VMEM_BYTES
        ),
    )(*(pltpu.with_memory_space_constraint(a, pltpu.HBM) for a in (embeddings, centroids)))
    return out, mass.reshape(own_cols)


VMEM_BYTES = 48 << 20


def local(nd, nc, embeddings, centroids):
    rows, features = embeddings.shape
    docs = rows * nd * nc
    half = centroids.shape[0] // 2
    held = docs * (2 * features + 4 * half)
    form = replicated if 2 * held <= VMEM_BYTES else scattered
    return form(nd, nc, embeddings, centroids)


def solution(mesh):
    placed = (P(("doc", "clu"), None), P("clu", None))
    body = functools.partial(local, mesh.shape["doc"], mesh.shape["clu"])
    return jax.shard_map(
        body, mesh=mesh, in_specs=placed, out_specs=(P("doc", "clu"), P("clu")), check_vma=False
    )
```

```python
import functools
import math

import jax
import jax.numpy as jnp
from jax import lax
from jax.experimental import pallas as pl
from jax.experimental.pallas import tpu as pltpu
from jax.sharding import PartitionSpec as P

ITERS = 2
SMOOTHING = 0.05
LOG2E = math.log2(math.e)
MESH = pl.DeviceIdType.MESH
F32 = jnp.float32


def scattered_kernel(
    nd, nc,
    emb_ref, cent_ref, out_ref, mass_ref,
    emb_all, centers, scores, plan, rpot, colbuf, rowbuf, massbuf, sqbuf, sums, rsbuf, tot, pairbuf,
    own_sem, cent_sem, emb_ss, emb_rs, fwd_ss, col_ss, col_rs, row_ss, row_rs,
    mass_ss, mass_rs, sq_ss, sq_rs, sum_ss, sum_rs, pair_ss, pair_rs,
):
    nz = nd // 2
    nb = 2 * nc
    rows, features = emb_ref.shape
    half = cent_ref.shape[0] // 2
    own_f = features // nd
    log_docs = math.log2(rows * nd * nc)
    log_clusters = math.log2(2 * half * nc)
    d = lax.axis_index("doc")
    c = lax.axis_index("clu")
    core = lax.rem(d, 2)
    z = lax.div(d, 2)
    partner = d + 1 - 2 * core
    me = core * nc + c

    def block_peer(k):
        peer = lax.rem(me + k, nb)
        return peer, (2 * z + lax.div(peer, nc), lax.rem(peer, nc))

    def z_peer(k):
        peer = lax.rem(z + k, nz)
        return peer, (2 * peer + core, c)

    def doc_peer(k):
        peer = lax.rem(d + k, nd)
        return peer, (peer, c)

    def remote(src, dst, ss, rs, device):
        return pltpu.make_async_remote_copy(
            src_ref=src, dst_ref=dst, send_sem=ss, recv_sem=rs,
            device_id=device, device_id_type=MESH,
        )

    sends = []

    def send(*args):
        copy = remote(*args)
        copy.start()
        sends.append(copy)

    own_copy = pltpu.make_async_copy(emb_ref, emb_all.at[me], own_sem)
    own_copy.start()
    cent_copy = pltpu.make_async_copy(
        cent_ref.at[pl.ds(pl.multiple_of(core * half, half), half), :], centers, cent_sem
    )
    cent_copy.start()
    barrier = pltpu.get_barrier_semaphore()
    for k in range(1, nb):
        pl.semaphore_signal(barrier, inc=1, device_id=block_peer(k)[1], device_id_type=MESH)
    for k in range(1, nd):
        pl.semaphore_signal(barrier, inc=1, device_id=doc_peer(k)[1], device_id_type=MESH)

    def col_update(state, t):
        high, total = state
        t = t.reshape(rows // 8, 8, half)
        new = jnp.maximum(high, jnp.max(t, axis=0))
        total = total * jnp.exp2(high - new) + jnp.sum(jnp.exp2(t - new[None]), axis=0)
        return new, total

    state = (jnp.full((8, half), -jnp.inf, F32), jnp.zeros((8, half), F32))

    def first_block(state, slot):
        s = lax.dot_general(
            emb_all[slot], centers[...], (((1,), (1,)), ((), ())), preferred_element_type=F32
        ) * (LOG2E / SMOOTHING)
        scores[slot] = s
        return col_update(state, s)

    def arrive(slot):
        remote(
            emb_all.at[slot], emb_all.at[slot], emb_ss.at[0], emb_rs.at[slot], (partner, c)
        ).wait_recv()

    def clu_peer(k):
        if nc & (nc - 1):
            return lax.rem(c + k, nc)
        bits = [1 << i for i in range(nc.bit_length() - 1)]
        return sum(lax.rem(lax.div(c, b) + k // b, 2) * b for b in bits)

    own_copy.wait()
    cent_copy.wait()
    state = first_block(state, me)
    pl.semaphore_wait(barrier, nb - 1 + nd - 1)

    own = emb_all.at[me]
    for k in reversed(range(1, nc)):
        send(own, own, emb_ss.at[k], emb_rs.at[me], (d, clu_peer(k)))
    send(own, own, emb_ss.at[0], emb_rs.at[me], (partner, c))
    other = 1 - core
    for k in range(1, nc):
        slot = core * nc + clu_peer(k)
        arrive(slot)
        send(emb_all.at[slot], emb_all.at[slot], fwd_ss.at[k], emb_rs.at[slot], (partner, c))
        state = first_block(state, slot)
    for k in range(nc):
        slot = other * nc + clu_peer(k)
        arrive(slot)
        state = first_block(state, slot)

    diagonal = lax.broadcasted_iota(jnp.int32, (rows, rows), 0) == lax.broadcasted_iota(
        jnp.int32, (rows, rows), 1
    )

    def to_lanes(x):
        return jnp.sum(jnp.where(diagonal, x, 0.0), axis=0, keepdims=True)

    def to_sublanes(x):
        return jnp.sum(jnp.where(diagonal, x, 0.0), axis=1, keepdims=True)

    def column_potential(it, state):
        high, total = state
        top = jnp.max(high, axis=0, keepdims=True)
        total = jnp.sum(total * jnp.exp2(high - top), axis=0, keepdims=True)
        colbuf[it, z] = top + jnp.log2(total)
        mine = colbuf.at[it, z]
        for k in range(1, nz):
            send(mine, mine, col_ss.at[it, k], col_rs.at[it, z], z_peer(k)[1])
        for k in range(1, nz):
            peer, device = z_peer(k)
            theirs = colbuf.at[it, peer]
            remote(theirs, theirs, col_ss.at[it, k], col_rs.at[it, peer], device).wait_recv()
        logs = [colbuf[it, s] for s in range(nz)]
        top = functools.reduce(jnp.maximum, logs)
        return -log_clusters - (top + jnp.log2(sum(jnp.exp2(x - top) for x in logs)))

    part = nb // 2

    def row_send(it, h, col_pot):
        def block(b, carry):
            t = scores[h * part + b] + col_pot
            high = jnp.max(t, axis=1, keepdims=True)
            total = jnp.sum(jnp.exp2(t - high), axis=1, keepdims=True)
            rowbuf[it, h, me, pl.ds(b, 1), :] = to_lanes(high + jnp.log2(total))
            return carry

        lax.fori_loop(0, part, block, 0, unroll=4)
        mine = rowbuf.at[it, h, me]
        for k in range(1, nb):
            send(mine, mine, row_ss.at[it, h, k], row_rs.at[it, h, me], block_peer(k)[1])

    def row_receive(it, h):
        for k in range(1, nb):
            peer, device = block_peer(k)
            theirs = rowbuf.at[it, h, peer]
            remote(
                theirs, theirs, row_ss.at[it, h, k], row_rs.at[it, h, peer], device
            ).wait_recv()
        logs = rowbuf[it, h]
        top = jnp.max(logs, axis=0)
        total = jnp.sum(jnp.exp2(logs - top[None]), axis=0)
        rpot[h] = -log_docs - (top + jnp.log2(total))

    for it in range(ITERS):
        if it > 0:
            state = (jnp.full((8, half), -jnp.inf, F32), jnp.zeros((8, half), F32))
            for h in range(2):
                def again(b, state):
                    t = scores[h * part + b] + to_sublanes(rpot[h, pl.ds(b, 1), :])
                    return col_update(state, t)

                row_receive(it - 1, h)
                state = lax.fori_loop(0, part, again, state, unroll=4)
        col_pot = column_potential(it, state)
        for h in range(2):
            row_send(it, h, col_pot)

    mass = jnp.zeros((8, half), F32)
    for h in range(2):
        def plan_block(b, mass):
            t = scores[h * part + b] + to_sublanes(rpot[h, pl.ds(b, 1), :]) + col_pot + log_docs
            p = jnp.exp2(t)
            plan[h, pl.ds(pl.multiple_of(b * rows, rows), rows), :] = p.astype(jnp.bfloat16)
            return mass + jnp.sum(p.reshape(rows // 8, 8, half), axis=0)

        row_receive(ITERS - 1, h)
        mass = lax.fori_loop(0, part, plan_block, mass, unroll=4)
        product = lax.dot_general(
            emb_all[h * part:(h + 1) * part].reshape(part * rows, features), plan[h],
            (((0,), (0,)), ((), ())), preferred_element_type=F32,
        )
        sums[...] = product if h == 0 else sums[...] + product
    massbuf[d] = jnp.sum(mass, axis=0, keepdims=True)
    far = sorted(range(1, nz), key=lambda k: -min(k, nz - k))

    def share(peer):
        return sums.at[pl.ds(pl.multiple_of(peer * 2 * own_f, 2 * own_f), 2 * own_f), :]

    for k in far:
        peer, device = z_peer(k)
        send(share(peer), rsbuf.at[z], sum_ss.at[k], sum_rs.at[z], device)
    for k in range(1, nd):
        send(massbuf.at[d], massbuf.at[d], mass_ss.at[k], mass_rs.at[d], doc_peer(k)[1])
    total = share(z)[...]
    for k in reversed(far):
        peer, device = z_peer(k)
        remote(share(z), rsbuf.at[peer], sum_ss.at[k], sum_rs.at[peer], device).wait_recv()
        total = total + rsbuf[peer]
    tot[...] = total
    sqbuf[d] = jnp.sum(total * total, axis=0, keepdims=True)

    def features_of(which):
        return tot.at[pl.ds(pl.multiple_of(which * own_f, own_f), own_f), :]

    for k in range(1, nd):
        send(sqbuf.at[d], sqbuf.at[d], sq_ss.at[k], sq_rs.at[d], doc_peer(k)[1])
    send(features_of(other), pairbuf, pair_ss, pair_rs, (partner, c))
    for k in range(1, nd):
        peer, device = doc_peer(k)
        theirs = massbuf.at[peer]
        remote(theirs, theirs, mass_ss.at[k], mass_rs.at[peer], device).wait_recv()
        theirs = sqbuf.at[peer]
        remote(theirs, theirs, sq_ss.at[k], sq_rs.at[peer], device).wait_recv()
    remote(features_of(core), pairbuf, pair_ss, pair_rs, (partner, c)).wait_recv()

    def finish(which, block):
        columns = pl.ds(pl.multiple_of(which * half, half), half)
        squares = sum(sqbuf[2 * s + which] for s in range(nz))
        out_ref[:, columns] = block * lax.rsqrt(squares / features + 1e-06)
        mass_ref[:, columns] = sum(massbuf[2 * s + which] for s in range(nz)) * (
            2 * half * nc / (rows * nd * nc)
        )

    finish(core, features_of(core)[...])
    finish(other, pairbuf[...])
    for copy in sends:
        copy.wait_send()


def scattered(nd, nc, embeddings, centroids):
    rows, features = embeddings.shape
    own_cols = centroids.shape[0]
    half, nz, nb = own_cols // 2, nd // 2, 2 * nc
    own_f = features // nd
    dma = pltpu.SemaphoreType.DMA
    out, mass = pl.pallas_call(
        functools.partial(scattered_kernel, nd, nc),
        out_shape=(
            jax.ShapeDtypeStruct((own_f, own_cols), F32),
            jax.ShapeDtypeStruct((1, own_cols), F32),
        ),
        in_specs=[pl.BlockSpec(memory_space=pltpu.HBM)] * 2,
        out_specs=(pl.BlockSpec(memory_space=pltpu.VMEM),) * 2,
        scratch_shapes=[
            pltpu.VMEM((nb, rows, features), jnp.bfloat16),
            pltpu.VMEM((half, features), jnp.bfloat16),
            pltpu.VMEM((nb, rows, half), F32),
            pltpu.VMEM((2, nc * rows, half), jnp.bfloat16),
            pltpu.VMEM((2, nc, rows), F32),
            pltpu.VMEM((ITERS, nz, 1, half), F32),
            pltpu.VMEM((ITERS, 2, nb, nc, rows), F32),
            pltpu.VMEM((nd, 1, half), F32),
            pltpu.VMEM((nd, 1, half), F32),
            pltpu.VMEM((features, half), F32),
            pltpu.VMEM((nz, 2 * own_f, half), F32),
            pltpu.VMEM((2 * own_f, half), F32),
            pltpu.VMEM((own_f, half), F32),
            dma, dma, dma((nc,)), dma((nb,)), dma((nc,)),
            dma((ITERS, nz)), dma((ITERS, nz)), dma((ITERS, 2, nb)), dma((ITERS, 2, nb)),
            dma((nd,)), dma((nd,)), dma((nd,)), dma((nd,)),
            dma((nz,)), dma((nz,)), dma, dma,
        ],
        compiler_params=pltpu.CompilerParams(
            collective_id=0, has_side_effects=True
        ),
    )(embeddings, centroids)
    return out, mass.reshape(own_cols)


def replicated_kernel(
    nd, nc,
    emb_ref, cent_ref, out_ref, mass_ref,
    emb_all, centers, scores, plan, high, total, wide, pots, share, colbuf, rowbuf, sums, finished, pairbuf, pairmass,
    own_sem, cent_sem, own_ss, emb_rs, core_ss, plane_ss, col_ss, col_rs, row_ss, row_rs,
    pot_ss, pot_rs, pair_ss, pair_rs,
):
    nz = nd // 2
    nb = 2 * nc
    rows, features = emb_ref.shape
    half = cent_ref.shape[0] // 2
    own_f = features // nd
    docs, clusters = rows * nd * nc, 2 * half * nc
    log_docs, log_clusters = math.log2(docs), math.log2(clusters)
    d = lax.axis_index("doc")
    c = lax.axis_index("clu")
    core = lax.rem(d, 2)
    other = 1 - core
    z = lax.div(d, 2)
    partner = d + other - core
    me = core * nc + c
    step = min(half, 64)
    tiles = step // 8

    def paired(i, k, n):
        if n & (n - 1):
            return lax.rem(i + k, n)
        bits = [1 << b for b in range(n.bit_length() - 1)]
        return sum(lax.rem(lax.div(i, b) + k // b, 2) * b for b in bits)

    def block_peer(k):
        peer = paired(me, k, nb)
        return peer, (2 * z + lax.div(peer, nc), lax.rem(peer, nc))

    def clu_peer(k):
        return paired(c, k, nc)

    def z_peer(k):
        return paired(z, k, nz)

    def slot_of(plane, side, cluster):
        return plane * nb + side * nc + cluster

    def remote(src, dst, ss, rs, device):
        return pltpu.make_async_remote_copy(
            src_ref=src, dst_ref=dst, send_sem=ss, recv_sem=rs,
            device_id=device, device_id_type=MESH,
        )

    sends = []

    def send(*args):
        copy = remote(*args)
        copy.start()
        sends.append(copy)

    mine = slot_of(z, core, c)
    own = emb_all.at[mine]
    own_copy = pltpu.make_async_copy(emb_ref, own, own_sem)
    own_copy.start()
    cent_copy = pltpu.make_async_copy(
        cent_ref.at[pl.ds(pl.multiple_of(core * half, half), half), :], centers, cent_sem
    )
    cent_copy.start()
    barrier = pltpu.get_barrier_semaphore()
    for k in range(1, nb):
        pl.semaphore_signal(barrier, inc=1, device_id=block_peer(k)[1], device_id_type=MESH)
    for k in range(1, nz):
        pl.semaphore_signal(
            barrier, inc=1, device_id=(2 * z_peer(k) + core, c), device_id_type=MESH
        )

    def score(slot):
        return lax.dot_general(
            centers[...], emb_all[slot], (((1,), (1,)), ((), ())), preferred_element_type=F32
        ) * (LOG2E / SMOOTHING)

    def arrive(slot):
        remote(
            emb_all.at[slot], emb_all.at[slot], own_ss.at[0], emb_rs.at[slot], (partner, c)
        ).wait_recv()

    def to_partner(slot, k):
        send(emb_all.at[slot], emb_all.at[slot], core_ss.at[k], emb_rs.at[slot], (partner, c))

    near = [j for j in range(1, nc) if not j & (j - 1)]
    far = [j for j in range(1, nc) if j & (j - 1)]

    def to_plane(slot, k, which):
        for j in which:
            send(
                emb_all.at[slot], emb_all.at[slot], plane_ss.at[k, j], emb_rs.at[slot],
                (d, clu_peer(j)),
            )

    def pair_scores(k, side, pair):
        slot = slot_of(z_peer(k), side, 2 * pair)
        both = lax.dot_general(
            centers[...], emb_all[pl.ds(slot, 2)].reshape(2 * rows, features),
            (((1,), (1,)), ((), ())), preferred_element_type=F32,
        ) * (LOG2E / SMOOTHING)
        scores[slot] = both[:, :rows] + wide[...]
        scores[slot + 1] = both[:, rows:] + wide[...]

    def plane_scores(k, first, count):
        for j in range(2 * first, 2 * (first + count)):
            arrive(slot_of(z_peer(k), other, clu_peer(j)))
        for j in range(first, first + count):
            for side in (core, other):
                pair_scores(k, side, paired(lax.div(c, 2), j, nc // 2))

    def piece(g):
        return pl.ds(pl.multiple_of(g * step, step), step)

    def column_update(slots, first):
        def body(g, carry):
            at = piece(g)
            ts = [scores[s, at, :] for s in slots]
            old = None if first else high[at, :]
            new = functools.reduce(jnp.maximum, ts if first else ts + [old])
            part = sum(jnp.exp2(t - new) for t in ts)
            total[at, :] = part if first else part + total[at, :] * jnp.exp2(old - new)
            high[at, :] = new
            return carry

        lax.fori_loop(0, half // step, body, 0, unroll=2)

    own_copy.wait()
    cent_copy.wait()
    scores[mine] = score(mine)
    pl.semaphore_wait(barrier, nb - 1 + nz - 1)

    to_plane(mine, 0, far + near)
    to_partner(mine, 0)
    for k in range(1, nz):
        send(own, own, own_ss.at[k], emb_rs.at[mine], (2 * z_peer(k) + core, c))
    column_update([mine], True)
    for k in range(1, nc):
        slot = slot_of(z, core, clu_peer(k))
        arrive(slot)
        to_partner(slot, k)
        scores[slot] = score(slot)
    column_update([slot_of(z, core, clu_peer(k)) for k in range(1, nc)], False)

    def from_plane(k):
        slot = slot_of(z_peer(k), core, c)
        arrive(slot)
        to_plane(slot, k, near)
        to_partner(slot, k * nc)

    def across(k, which):
        for j in which:
            slot = slot_of(z_peer(k), core, clu_peer(j))
            arrive(slot)
            to_partner(slot, k * nc + j)

    if nz > 1:
        from_plane(1)
    for k in range(nc):
        slot = slot_of(z, other, clu_peer(k))
        arrive(slot)
        scores[slot] = score(slot)
        if k % 2:
            column_update([slot_of(z, other, clu_peer(k - 1)), slot], False)
    if nc % 2:
        column_update([slot_of(z, other, clu_peer(nc - 1))], False)

    def spread(x):
        wide[...] = jnp.transpose(jnp.broadcast_to(x, (rows, half)))

    def column_send(it, x):
        colbuf[it, z] = x
        ref = colbuf.at[it, z]
        for k in range(1, nz):
            send(ref, ref, col_ss.at[it, k], col_rs.at[it, z], (2 * z_peer(k) + core, c))

    def column_receive(it):
        for k in range(1, nz):
            theirs = colbuf.at[it, z_peer(k)]
            remote(
                theirs, theirs, col_ss.at[it, k], col_rs.at[it, z_peer(k)], (partner, c)
            ).wait_recv()
        return [colbuf[it, s] for s in range(nz)]

    def row_send(it, k):
        ref = rowbuf.at[it, k, me]
        for j in range(1, nb):
            send(ref, ref, row_ss.at[it, k, j], row_rs.at[it, k, me], block_peer(j)[1])

    def row_receive(it, k):
        for j in range(1, nb):
            peer, device = block_peer(j)
            theirs = rowbuf.at[it, k, peer]
            remote(
                theirs, theirs, row_ss.at[it, k, j], row_rs.at[it, k, peer], device
            ).wait_recv()
        return [rowbuf[it, k, s] for s in range(nb)]

    def folded(x, op):
        return functools.reduce(op, [x[8 * i:8 * i + 8] for i in range(tiles)])

    def row_first(b, carry):
        slot = z * nb + b
        top = jnp.full((8, rows), -jnp.inf, F32)
        for g in range(half // step):
            at = pl.ds(g * step, step)
            t = scores[slot, at, :] + wide[at, :]
            scores[slot, at, :] = t
            top = jnp.maximum(top, folded(t, jnp.maximum))
        top = jnp.max(top, axis=0, keepdims=True)
        acc = jnp.zeros((8, rows), F32)
        for g in range(half // step):
            at = pl.ds(g * step, step)
            acc = acc + folded(jnp.exp2(scores[slot, at, :] - top), jnp.add)
        rowbuf[0, 0, me, pl.ds(b, 1), :] = top + jnp.log2(jnp.sum(acc, axis=0, keepdims=True))
        return carry

    def row_next(it, k, last, b, carry):
        plane = z_peer(k)
        slot = plane * nb + b
        r = pots[plane, pl.ds(b, 1), :]
        acc = jnp.zeros((8, rows), F32)
        for g in range(half // step):
            at = pl.ds(g * step, step)
            t = scores[slot, at, :] + wide[at, :]
            e = jnp.exp2(t + r)
            scores[slot, at, :] = e if last else t
            acc = acc + folded(e, jnp.add)
        rowbuf[it, k, me, pl.ds(b, 1), :] = jnp.sum(acc, axis=0, keepdims=True)
        return carry

    def column_next(g, carry):
        at = piece(g)
        acc = jnp.zeros((step, rows), F32)
        for b in range(nb):
            acc = acc + jnp.exp2(scores[z * nb + b, at, :] + pots[z, pl.ds(b, 1), :])
        total[at, :] = acc
        return carry

    tops = jnp.transpose(high[...])
    top = jnp.max(tops, axis=0, keepdims=True)
    column_send(
        0,
        top + jnp.log2(
            jnp.sum(jnp.transpose(total[...]) * jnp.exp2(tops - top), axis=0, keepdims=True)
        ),
    )
    for k in range(1, nz):
        for j in far:
            slot = slot_of(z, core, clu_peer(j))
            send(
                emb_all.at[slot], emb_all.at[slot], plane_ss.at[k, j], emb_rs.at[slot],
                (2 * z_peer(k) + core, c),
            )
    for k in range(2, nz):
        from_plane(k)
    logs = column_receive(0)
    top = functools.reduce(jnp.maximum, logs)
    spread(-log_clusters - (top + jnp.log2(sum(jnp.exp2(x - top) for x in logs))))
    lax.fori_loop(0, nb, row_first, 0, unroll=4)
    row_send(0, 0)
    for k in range(1, nz):
        across(k, near + far if k == 1 else near)
    for k in range(1, nz):
        plane_scores(k, 0, nc // 2 if k == 1 else 1)
    logs = row_receive(0, 0)
    top = functools.reduce(jnp.maximum, logs)
    pots[z] = -log_docs - (top + jnp.log2(sum(jnp.exp2(x - top) for x in logs)))

    for it in range(1, ITERS):
        last = it == ITERS - 1
        if last:
            ref = pots.at[z]
            for k in range(1, nz):
                send(ref, ref, pot_ss.at[k], pot_rs.at[z], (2 * z_peer(k) + core, c))
        lax.fori_loop(0, half // step, column_next, 0, unroll=4)
        column_send(it, jnp.sum(jnp.transpose(total[...]), axis=0, keepdims=True))
        if it == 1:
            for k in range(2, nz):
                across(k, far)
            for k in range(2, nz):
                plane_scores(k, 1, nc // 2 - 1)
        change = -log_clusters - jnp.log2(sum(column_receive(it)))
        spread(change)
        for k in range(nz if last else 1):
            if k:
                theirs = pots.at[z_peer(k)]
                remote(
                    theirs, theirs, pot_ss.at[k], pot_rs.at[z_peer(k)], (partner, c)
                ).wait_recv()
            lax.fori_loop(0, nb, functools.partial(row_next, it, k, last), 0, unroll=4)
            row_send(it, k)
        if not last:
            pots[z] = pots[z] - log_docs - jnp.log2(sum(row_receive(it, 0)))

    wider = min(half, 256)

    def plane_plan(k):
        plane = z_peer(k)
        share[k] = 1.0 / sum(row_receive(ITERS - 1, k))
        block = emb_all[pl.ds(plane * nb, nb)].reshape(nb * rows, features)
        for g in range(half // wider):
            for i in range(wider // step):
                at = pl.ds(g * wider + i * step, step)
                acc = jnp.zeros((step, rows), F32)
                for b in range(nb):
                    p = scores[plane * nb + b, at, :] * share[k, pl.ds(b, 1), :]
                    plan[at, b * rows:(b + 1) * rows] = p.astype(jnp.bfloat16)
                    acc = acc + p
                total[at, :] = acc + total[at, :] if k else acc
            at = pl.ds(g * wider, wider)
            product = lax.dot_general(
                plan[at, :], block, (((1,), (0,)), ((), ())), preferred_element_type=F32
            )
            sums[at, :] = sums[at, :] + product if k else product

    for k in range(nz):
        plane_plan(k)

    everything = jnp.transpose(sums[...])
    scale = lax.rsqrt(jnp.sum(everything * everything, axis=0, keepdims=True) / features + 1e-06)
    finished[...] = everything * scale
    pairmass[0] = jnp.sum(jnp.transpose(total[...]), axis=0, keepdims=True) * (clusters / docs)

    def features_of(which):
        return finished.at[pl.ds(pl.multiple_of((2 * z + which) * own_f, own_f), own_f), :]

    send(features_of(other), pairbuf, pair_ss.at[0], pair_rs.at[0], (partner, c))
    send(pairmass.at[0], pairmass.at[1], pair_ss.at[1], pair_rs.at[1], (partner, c))
    columns = pl.ds(pl.multiple_of(core * half, half), half)
    out_ref[:, columns] = features_of(core)[...]
    mass_ref[:, columns] = pairmass[0]
    columns = pl.ds(pl.multiple_of(other * half, half), half)
    remote(pairbuf, pairbuf, pair_ss.at[0], pair_rs.at[0], (partner, c)).wait_recv()
    out_ref[:, columns] = pairbuf[...]
    remote(
        pairmass.at[1], pairmass.at[1], pair_ss.at[1], pair_rs.at[1], (partner, c)
    ).wait_recv()
    mass_ref[:, columns] = pairmass[1]
    for copy in sends:
        copy.wait_send()


def replicated(nd, nc, embeddings, centroids):
    rows, features = embeddings.shape
    own_cols = centroids.shape[0]
    half, nz, nb = own_cols // 2, nd // 2, 2 * nc
    own_f = features // nd
    dma = pltpu.SemaphoreType.DMA
    out, mass = pl.pallas_call(
        functools.partial(replicated_kernel, nd, nc),
        out_shape=(
            jax.ShapeDtypeStruct((own_f, own_cols), F32),
            jax.ShapeDtypeStruct((1, own_cols), F32),
        ),
        in_specs=[pl.BlockSpec(memory_space=pltpu.HBM)] * 2,
        out_specs=(pl.BlockSpec(memory_space=pltpu.VMEM),) * 2,
        scratch_shapes=[
            pltpu.VMEM((nz * nb, rows, features), jnp.bfloat16),
            pltpu.VMEM((half, features), jnp.bfloat16),
            pltpu.VMEM((nz * nb, half, rows), F32),
            pltpu.VMEM((half, nb * rows), jnp.bfloat16),
            pltpu.VMEM((half, rows), F32),
            pltpu.VMEM((half, rows), F32),
            pltpu.VMEM((half, rows), F32),
            pltpu.VMEM((nz, nb, rows), F32),
            pltpu.VMEM((nz, nb, rows), F32),
            pltpu.VMEM((ITERS, nz, 1, half), F32),
            pltpu.VMEM((ITERS, nz, nb, nb, rows), F32),
            pltpu.VMEM((half, features), F32),
            pltpu.VMEM((features, half), F32),
            pltpu.VMEM((own_f, half), F32),
            pltpu.VMEM((2, 1, half), F32),
            dma, dma, dma((nz,)), dma((nz * nb,)), dma((nz * nc,)), dma((nz, nc)),
            dma((ITERS, nz)), dma((ITERS, nz)), dma((ITERS, nz, nb)), dma((ITERS, nz, nb)),
            dma((nz,)), dma((nz,)), dma((2,)), dma((2,)),
        ],
        compiler_params=pltpu.CompilerParams(
            collective_id=0, has_side_effects=True, vmem_limit_bytes=VMEM_BYTES
        ),
    )(*(pltpu.with_memory_space_constraint(a, pltpu.HBM) for a in (embeddings, centroids)))
    return out, mass.reshape(own_cols)


VMEM_BYTES = 48 << 20


def local(nd, nc, embeddings, centroids):
    rows, features = embeddings.shape
    docs = rows * nd * nc
    half = centroids.shape[0] // 2
    held = docs * (2 * features + 4 * half)
    fits = 2 * held <= VMEM_BYTES and nd > 2 and nc > 1 and not nc & (nc - 1)
    form = replicated if fits else scattered
    return form(nd, nc, embeddings, centroids)


def solution(mesh):
    placed = (P(("doc", "clu"), None), P("clu", None))
    body = functools.partial(local, mesh.shape["doc"], mesh.shape["clu"])
    return jax.shard_map(
        body, mesh=mesh, in_specs=placed, out_specs=(P("doc", "clu"), P("clu")), check_vma=False
    )
```

```python
import functools
import math

import jax
import jax.numpy as jnp
from jax import lax
from jax.experimental import pallas as pl
from jax.experimental.pallas import tpu as pltpu
from jax.sharding import PartitionSpec as P

ITERS = 2
SMOOTHING = 0.05
LOG2E = math.log2(math.e)
MESH = pl.DeviceIdType.MESH
F32 = jnp.float32


def scattered_kernel(
    nd, nc,
    emb_ref, cent_ref, out_ref, mass_ref,
    emb_all, centers, scores, plan, rpot, colbuf, rowbuf, massbuf, sqbuf, sums, rsbuf, tot, pairbuf,
    own_sem, cent_sem, emb_ss, emb_rs, fwd_ss, col_ss, col_rs, row_ss, row_rs,
    mass_ss, mass_rs, sq_ss, sq_rs, sum_ss, sum_rs, pair_ss, pair_rs,
):
    nz = nd // 2
    nb = 2 * nc
    rows, features = emb_ref.shape
    half = cent_ref.shape[0] // 2
    own_f = features // nd
    log_docs = math.log2(rows * nd * nc)
    log_clusters = math.log2(2 * half * nc)
    d = lax.axis_index("doc")
    c = lax.axis_index("clu")
    core = lax.rem(d, 2)
    z = lax.div(d, 2)
    partner = d + 1 - 2 * core
    me = core * nc + c

    def block_peer(k):
        peer = lax.rem(me + k, nb)
        return peer, (2 * z + lax.div(peer, nc), lax.rem(peer, nc))

    def z_peer(k):
        peer = lax.rem(z + k, nz)
        return peer, (2 * peer + core, c)

    def doc_peer(k):
        peer = lax.rem(d + k, nd)
        return peer, (peer, c)

    def remote(src, dst, ss, rs, device):
        return pltpu.make_async_remote_copy(
            src_ref=src, dst_ref=dst, send_sem=ss, recv_sem=rs,
            device_id=device, device_id_type=MESH,
        )

    sends = []

    def send(*args):
        copy = remote(*args)
        copy.start()
        sends.append(copy)

    own_copy = pltpu.make_async_copy(emb_ref, emb_all.at[me], own_sem)
    own_copy.start()
    cent_copy = pltpu.make_async_copy(
        cent_ref.at[pl.ds(pl.multiple_of(core * half, half), half), :], centers, cent_sem
    )
    cent_copy.start()
    barrier = pltpu.get_barrier_semaphore()
    for k in range(1, nb):
        pl.semaphore_signal(barrier, inc=1, device_id=block_peer(k)[1], device_id_type=MESH)
    for k in range(1, nd):
        pl.semaphore_signal(barrier, inc=1, device_id=doc_peer(k)[1], device_id_type=MESH)

    def col_update(state, t):
        high, total = state
        t = t.reshape(rows // 8, 8, half)
        new = jnp.maximum(high, jnp.max(t, axis=0))
        total = total * jnp.exp2(high - new) + jnp.sum(jnp.exp2(t - new[None]), axis=0)
        return new, total

    state = (jnp.full((8, half), -jnp.inf, F32), jnp.zeros((8, half), F32))

    def first_block(state, slot):
        s = lax.dot_general(
            emb_all[slot], centers[...], (((1,), (1,)), ((), ())), preferred_element_type=F32
        ) * (LOG2E / SMOOTHING)
        scores[slot] = s
        return col_update(state, s)

    def arrive(slot):
        remote(
            emb_all.at[slot], emb_all.at[slot], emb_ss.at[0], emb_rs.at[slot], (partner, c)
        ).wait_recv()

    def clu_peer(k):
        if nc & (nc - 1):
            return lax.rem(c + k, nc)
        bits = [1 << i for i in range(nc.bit_length() - 1)]
        return sum(lax.rem(lax.div(c, b) + k // b, 2) * b for b in bits)

    own_copy.wait()
    cent_copy.wait()
    state = first_block(state, me)
    pl.semaphore_wait(barrier, nb - 1 + nd - 1)

    own = emb_all.at[me]
    for k in reversed(range(1, nc)):
        send(own, own, emb_ss.at[k], emb_rs.at[me], (d, clu_peer(k)))
    send(own, own, emb_ss.at[0], emb_rs.at[me], (partner, c))
    other = 1 - core
    for k in range(1, nc):
        slot = core * nc + clu_peer(k)
        arrive(slot)
        send(emb_all.at[slot], emb_all.at[slot], fwd_ss.at[k], emb_rs.at[slot], (partner, c))
        state = first_block(state, slot)
    for k in range(nc):
        slot = other * nc + clu_peer(k)
        arrive(slot)
        state = first_block(state, slot)

    diagonal = lax.broadcasted_iota(jnp.int32, (rows, rows), 0) == lax.broadcasted_iota(
        jnp.int32, (rows, rows), 1
    )

    def to_lanes(x):
        return jnp.sum(jnp.where(diagonal, x, 0.0), axis=0, keepdims=True)

    def to_sublanes(x):
        return jnp.sum(jnp.where(diagonal, x, 0.0), axis=1, keepdims=True)

    def column_potential(it, state):
        high, total = state
        top = jnp.max(high, axis=0, keepdims=True)
        total = jnp.sum(total * jnp.exp2(high - top), axis=0, keepdims=True)
        colbuf[it, z] = top + jnp.log2(total)
        mine = colbuf.at[it, z]
        for k in range(1, nz):
            send(mine, mine, col_ss.at[it, k], col_rs.at[it, z], z_peer(k)[1])
        for k in range(1, nz):
            peer, device = z_peer(k)
            theirs = colbuf.at[it, peer]
            remote(theirs, theirs, col_ss.at[it, k], col_rs.at[it, peer], device).wait_recv()
        logs = [colbuf[it, s] for s in range(nz)]
        top = functools.reduce(jnp.maximum, logs)
        return -log_clusters - (top + jnp.log2(sum(jnp.exp2(x - top) for x in logs)))

    part = nb // 2

    def row_send(it, h, col_pot):
        def block(b, carry):
            t = scores[h * part + b] + col_pot
            high = jnp.max(t, axis=1, keepdims=True)
            total = jnp.sum(jnp.exp2(t - high), axis=1, keepdims=True)
            rowbuf[it, h, me, pl.ds(b, 1), :] = to_lanes(high + jnp.log2(total))
            return carry

        lax.fori_loop(0, part, block, 0, unroll=4)
        mine = rowbuf.at[it, h, me]
        for k in range(1, nb):
            send(mine, mine, row_ss.at[it, h, k], row_rs.at[it, h, me], block_peer(k)[1])

    def row_receive(it, h):
        for k in range(1, nb):
            peer, device = block_peer(k)
            theirs = rowbuf.at[it, h, peer]
            remote(
                theirs, theirs, row_ss.at[it, h, k], row_rs.at[it, h, peer], device
            ).wait_recv()
        logs = rowbuf[it, h]
        top = jnp.max(logs, axis=0)
        total = jnp.sum(jnp.exp2(logs - top[None]), axis=0)
        rpot[h] = -log_docs - (top + jnp.log2(total))

    for it in range(ITERS):
        if it > 0:
            state = (jnp.full((8, half), -jnp.inf, F32), jnp.zeros((8, half), F32))
            for h in range(2):
                def again(b, state):
                    t = scores[h * part + b] + to_sublanes(rpot[h, pl.ds(b, 1), :])
                    return col_update(state, t)

                row_receive(it - 1, h)
                state = lax.fori_loop(0, part, again, state, unroll=4)
        col_pot = column_potential(it, state)
        for h in range(2):
            row_send(it, h, col_pot)

    mass = jnp.zeros((8, half), F32)
    for h in range(2):
        def plan_block(b, mass):
            t = scores[h * part + b] + to_sublanes(rpot[h, pl.ds(b, 1), :]) + col_pot + log_docs
            p = jnp.exp2(t)
            plan[h, pl.ds(pl.multiple_of(b * rows, rows), rows), :] = p.astype(jnp.bfloat16)
            return mass + jnp.sum(p.reshape(rows // 8, 8, half), axis=0)

        row_receive(ITERS - 1, h)
        mass = lax.fori_loop(0, part, plan_block, mass, unroll=4)
        product = lax.dot_general(
            emb_all[h * part:(h + 1) * part].reshape(part * rows, features), plan[h],
            (((0,), (0,)), ((), ())), preferred_element_type=F32,
        )
        sums[...] = product if h == 0 else sums[...] + product
    massbuf[d] = jnp.sum(mass, axis=0, keepdims=True)
    far = sorted(range(1, nz), key=lambda k: -min(k, nz - k))

    def share(peer):
        return sums.at[pl.ds(pl.multiple_of(peer * 2 * own_f, 2 * own_f), 2 * own_f), :]

    for k in far:
        peer, device = z_peer(k)
        send(share(peer), rsbuf.at[z], sum_ss.at[k], sum_rs.at[z], device)
    for k in range(1, nd):
        send(massbuf.at[d], massbuf.at[d], mass_ss.at[k], mass_rs.at[d], doc_peer(k)[1])
    total = share(z)[...]
    for k in reversed(far):
        peer, device = z_peer(k)
        remote(share(z), rsbuf.at[peer], sum_ss.at[k], sum_rs.at[peer], device).wait_recv()
        total = total + rsbuf[peer]
    tot[...] = total
    sqbuf[d] = jnp.sum(total * total, axis=0, keepdims=True)

    def features_of(which):
        return tot.at[pl.ds(pl.multiple_of(which * own_f, own_f), own_f), :]

    for k in range(1, nd):
        send(sqbuf.at[d], sqbuf.at[d], sq_ss.at[k], sq_rs.at[d], doc_peer(k)[1])
    send(features_of(other), pairbuf, pair_ss, pair_rs, (partner, c))
    for k in range(1, nd):
        peer, device = doc_peer(k)
        theirs = massbuf.at[peer]
        remote(theirs, theirs, mass_ss.at[k], mass_rs.at[peer], device).wait_recv()
        theirs = sqbuf.at[peer]
        remote(theirs, theirs, sq_ss.at[k], sq_rs.at[peer], device).wait_recv()
    remote(features_of(core), pairbuf, pair_ss, pair_rs, (partner, c)).wait_recv()

    def finish(which, block):
        columns = pl.ds(pl.multiple_of(which * half, half), half)
        squares = sum(sqbuf[2 * s + which] for s in range(nz))
        out_ref[:, columns] = block * lax.rsqrt(squares / features + 1e-06)
        mass_ref[:, columns] = sum(massbuf[2 * s + which] for s in range(nz)) * (
            2 * half * nc / (rows * nd * nc)
        )

    finish(core, features_of(core)[...])
    finish(other, pairbuf[...])
    for copy in sends:
        copy.wait_send()


def scattered(nd, nc, embeddings, centroids):
    rows, features = embeddings.shape
    own_cols = centroids.shape[0]
    half, nz, nb = own_cols // 2, nd // 2, 2 * nc
    own_f = features // nd
    dma = pltpu.SemaphoreType.DMA
    out, mass = pl.pallas_call(
        functools.partial(scattered_kernel, nd, nc),
        out_shape=(
            jax.ShapeDtypeStruct((own_f, own_cols), F32),
            jax.ShapeDtypeStruct((1, own_cols), F32),
        ),
        in_specs=[pl.BlockSpec(memory_space=pltpu.HBM)] * 2,
        out_specs=(pl.BlockSpec(memory_space=pltpu.VMEM),) * 2,
        scratch_shapes=[
            pltpu.VMEM((nb, rows, features), jnp.bfloat16),
            pltpu.VMEM((half, features), jnp.bfloat16),
            pltpu.VMEM((nb, rows, half), F32),
            pltpu.VMEM((2, nc * rows, half), jnp.bfloat16),
            pltpu.VMEM((2, nc, rows), F32),
            pltpu.VMEM((ITERS, nz, 1, half), F32),
            pltpu.VMEM((ITERS, 2, nb, nc, rows), F32),
            pltpu.VMEM((nd, 1, half), F32),
            pltpu.VMEM((nd, 1, half), F32),
            pltpu.VMEM((features, half), F32),
            pltpu.VMEM((nz, 2 * own_f, half), F32),
            pltpu.VMEM((2 * own_f, half), F32),
            pltpu.VMEM((own_f, half), F32),
            dma, dma, dma((nc,)), dma((nb,)), dma((nc,)),
            dma((ITERS, nz)), dma((ITERS, nz)), dma((ITERS, 2, nb)), dma((ITERS, 2, nb)),
            dma((nd,)), dma((nd,)), dma((nd,)), dma((nd,)),
            dma((nz,)), dma((nz,)), dma, dma,
        ],
        compiler_params=pltpu.CompilerParams(
            collective_id=0, has_side_effects=True
        ),
    )(embeddings, centroids)
    return out, mass.reshape(own_cols)


def replicated_kernel(
    nd, nc,
    emb_ref, cent_ref, out_ref, mass_ref,
    emb_all, centers, scores, plan, high, total, wide, pots, share, colbuf, rowbuf, sums, finished, pairbuf, pairmass,
    own_sem, cent_sem, own_ss, emb_rs, core_ss, plane_ss, col_ss, col_rs, row_ss, row_rs,
    pot_ss, pot_rs, pair_ss, pair_rs,
):
    nz = nd // 2
    nb = 2 * nc
    rows, features = emb_ref.shape
    half = cent_ref.shape[0] // 2
    own_f = features // nd
    docs, clusters = rows * nd * nc, 2 * half * nc
    log_docs, log_clusters = math.log2(docs), math.log2(clusters)
    d = lax.axis_index("doc")
    c = lax.axis_index("clu")
    core = lax.rem(d, 2)
    other = 1 - core
    z = lax.div(d, 2)
    partner = d + other - core
    me = core * nc + c
    step = min(half, 64)
    tiles = step // 8

    def paired(i, k, n):
        if n & (n - 1):
            return lax.rem(i + k, n)
        bits = [1 << b for b in range(n.bit_length() - 1)]
        return sum(lax.rem(lax.div(i, b) + k // b, 2) * b for b in bits)

    def block_peer(k):
        peer = paired(me, k, nb)
        return peer, (2 * z + lax.div(peer, nc), lax.rem(peer, nc))

    def clu_peer(k):
        return paired(c, k, nc)

    def z_peer(k):
        return paired(z, k, nz)

    def slot_of(plane, side, cluster):
        return plane * nb + side * nc + cluster

    def remote(src, dst, ss, rs, device):
        return pltpu.make_async_remote_copy(
            src_ref=src, dst_ref=dst, send_sem=ss, recv_sem=rs,
            device_id=device, device_id_type=MESH,
        )

    sends = []

    def send(*args):
        copy = remote(*args)
        copy.start()
        sends.append(copy)

    mine = slot_of(z, core, c)
    own = emb_all.at[mine]
    own_copy = pltpu.make_async_copy(emb_ref, own, own_sem)
    own_copy.start()
    cent_copy = pltpu.make_async_copy(
        cent_ref.at[pl.ds(pl.multiple_of(core * half, half), half), :], centers, cent_sem
    )
    cent_copy.start()
    barrier = pltpu.get_barrier_semaphore()
    for k in range(1, nb):
        pl.semaphore_signal(barrier, inc=1, device_id=block_peer(k)[1], device_id_type=MESH)
    for k in range(1, nz):
        pl.semaphore_signal(
            barrier, inc=1, device_id=(2 * z_peer(k) + core, c), device_id_type=MESH
        )

    def score(slot):
        return lax.dot_general(
            centers[...], emb_all[slot], (((1,), (1,)), ((), ())), preferred_element_type=F32
        ) * (LOG2E / SMOOTHING)

    def arrive(slot):
        remote(
            emb_all.at[slot], emb_all.at[slot], own_ss.at[0], emb_rs.at[slot], (partner, c)
        ).wait_recv()

    def to_partner(slot, k):
        send(emb_all.at[slot], emb_all.at[slot], core_ss.at[k], emb_rs.at[slot], (partner, c))

    near = [j for j in range(1, nc) if not j & (j - 1)]
    far = [j for j in range(1, nc) if j & (j - 1)]

    def to_plane(slot, k, which):
        for j in which:
            send(
                emb_all.at[slot], emb_all.at[slot], plane_ss.at[k, j], emb_rs.at[slot],
                (d, clu_peer(j)),
            )

    def pair_scores(k, side, pair):
        slot = slot_of(z_peer(k), side, 2 * pair)
        both = lax.dot_general(
            centers[...], emb_all[pl.ds(slot, 2)].reshape(2 * rows, features),
            (((1,), (1,)), ((), ())), preferred_element_type=F32,
        ) * (LOG2E / SMOOTHING)
        scores[slot] = both[:, :rows] + wide[...]
        scores[slot + 1] = both[:, rows:] + wide[...]

    def plane_scores(k, first, count):
        for j in range(2 * first, 2 * (first + count)):
            arrive(slot_of(z_peer(k), other, clu_peer(j)))
        for j in range(first, first + count):
            for side in (core, other):
                pair_scores(k, side, paired(lax.div(c, 2), j, nc // 2))

    def piece(g):
        return pl.ds(pl.multiple_of(g * step, step), step)

    def column_update(slots, first):
        def body(g, carry):
            at = piece(g)
            ts = [scores[s, at, :] for s in slots]
            old = None if first else high[at, :]
            new = functools.reduce(jnp.maximum, ts if first else ts + [old])
            part = sum(jnp.exp2(t - new) for t in ts)
            total[at, :] = part if first else part + total[at, :] * jnp.exp2(old - new)
            high[at, :] = new
            return carry

        lax.fori_loop(0, half // step, body, 0, unroll=2)

    own_copy.wait()
    pl.semaphore_wait(barrier, nb - 1 + nz - 1)

    to_plane(mine, 0, far + near)
    to_partner(mine, 0)
    for k in range(1, nz):
        send(own, own, own_ss.at[k], emb_rs.at[mine], (2 * z_peer(k) + core, c))
    cent_copy.wait()
    scores[mine] = score(mine)
    column_update([mine], True)
    for k in range(1, nc):
        slot = slot_of(z, core, clu_peer(k))
        arrive(slot)
        to_partner(slot, k)
        scores[slot] = score(slot)
    column_update([slot_of(z, core, clu_peer(k)) for k in range(1, nc)], False)

    def from_plane(k):
        slot = slot_of(z_peer(k), core, c)
        arrive(slot)
        to_plane(slot, k, near)
        to_partner(slot, k * nc)

    def across(k, which):
        for j in which:
            slot = slot_of(z_peer(k), core, clu_peer(j))
            arrive(slot)
            to_partner(slot, k * nc + j)

    if nz > 1:
        from_plane(1)
    for k in range(nc):
        slot = slot_of(z, other, clu_peer(k))
        arrive(slot)
        scores[slot] = score(slot)
        if k % 2:
            column_update([slot_of(z, other, clu_peer(k - 1)), slot], False)
    if nc % 2:
        column_update([slot_of(z, other, clu_peer(nc - 1))], False)

    def spread(x):
        wide[...] = jnp.transpose(jnp.broadcast_to(x, (rows, half)))

    def column_send(it, x):
        colbuf[it, z] = x
        ref = colbuf.at[it, z]
        for k in range(1, nz):
            send(ref, ref, col_ss.at[it, k], col_rs.at[it, z], (2 * z_peer(k) + core, c))

    def column_receive(it):
        for k in range(1, nz):
            theirs = colbuf.at[it, z_peer(k)]
            remote(
                theirs, theirs, col_ss.at[it, k], col_rs.at[it, z_peer(k)], (partner, c)
            ).wait_recv()
        return [colbuf[it, s] for s in range(nz)]

    def row_send(it, k):
        ref = rowbuf.at[it, k, me]
        for j in range(1, nb):
            send(ref, ref, row_ss.at[it, k, j], row_rs.at[it, k, me], block_peer(j)[1])

    def row_receive(it, k):
        for j in range(1, nb):
            peer, device = block_peer(j)
            theirs = rowbuf.at[it, k, peer]
            remote(
                theirs, theirs, row_ss.at[it, k, j], row_rs.at[it, k, peer], device
            ).wait_recv()
        return [rowbuf[it, k, s] for s in range(nb)]

    def folded(x, op):
        return functools.reduce(op, [x[8 * i:8 * i + 8] for i in range(tiles)])

    def row_first(b, carry):
        slot = z * nb + b
        top = jnp.full((8, rows), -jnp.inf, F32)
        for g in range(half // step):
            at = pl.ds(g * step, step)
            t = scores[slot, at, :] + wide[at, :]
            scores[slot, at, :] = t
            top = jnp.maximum(top, folded(t, jnp.maximum))
        top = jnp.max(top, axis=0, keepdims=True)
        acc = jnp.zeros((8, rows), F32)
        for g in range(half // step):
            at = pl.ds(g * step, step)
            acc = acc + folded(jnp.exp2(scores[slot, at, :] - top), jnp.add)
        rowbuf[0, 0, me, pl.ds(b, 1), :] = top + jnp.log2(jnp.sum(acc, axis=0, keepdims=True))
        return carry

    def row_next(it, k, last, b, carry):
        plane = z_peer(k)
        slot = plane * nb + b
        r = pots[plane, pl.ds(b, 1), :]
        acc = jnp.zeros((8, rows), F32)
        for g in range(half // step):
            at = pl.ds(g * step, step)
            t = scores[slot, at, :] + wide[at, :]
            e = jnp.exp2(t + r)
            scores[slot, at, :] = e if last else t
            acc = acc + folded(e, jnp.add)
        rowbuf[it, k, me, pl.ds(b, 1), :] = jnp.sum(acc, axis=0, keepdims=True)
        return carry

    def column_next(g, carry):
        at = piece(g)
        acc = jnp.zeros((step, rows), F32)
        for b in range(nb):
            acc = acc + jnp.exp2(scores[z * nb + b, at, :] + pots[z, pl.ds(b, 1), :])
        total[at, :] = acc
        return carry

    tops = jnp.transpose(high[...])
    top = jnp.max(tops, axis=0, keepdims=True)
    column_send(
        0,
        top + jnp.log2(
            jnp.sum(jnp.transpose(total[...]) * jnp.exp2(tops - top), axis=0, keepdims=True)
        ),
    )
    for k in range(1, nz):
        for j in far:
            slot = slot_of(z, core, clu_peer(j))
            send(
                emb_all.at[slot], emb_all.at[slot], plane_ss.at[k, j], emb_rs.at[slot],
                (2 * z_peer(k) + core, c),
            )
    for k in range(2, nz):
        from_plane(k)
    logs = column_receive(0)
    top = functools.reduce(jnp.maximum, logs)
    spread(-log_clusters - (top + jnp.log2(sum(jnp.exp2(x - top) for x in logs))))
    lax.fori_loop(0, nb, row_first, 0, unroll=8)
    row_send(0, 0)
    for k in range(1, nz):
        across(k, near + far if k == 1 else near)
    for k in range(1, nz):
        plane_scores(k, 0, nc // 2 if k == 1 else 1)
    logs = row_receive(0, 0)
    top = functools.reduce(jnp.maximum, logs)
    pots[z] = -log_docs - (top + jnp.log2(sum(jnp.exp2(x - top) for x in logs)))

    for it in range(1, ITERS):
        last = it == ITERS - 1
        if last:
            ref = pots.at[z]
            for k in range(1, nz):
                send(ref, ref, pot_ss.at[k], pot_rs.at[z], (2 * z_peer(k) + core, c))
        lax.fori_loop(0, half // step, column_next, 0, unroll=8)
        column_send(it, jnp.sum(jnp.transpose(total[...]), axis=0, keepdims=True))
        if it == 1:
            for k in range(2, nz):
                across(k, far)
            for k in range(2, nz):
                plane_scores(k, 1, nc // 2 - 1)
        change = -log_clusters - jnp.log2(sum(column_receive(it)))
        spread(change)
        for k in range(nz if last else 1):
            if k:
                theirs = pots.at[z_peer(k)]
                remote(
                    theirs, theirs, pot_ss.at[k], pot_rs.at[z_peer(k)], (partner, c)
                ).wait_recv()
            lax.fori_loop(0, nb, functools.partial(row_next, it, k, last), 0, unroll=8)
            row_send(it, k)
        if not last:
            pots[z] = pots[z] - log_docs - jnp.log2(sum(row_receive(it, 0)))

    wider = min(half, 256)

    def plane_plan(k):
        plane = z_peer(k)
        share[k] = 1.0 / sum(row_receive(ITERS - 1, k))
        block = emb_all[pl.ds(plane * nb, nb)].reshape(nb * rows, features)
        for g in range(half // wider):
            for i in range(wider // step):
                at = pl.ds(g * wider + i * step, step)
                acc = jnp.zeros((step, rows), F32)
                for b in range(nb):
                    p = scores[plane * nb + b, at, :] * share[k, pl.ds(b, 1), :]
                    plan[at, b * rows:(b + 1) * rows] = p.astype(jnp.bfloat16)
                    acc = acc + p
                total[at, :] = acc + total[at, :] if k else acc
            at = pl.ds(g * wider, wider)
            product = lax.dot_general(
                plan[at, :], block, (((1,), (0,)), ((), ())), preferred_element_type=F32
            )
            sums[at, :] = sums[at, :] + product if k else product

    for k in range(nz):
        plane_plan(k)

    everything = jnp.transpose(sums[...])
    scale = lax.rsqrt(jnp.sum(everything * everything, axis=0, keepdims=True) / features + 1e-06)
    finished[...] = everything * scale
    pairmass[0] = jnp.sum(jnp.transpose(total[...]), axis=0, keepdims=True) * (clusters / docs)

    def features_of(which):
        return finished.at[pl.ds(pl.multiple_of((2 * z + which) * own_f, own_f), own_f), :]

    send(features_of(other), pairbuf, pair_ss.at[0], pair_rs.at[0], (partner, c))
    send(pairmass.at[0], pairmass.at[1], pair_ss.at[1], pair_rs.at[1], (partner, c))
    columns = pl.ds(pl.multiple_of(core * half, half), half)
    out_ref[:, columns] = features_of(core)[...]
    mass_ref[:, columns] = pairmass[0]
    columns = pl.ds(pl.multiple_of(other * half, half), half)
    remote(pairbuf, pairbuf, pair_ss.at[0], pair_rs.at[0], (partner, c)).wait_recv()
    out_ref[:, columns] = pairbuf[...]
    remote(
        pairmass.at[1], pairmass.at[1], pair_ss.at[1], pair_rs.at[1], (partner, c)
    ).wait_recv()
    mass_ref[:, columns] = pairmass[1]
    for copy in sends:
        copy.wait_send()


def store_kernel(part_ref, mass_ref, out_ref, total_ref):
    out_ref[...] = part_ref[...]
    total_ref[...] = mass_ref[...].reshape(total_ref.shape)


def replicated(nd, nc, embeddings, centroids):
    rows, features = embeddings.shape
    own_cols = centroids.shape[0]
    half, nz, nb = own_cols // 2, nd // 2, 2 * nc
    own_f = features // nd
    dma = pltpu.SemaphoreType.DMA
    out, mass = pl.pallas_call(
        functools.partial(replicated_kernel, nd, nc),
        out_shape=(
            jax.ShapeDtypeStruct((own_f, own_cols), F32),
            jax.ShapeDtypeStruct((1, own_cols), F32),
        ),
        in_specs=[pl.BlockSpec(memory_space=pltpu.HBM)] * 2,
        out_specs=(pl.BlockSpec(memory_space=pltpu.VMEM),) * 2,
        scratch_shapes=[
            pltpu.VMEM((nz * nb, rows, features), jnp.bfloat16),
            pltpu.VMEM((half, features), jnp.bfloat16),
            pltpu.VMEM((nz * nb, half, rows), F32),
            pltpu.VMEM((half, nb * rows), jnp.bfloat16),
            pltpu.VMEM((half, rows), F32),
            pltpu.VMEM((half, rows), F32),
            pltpu.VMEM((half, rows), F32),
            pltpu.VMEM((nz, nb, rows), F32),
            pltpu.VMEM((nz, nb, rows), F32),
            pltpu.VMEM((ITERS, nz, 1, half), F32),
            pltpu.VMEM((ITERS, nz, nb, nb, rows), F32),
            pltpu.VMEM((half, features), F32),
            pltpu.VMEM((features, half), F32),
            pltpu.VMEM((own_f, half), F32),
            pltpu.VMEM((2, 1, half), F32),
            dma, dma, dma((nz,)), dma((nz * nb,)), dma((nz * nc,)), dma((nz, nc)),
            dma((ITERS, nz)), dma((ITERS, nz)), dma((ITERS, nz, nb)), dma((ITERS, nz, nb)),
            dma((nz,)), dma((nz,)), dma((2,)), dma((2,)),
        ],
        compiler_params=pltpu.CompilerParams(
            collective_id=0, has_side_effects=True, vmem_limit_bytes=VMEM_BYTES
        ),
    )(*(pltpu.with_memory_space_constraint(a, pltpu.HBM) for a in (embeddings, centroids)))
    return pl.pallas_call(
        store_kernel,
        out_shape=(
            jax.ShapeDtypeStruct((own_f, own_cols), F32),
            jax.ShapeDtypeStruct((own_cols,), F32),
        ),
        in_specs=[pl.BlockSpec(memory_space=pltpu.VMEM)] * 2,
        out_specs=(pl.BlockSpec(memory_space=pltpu.VMEM),) * 2,
        compiler_params=pltpu.CompilerParams(vmem_limit_bytes=4 << 20),
    )(out, mass)


VMEM_BYTES = 48 << 20


def local(nd, nc, embeddings, centroids):
    rows, features = embeddings.shape
    docs = rows * nd * nc
    half = centroids.shape[0] // 2
    held = docs * (2 * features + 4 * half)
    fits = 2 * held <= VMEM_BYTES and nd > 2 and nc > 1 and not nc & (nc - 1)
    form = replicated if fits else scattered
    return form(nd, nc, embeddings, centroids)


def solution(mesh):
    placed = (P(("doc", "clu"), None), P("clu", None))
    body = functools.partial(local, mesh.shape["doc"], mesh.shape["clu"])
    return jax.shard_map(
        body, mesh=mesh, in_specs=placed, out_specs=(P("doc", "clu"), P("clu")), check_vma=False
    )
```

```python
import functools
import math

import jax
import jax.numpy as jnp
from jax import lax
from jax.experimental import pallas as pl
from jax.experimental.pallas import tpu as pltpu
from jax.sharding import PartitionSpec as P

ITERS = 2
SMOOTHING = 0.05
LOG2E = math.log2(math.e)
MESH = pl.DeviceIdType.MESH
F32 = jnp.float32


def scattered_kernel(
    nd, nc,
    emb_ref, cent_ref, out_ref, mass_ref,
    emb_all, centers, scores, plan, rpot, colbuf, rowbuf, massbuf, sqbuf, sums, rsbuf, tot, pairbuf,
    own_sem, cent_sem, emb_ss, emb_rs, fwd_ss, col_ss, col_rs, row_ss, row_rs,
    mass_ss, mass_rs, sq_ss, sq_rs, sum_ss, sum_rs, pair_ss, pair_rs,
):
    nz = nd // 2
    nb = 2 * nc
    rows, features = emb_ref.shape
    half = cent_ref.shape[0] // 2
    own_f = features // nd
    log_docs = math.log2(rows * nd * nc)
    log_clusters = math.log2(2 * half * nc)
    d = lax.axis_index("doc")
    c = lax.axis_index("clu")
    core = lax.rem(d, 2)
    z = lax.div(d, 2)
    partner = d + 1 - 2 * core
    me = core * nc + c

    def block_peer(k):
        peer = lax.rem(me + k, nb)
        return peer, (2 * z + lax.div(peer, nc), lax.rem(peer, nc))

    def z_peer(k):
        peer = lax.rem(z + k, nz)
        return peer, (2 * peer + core, c)

    def doc_peer(k):
        peer = lax.rem(d + k, nd)
        return peer, (peer, c)

    def remote(src, dst, ss, rs, device):
        return pltpu.make_async_remote_copy(
            src_ref=src, dst_ref=dst, send_sem=ss, recv_sem=rs,
            device_id=device, device_id_type=MESH,
        )

    sends = []

    def send(*args):
        copy = remote(*args)
        copy.start()
        sends.append(copy)

    own_copy = pltpu.make_async_copy(emb_ref, emb_all.at[me], own_sem)
    own_copy.start()
    cent_copy = pltpu.make_async_copy(
        cent_ref.at[pl.ds(pl.multiple_of(core * half, half), half), :], centers, cent_sem
    )
    cent_copy.start()
    barrier = pltpu.get_barrier_semaphore()
    for k in range(1, nb):
        pl.semaphore_signal(barrier, inc=1, device_id=block_peer(k)[1], device_id_type=MESH)
    for k in range(1, nd):
        pl.semaphore_signal(barrier, inc=1, device_id=doc_peer(k)[1], device_id_type=MESH)

    def col_update(state, t):
        high, total = state
        t = t.reshape(rows // 8, 8, half)
        new = jnp.maximum(high, jnp.max(t, axis=0))
        total = total * jnp.exp2(high - new) + jnp.sum(jnp.exp2(t - new[None]), axis=0)
        return new, total

    state = (jnp.full((8, half), -jnp.inf, F32), jnp.zeros((8, half), F32))

    def first_block(state, slot):
        s = lax.dot_general(
            emb_all[slot], centers[...], (((1,), (1,)), ((), ())), preferred_element_type=F32
        ) * (LOG2E / SMOOTHING)
        scores[slot] = s
        return col_update(state, s)

    def arrive(slot):
        remote(
            emb_all.at[slot], emb_all.at[slot], emb_ss.at[0], emb_rs.at[slot], (partner, c)
        ).wait_recv()

    def clu_peer(k):
        if nc & (nc - 1):
            return lax.rem(c + k, nc)
        bits = [1 << i for i in range(nc.bit_length() - 1)]
        return sum(lax.rem(lax.div(c, b) + k // b, 2) * b for b in bits)

    own_copy.wait()
    cent_copy.wait()
    state = first_block(state, me)
    pl.semaphore_wait(barrier, nb - 1 + nd - 1)

    own = emb_all.at[me]
    for k in reversed(range(1, nc)):
        send(own, own, emb_ss.at[k], emb_rs.at[me], (d, clu_peer(k)))
    send(own, own, emb_ss.at[0], emb_rs.at[me], (partner, c))
    other = 1 - core
    for k in range(1, nc):
        slot = core * nc + clu_peer(k)
        arrive(slot)
        send(emb_all.at[slot], emb_all.at[slot], fwd_ss.at[k], emb_rs.at[slot], (partner, c))
        state = first_block(state, slot)
    for k in range(nc):
        slot = other * nc + clu_peer(k)
        arrive(slot)
        state = first_block(state, slot)

    diagonal = lax.broadcasted_iota(jnp.int32, (rows, rows), 0) == lax.broadcasted_iota(
        jnp.int32, (rows, rows), 1
    )

    def to_lanes(x):
        return jnp.sum(jnp.where(diagonal, x, 0.0), axis=0, keepdims=True)

    def to_sublanes(x):
        return jnp.sum(jnp.where(diagonal, x, 0.0), axis=1, keepdims=True)

    def column_potential(it, state):
        high, total = state
        top = jnp.max(high, axis=0, keepdims=True)
        total = jnp.sum(total * jnp.exp2(high - top), axis=0, keepdims=True)
        colbuf[it, z] = top + jnp.log2(total)
        mine = colbuf.at[it, z]
        for k in range(1, nz):
            send(mine, mine, col_ss.at[it, k], col_rs.at[it, z], z_peer(k)[1])
        for k in range(1, nz):
            peer, device = z_peer(k)
            theirs = colbuf.at[it, peer]
            remote(theirs, theirs, col_ss.at[it, k], col_rs.at[it, peer], device).wait_recv()
        logs = [colbuf[it, s] for s in range(nz)]
        top = functools.reduce(jnp.maximum, logs)
        return -log_clusters - (top + jnp.log2(sum(jnp.exp2(x - top) for x in logs)))

    part = nb // 2

    def row_send(it, h, col_pot):
        def block(b, carry):
            t = scores[h * part + b] + col_pot
            high = jnp.max(t, axis=1, keepdims=True)
            total = jnp.sum(jnp.exp2(t - high), axis=1, keepdims=True)
            rowbuf[it, h, me, pl.ds(b, 1), :] = to_lanes(high + jnp.log2(total))
            return carry

        lax.fori_loop(0, part, block, 0, unroll=4)
        mine = rowbuf.at[it, h, me]
        for k in range(1, nb):
            send(mine, mine, row_ss.at[it, h, k], row_rs.at[it, h, me], block_peer(k)[1])

    def row_receive(it, h):
        for k in range(1, nb):
            peer, device = block_peer(k)
            theirs = rowbuf.at[it, h, peer]
            remote(
                theirs, theirs, row_ss.at[it, h, k], row_rs.at[it, h, peer], device
            ).wait_recv()
        logs = rowbuf[it, h]
        top = jnp.max(logs, axis=0)
        total = jnp.sum(jnp.exp2(logs - top[None]), axis=0)
        rpot[h] = -log_docs - (top + jnp.log2(total))

    for it in range(ITERS):
        if it > 0:
            state = (jnp.full((8, half), -jnp.inf, F32), jnp.zeros((8, half), F32))
            for h in range(2):
                def again(b, state):
                    t = scores[h * part + b] + to_sublanes(rpot[h, pl.ds(b, 1), :])
                    return col_update(state, t)

                row_receive(it - 1, h)
                state = lax.fori_loop(0, part, again, state, unroll=4)
        col_pot = column_potential(it, state)
        for h in range(2):
            row_send(it, h, col_pot)

    mass = jnp.zeros((8, half), F32)
    for h in range(2):
        def plan_block(b, mass):
            t = scores[h * part + b] + to_sublanes(rpot[h, pl.ds(b, 1), :]) + col_pot + log_docs
            p = jnp.exp2(t)
            plan[h, pl.ds(pl.multiple_of(b * rows, rows), rows), :] = p.astype(jnp.bfloat16)
            return mass + jnp.sum(p.reshape(rows // 8, 8, half), axis=0)

        row_receive(ITERS - 1, h)
        mass = lax.fori_loop(0, part, plan_block, mass, unroll=4)
        product = lax.dot_general(
            emb_all[h * part:(h + 1) * part].reshape(part * rows, features), plan[h],
            (((0,), (0,)), ((), ())), preferred_element_type=F32,
        )
        sums[...] = product if h == 0 else sums[...] + product
    massbuf[d] = jnp.sum(mass, axis=0, keepdims=True)
    far = sorted(range(1, nz), key=lambda k: -min(k, nz - k))

    def share(peer):
        return sums.at[pl.ds(pl.multiple_of(peer * 2 * own_f, 2 * own_f), 2 * own_f), :]

    for k in far:
        peer, device = z_peer(k)
        send(share(peer), rsbuf.at[z], sum_ss.at[k], sum_rs.at[z], device)
    for k in range(1, nd):
        send(massbuf.at[d], massbuf.at[d], mass_ss.at[k], mass_rs.at[d], doc_peer(k)[1])
    total = share(z)[...]
    for k in reversed(far):
        peer, device = z_peer(k)
        remote(share(z), rsbuf.at[peer], sum_ss.at[k], sum_rs.at[peer], device).wait_recv()
        total = total + rsbuf[peer]
    tot[...] = total
    sqbuf[d] = jnp.sum(total * total, axis=0, keepdims=True)

    def features_of(which):
        return tot.at[pl.ds(pl.multiple_of(which * own_f, own_f), own_f), :]

    for k in range(1, nd):
        send(sqbuf.at[d], sqbuf.at[d], sq_ss.at[k], sq_rs.at[d], doc_peer(k)[1])
    send(features_of(other), pairbuf, pair_ss, pair_rs, (partner, c))
    for k in range(1, nd):
        peer, device = doc_peer(k)
        theirs = massbuf.at[peer]
        remote(theirs, theirs, mass_ss.at[k], mass_rs.at[peer], device).wait_recv()
        theirs = sqbuf.at[peer]
        remote(theirs, theirs, sq_ss.at[k], sq_rs.at[peer], device).wait_recv()
    remote(features_of(core), pairbuf, pair_ss, pair_rs, (partner, c)).wait_recv()

    def finish(which, block):
        columns = pl.ds(pl.multiple_of(which * half, half), half)
        squares = sum(sqbuf[2 * s + which] for s in range(nz))
        out_ref[:, columns] = block * lax.rsqrt(squares / features + 1e-06)
        mass_ref[:, columns] = sum(massbuf[2 * s + which] for s in range(nz)) * (
            2 * half * nc / (rows * nd * nc)
        )

    finish(core, features_of(core)[...])
    finish(other, pairbuf[...])
    for copy in sends:
        copy.wait_send()


def scattered(nd, nc, embeddings, centroids):
    rows, features = embeddings.shape
    own_cols = centroids.shape[0]
    half, nz, nb = own_cols // 2, nd // 2, 2 * nc
    own_f = features // nd
    dma = pltpu.SemaphoreType.DMA
    out, mass = pl.pallas_call(
        functools.partial(scattered_kernel, nd, nc),
        out_shape=(
            jax.ShapeDtypeStruct((own_f, own_cols), F32),
            jax.ShapeDtypeStruct((1, own_cols), F32),
        ),
        in_specs=[pl.BlockSpec(memory_space=pltpu.HBM)] * 2,
        out_specs=(pl.BlockSpec(memory_space=pltpu.VMEM),) * 2,
        scratch_shapes=[
            pltpu.VMEM((nb, rows, features), jnp.bfloat16),
            pltpu.VMEM((half, features), jnp.bfloat16),
            pltpu.VMEM((nb, rows, half), F32),
            pltpu.VMEM((2, nc * rows, half), jnp.bfloat16),
            pltpu.VMEM((2, nc, rows), F32),
            pltpu.VMEM((ITERS, nz, 1, half), F32),
            pltpu.VMEM((ITERS, 2, nb, nc, rows), F32),
            pltpu.VMEM((nd, 1, half), F32),
            pltpu.VMEM((nd, 1, half), F32),
            pltpu.VMEM((features, half), F32),
            pltpu.VMEM((nz, 2 * own_f, half), F32),
            pltpu.VMEM((2 * own_f, half), F32),
            pltpu.VMEM((own_f, half), F32),
            dma, dma, dma((nc,)), dma((nb,)), dma((nc,)),
            dma((ITERS, nz)), dma((ITERS, nz)), dma((ITERS, 2, nb)), dma((ITERS, 2, nb)),
            dma((nd,)), dma((nd,)), dma((nd,)), dma((nd,)),
            dma((nz,)), dma((nz,)), dma, dma,
        ],
        compiler_params=pltpu.CompilerParams(
            collective_id=0, has_side_effects=True
        ),
    )(embeddings, centroids)
    return out, mass.reshape(own_cols)


def replicated_kernel(
    nd, nc,
    emb_ref, cent_ref, out_ref, mass_ref,
    emb_all, centers, scores, plan, high, total, wide, pots, share, colbuf, rowbuf, sums, finished, pairbuf, pairmass,
    own_sem, cent_sem, own_ss, emb_rs, core_ss, plane_ss, col_ss, col_rs, row_ss, row_rs,
    pot_ss, pot_rs, pair_ss, pair_rs,
):
    nz = nd // 2
    nb = 2 * nc
    rows, features = emb_ref.shape
    half = cent_ref.shape[0] // 2
    own_f = features // nd
    docs, clusters = rows * nd * nc, 2 * half * nc
    log_docs, log_clusters = math.log2(docs), math.log2(clusters)
    d = lax.axis_index("doc")
    c = lax.axis_index("clu")
    core = lax.rem(d, 2)
    other = 1 - core
    z = lax.div(d, 2)
    partner = d + other - core
    me = core * nc + c
    step = min(half, 64)
    tiles = step // 8

    def paired(i, k, n):
        if n & (n - 1):
            return lax.rem(i + k, n)
        bits = [1 << b for b in range(n.bit_length() - 1)]
        return sum(lax.rem(lax.div(i, b) + k // b, 2) * b for b in bits)

    block_peers = [paired(me, k, nb) for k in range(nb)]
    block_peers = [(p, (2 * z + lax.div(p, nc), lax.rem(p, nc))) for p in block_peers]
    clu_peers = [paired(c, k, nc) for k in range(nc)]
    z_peers = [paired(z, k, nz) for k in range(nz)]

    pair_peers = [paired(lax.div(c, 2), k, nc // 2) for k in range(nc // 2)]

    def block_peer(k):
        return block_peers[k]

    def clu_peer(k):
        return clu_peers[k]

    def z_peer(k):
        return z_peers[k]

    def slot_of(plane, side, cluster):
        return plane * nb + side * nc + cluster

    def remote(src, dst, ss, rs, device):
        return pltpu.make_async_remote_copy(
            src_ref=src, dst_ref=dst, send_sem=ss, recv_sem=rs,
            device_id=device, device_id_type=MESH,
        )

    sends = []

    def send(*args):
        copy = remote(*args)
        copy.start()
        sends.append(copy)

    mine = slot_of(z, core, c)
    own = emb_all.at[mine]
    own_copy = pltpu.make_async_copy(emb_ref, own, own_sem)
    own_copy.start()
    cent_copy = pltpu.make_async_copy(
        cent_ref.at[pl.ds(pl.multiple_of(core * half, half), half), :], centers, cent_sem
    )
    cent_copy.start()
    barrier = pltpu.get_barrier_semaphore()
    for k in range(1, nb):
        pl.semaphore_signal(barrier, inc=1, device_id=block_peer(k)[1], device_id_type=MESH)
    for k in range(1, nz):
        pl.semaphore_signal(
            barrier, inc=1, device_id=(2 * z_peer(k) + core, c), device_id_type=MESH
        )

    def score(slot):
        return lax.dot_general(
            centers[...], emb_all[slot], (((1,), (1,)), ((), ())), preferred_element_type=F32
        ) * (LOG2E / SMOOTHING)

    def arrive(slot):
        remote(
            emb_all.at[slot], emb_all.at[slot], own_ss.at[0], emb_rs.at[slot], (partner, c)
        ).wait_recv()

    def to_partner(slot, k):
        send(emb_all.at[slot], emb_all.at[slot], core_ss.at[k], emb_rs.at[slot], (partner, c))

    near = [j for j in range(1, nc) if not j & (j - 1)]
    far = [j for j in range(1, nc) if j & (j - 1)]

    def to_plane(slot, k, which):
        for j in which:
            send(
                emb_all.at[slot], emb_all.at[slot], plane_ss.at[k, j], emb_rs.at[slot],
                (d, clu_peer(j)),
            )

    def pair_scores(k, side, pair):
        slot = slot_of(z_peer(k), side, 2 * pair)
        both = lax.dot_general(
            centers[...], emb_all[pl.ds(slot, 2)].reshape(2 * rows, features),
            (((1,), (1,)), ((), ())), preferred_element_type=F32,
        ) * (LOG2E / SMOOTHING)
        for n in range(2):
            block = both[:, n * rows:(n + 1) * rows]
            scores[slot + n] = block + wide[...] if k else block
        return slot, slot + 1

    def plane_scores(k, first, count):
        for j in range(2 * first, 2 * (first + count)):
            arrive(slot_of(z_peer(k), other, clu_peer(j)))
        for j in range(first, first + count):
            for side in (core, other):
                pair_scores(k, side, pair_peers[j])

    def piece(g):
        return pl.ds(pl.multiple_of(g * step, step), step)

    def column_update(slots, first):
        def body(g, carry):
            at = piece(g)
            ts = [scores[s, at, :] for s in slots]
            old = None if first else high[at, :]
            new = functools.reduce(jnp.maximum, ts if first else ts + [old])
            part = sum(jnp.exp2(t - new) for t in ts)
            total[at, :] = part if first else part + total[at, :] * jnp.exp2(old - new)
            high[at, :] = new
            return carry

        lax.fori_loop(0, half // step, body, 0, unroll=4)

    own_copy.wait()
    pl.semaphore_wait(barrier, nb - 1 + nz - 1)

    to_plane(mine, 0, far + near)
    to_partner(mine, 0)
    for k in range(1, nz):
        send(own, own, own_ss.at[k], emb_rs.at[mine], (2 * z_peer(k) + core, c))
    cent_copy.wait()
    scores[mine] = score(mine)
    column_update([mine], True)
    slot = slot_of(z, core, clu_peer(1))
    arrive(slot)
    to_partner(slot, 1)
    scores[slot] = score(slot)
    column_update([slot], False)
    for j in range(1, nc // 2):
        for k in (2 * j, 2 * j + 1):
            slot = slot_of(z, core, clu_peer(k))
            arrive(slot)
            to_partner(slot, k)
        column_update(pair_scores(0, core, pair_peers[j]), False)

    def from_plane(k):
        slot = slot_of(z_peer(k), core, c)
        arrive(slot)
        to_plane(slot, k, near)
        to_partner(slot, k * nc)

    def across(k, which):
        for j in which:
            slot = slot_of(z_peer(k), core, clu_peer(j))
            arrive(slot)
            to_partner(slot, k * nc + j)

    if nz > 1:
        from_plane(1)
    for j in range(nc // 2):
        for k in (2 * j, 2 * j + 1):
            arrive(slot_of(z, other, clu_peer(k)))
        column_update(pair_scores(0, other, pair_peers[j]), False)

    def spread(x):
        wide[...] = jnp.transpose(jnp.broadcast_to(x, (rows, half)))

    def column_send(it, x):
        colbuf[it, z] = x
        ref = colbuf.at[it, z]
        for k in range(1, nz):
            send(ref, ref, col_ss.at[it, k], col_rs.at[it, z], (2 * z_peer(k) + core, c))

    def column_receive(it):
        for k in range(1, nz):
            theirs = colbuf.at[it, z_peer(k)]
            remote(
                theirs, theirs, col_ss.at[it, k], col_rs.at[it, z_peer(k)], (partner, c)
            ).wait_recv()
        return [colbuf[it, s] for s in range(nz)]

    def row_send(it, k):
        ref = rowbuf.at[it, k, me]
        for j in range(1, nb):
            send(ref, ref, row_ss.at[it, k, j], row_rs.at[it, k, me], block_peer(j)[1])

    def row_receive(it, k):
        for j in range(1, nb):
            peer, device = block_peer(j)
            theirs = rowbuf.at[it, k, peer]
            remote(
                theirs, theirs, row_ss.at[it, k, j], row_rs.at[it, k, peer], device
            ).wait_recv()
        return [rowbuf[it, k, s] for s in range(nb)]

    def folded(x, op):
        return functools.reduce(op, [x[8 * i:8 * i + 8] for i in range(tiles)])

    def rows_of(parts, op):
        return jnp.concatenate([op(x, axis=0, keepdims=True) for x in parts], axis=0)

    def row_first():
        def shift(g, tops):
            at = piece(g)
            w = wide[at, :]
            new = []
            for b in range(nb):
                t = scores[z * nb + b, at, :] + w
                scores[z * nb + b, at, :] = t
                new.append(jnp.maximum(tops[b], folded(t, jnp.maximum)))
            return tuple(new)

        def add(g, accs):
            at = piece(g)
            return tuple(
                accs[b] + folded(jnp.exp2(scores[z * nb + b, at, :] - top[b:b + 1]), jnp.add)
                for b in range(nb)
            )

        count = half // step
        low = (jnp.full((8, rows), -jnp.inf, F32),) * nb
        top = rows_of(lax.fori_loop(0, count, shift, low, unroll=count), jnp.max)
        zero = (jnp.zeros((8, rows), F32),) * nb
        total = rows_of(lax.fori_loop(0, count, add, zero, unroll=count), jnp.sum)
        rowbuf[0, 0, me] = top + jnp.log2(total)

    def row_next(it, k, last):
        plane = z_peer(k)

        def body(g, accs):
            at = piece(g)
            w = wide[at, :]
            new = []
            for b in range(nb):
                t = scores[plane * nb + b, at, :] + w
                e = jnp.exp2(t + r[b:b + 1])
                scores[plane * nb + b, at, :] = e if last else t
                new.append(accs[b] + folded(e, jnp.add))
            return tuple(new)

        r = pots[plane]
        zero = (jnp.zeros((8, rows), F32),) * nb
        found = lax.fori_loop(0, half // step, body, zero, unroll=half // step)
        rowbuf[it, k, me] = rows_of(found, jnp.sum)

    def column_next(g, carry):
        at = piece(g)
        acc = jnp.zeros((step, rows), F32)
        for b in range(nb):
            acc = acc + jnp.exp2(scores[z * nb + b, at, :] + pots[z, pl.ds(b, 1), :])
        total[at, :] = acc
        return carry

    tops = jnp.transpose(high[...])
    top = jnp.max(tops, axis=0, keepdims=True)
    column_send(
        0,
        top + jnp.log2(
            jnp.sum(jnp.transpose(total[...]) * jnp.exp2(tops - top), axis=0, keepdims=True)
        ),
    )
    for k in range(1, nz):
        for j in far:
            slot = slot_of(z, core, clu_peer(j))
            send(
                emb_all.at[slot], emb_all.at[slot], plane_ss.at[k, j], emb_rs.at[slot],
                (2 * z_peer(k) + core, c),
            )
    for k in range(2, nz):
        from_plane(k)
    logs = column_receive(0)
    top = functools.reduce(jnp.maximum, logs)
    spread(-log_clusters - (top + jnp.log2(sum(jnp.exp2(x - top) for x in logs))))
    row_first()
    row_send(0, 0)
    for k in range(1, nz):
        across(k, near + far if k == 1 else near)
    for k in range(1, nz):
        plane_scores(k, 0, nc // 2 if k == 1 else 1)
    logs = row_receive(0, 0)
    top = functools.reduce(jnp.maximum, logs)
    pots[z] = -log_docs - (top + jnp.log2(sum(jnp.exp2(x - top) for x in logs)))

    for it in range(1, ITERS):
        last = it == ITERS - 1
        if last:
            gone = list(sends)
            sends.clear()
            ref = pots.at[z]
            for k in range(1, nz):
                send(ref, ref, pot_ss.at[k], pot_rs.at[z], (2 * z_peer(k) + core, c))
        lax.fori_loop(0, half // step, column_next, 0, unroll=8)
        column_send(it, jnp.sum(jnp.transpose(total[...]), axis=0, keepdims=True))
        if it == 1:
            for k in range(2, nz):
                across(k, far)
            for k in range(2, nz):
                plane_scores(k, 1, nc // 2 - 1)
        change = -log_clusters - jnp.log2(sum(column_receive(it)))
        spread(change)
        for k in range(nz if last else 1):
            if k:
                theirs = pots.at[z_peer(k)]
                remote(
                    theirs, theirs, pot_ss.at[k], pot_rs.at[z_peer(k)], (partner, c)
                ).wait_recv()
            row_next(it, k, last)
            row_send(it, k)
        if not last:
            pots[z] = pots[z] - log_docs - jnp.log2(sum(row_receive(it, 0)))

    for copy in gone:
        copy.wait_send()
    wider = min(half, 256)

    def plane_plan(k):
        plane = z_peer(k)
        share[k] = 1.0 / sum(row_receive(ITERS - 1, k))
        block = emb_all[pl.ds(plane * nb, nb)].reshape(nb * rows, features)
        for g in range(half // wider):
            for i in range(wider // step):
                at = pl.ds(g * wider + i * step, step)
                acc = jnp.zeros((step, rows), F32)
                for b in range(nb):
                    p = scores[plane * nb + b, at, :] * share[k, pl.ds(b, 1), :]
                    plan[at, b * rows:(b + 1) * rows] = p.astype(jnp.bfloat16)
                    acc = acc + p
                total[at, :] = acc + total[at, :] if k else acc
            at = pl.ds(g * wider, wider)
            product = lax.dot_general(
                plan[at, :], block, (((1,), (0,)), ((), ())), preferred_element_type=F32
            )
            sums[at, :] = sums[at, :] + product if k else product

    for k in range(nz):
        plane_plan(k)

    everything = jnp.transpose(sums[...])
    scale = lax.rsqrt(jnp.sum(everything * everything, axis=0, keepdims=True) / features + 1e-06)
    finished[...] = everything * scale
    pairmass[0] = jnp.sum(jnp.transpose(total[...]), axis=0, keepdims=True) * (clusters / docs)

    def features_of(which):
        return finished.at[pl.ds(pl.multiple_of((2 * z + which) * own_f, own_f), own_f), :]

    send(features_of(other), pairbuf, pair_ss.at[0], pair_rs.at[0], (partner, c))
    send(pairmass.at[0], pairmass.at[1], pair_ss.at[1], pair_rs.at[1], (partner, c))
    columns = pl.ds(pl.multiple_of(core * half, half), half)
    out_ref[:, columns] = features_of(core)[...]
    mass_ref[:, columns] = pairmass[0]
    for copy in sends:
        copy.wait_send()
    columns = pl.ds(pl.multiple_of(other * half, half), half)
    remote(pairbuf, pairbuf, pair_ss.at[0], pair_rs.at[0], (partner, c)).wait_recv()
    out_ref[:, columns] = pairbuf[...]
    remote(
        pairmass.at[1], pairmass.at[1], pair_ss.at[1], pair_rs.at[1], (partner, c)
    ).wait_recv()
    mass_ref[:, columns] = pairmass[1]


def store_kernel(part_ref, mass_ref, out_ref, total_ref):
    out_ref[...] = part_ref[...]
    total_ref[...] = mass_ref[...].reshape(total_ref.shape)


def replicated(nd, nc, embeddings, centroids):
    rows, features = embeddings.shape
    own_cols = centroids.shape[0]
    half, nz, nb = own_cols // 2, nd // 2, 2 * nc
    own_f = features // nd
    dma = pltpu.SemaphoreType.DMA
    out, mass = pl.pallas_call(
        functools.partial(replicated_kernel, nd, nc),
        out_shape=(
            jax.ShapeDtypeStruct((own_f, own_cols), F32),
            jax.ShapeDtypeStruct((1, own_cols), F32),
        ),
        in_specs=[pl.BlockSpec(memory_space=pltpu.HBM)] * 2,
        out_specs=(pl.BlockSpec(memory_space=pltpu.VMEM),) * 2,
        scratch_shapes=[
            pltpu.VMEM((nz * nb, rows, features), jnp.bfloat16),
            pltpu.VMEM((half, features), jnp.bfloat16),
            pltpu.VMEM((nz * nb, half, rows), F32),
            pltpu.VMEM((half, nb * rows), jnp.bfloat16),
            pltpu.VMEM((half, rows), F32),
            pltpu.VMEM((half, rows), F32),
            pltpu.VMEM((half, rows), F32),
            pltpu.VMEM((nz, nb, rows), F32),
            pltpu.VMEM((nz, nb, rows), F32),
            pltpu.VMEM((ITERS, nz, 1, half), F32),
            pltpu.VMEM((ITERS, nz, nb, nb, rows), F32),
            pltpu.VMEM((half, features), F32),
            pltpu.VMEM((features, half), F32),
            pltpu.VMEM((own_f, half), F32),
            pltpu.VMEM((2, 1, half), F32),
            dma, dma, dma((nz,)), dma((nz * nb,)), dma((nz * nc,)), dma((nz, nc)),
            dma((ITERS, nz)), dma((ITERS, nz)), dma((ITERS, nz, nb)), dma((ITERS, nz, nb)),
            dma((nz,)), dma((nz,)), dma((2,)), dma((2,)),
        ],
        compiler_params=pltpu.CompilerParams(
            collective_id=0, has_side_effects=True, vmem_limit_bytes=VMEM_BYTES
        ),
    )(*(pltpu.with_memory_space_constraint(a, pltpu.HBM) for a in (embeddings, centroids)))
    return pl.pallas_call(
        store_kernel,
        out_shape=(
            jax.ShapeDtypeStruct((own_f, own_cols), F32),
            jax.ShapeDtypeStruct((own_cols,), F32),
        ),
        in_specs=[pl.BlockSpec(memory_space=pltpu.VMEM)] * 2,
        out_specs=(pl.BlockSpec(memory_space=pltpu.VMEM),) * 2,
        compiler_params=pltpu.CompilerParams(vmem_limit_bytes=4 << 20),
    )(out, mass)


VMEM_BYTES = 48 << 20


def local(nd, nc, embeddings, centroids):
    rows, features = embeddings.shape
    docs = rows * nd * nc
    half = centroids.shape[0] // 2
    held = docs * (2 * features + 4 * half)
    fits = 2 * held <= VMEM_BYTES and nd > 2 and nc > 1 and not nc & (nc - 1)
    form = replicated if fits else scattered
    return form(nd, nc, embeddings, centroids)


def solution(mesh):
    placed = (P(("doc", "clu"), None), P("clu", None))
    body = functools.partial(local, mesh.shape["doc"], mesh.shape["clu"])
    return jax.shard_map(
        body, mesh=mesh, in_specs=placed, out_specs=(P("doc", "clu"), P("clu")), check_vma=False
    )
```

```python
import functools
import math

import jax
import jax.numpy as jnp
from jax import lax
from jax.experimental import pallas as pl
from jax.experimental.pallas import tpu as pltpu
from jax.sharding import PartitionSpec as P

ITERS = 2
SMOOTHING = 0.05
LOG2E = math.log2(math.e)
MESH = pl.DeviceIdType.MESH
F32 = jnp.float32


def scattered_kernel(
    nd, nc,
    emb_ref, cent_ref, out_ref, mass_ref,
    emb_all, centers, scores, plan, rpot, colbuf, rowbuf, massbuf, sqbuf, sums, rsbuf, tot, pairbuf,
    own_sem, cent_sem, emb_ss, emb_rs, fwd_ss, col_ss, col_rs, row_ss, row_rs,
    mass_ss, mass_rs, sq_ss, sq_rs, sum_ss, sum_rs, pair_ss, pair_rs,
):
    nz = nd // 2
    nb = 2 * nc
    rows, features = emb_ref.shape
    half = cent_ref.shape[0] // 2
    own_f = features // nd
    log_docs = math.log2(rows * nd * nc)
    log_clusters = math.log2(2 * half * nc)
    d = lax.axis_index("doc")
    c = lax.axis_index("clu")
    core = lax.rem(d, 2)
    z = lax.div(d, 2)
    partner = d + 1 - 2 * core
    me = core * nc + c

    def block_peer(k):
        peer = lax.rem(me + k, nb)
        return peer, (2 * z + lax.div(peer, nc), lax.rem(peer, nc))

    def z_peer(k):
        peer = lax.rem(z + k, nz)
        return peer, (2 * peer + core, c)

    def doc_peer(k):
        peer = lax.rem(d + k, nd)
        return peer, (peer, c)

    def remote(src, dst, ss, rs, device):
        return pltpu.make_async_remote_copy(
            src_ref=src, dst_ref=dst, send_sem=ss, recv_sem=rs,
            device_id=device, device_id_type=MESH,
        )

    sends = []

    def send(*args):
        copy = remote(*args)
        copy.start()
        sends.append(copy)

    own_copy = pltpu.make_async_copy(emb_ref, emb_all.at[me], own_sem)
    own_copy.start()
    cent_copy = pltpu.make_async_copy(
        cent_ref.at[pl.ds(pl.multiple_of(core * half, half), half), :], centers, cent_sem
    )
    cent_copy.start()
    barrier = pltpu.get_barrier_semaphore()
    for k in range(1, nb):
        pl.semaphore_signal(barrier, inc=1, device_id=block_peer(k)[1], device_id_type=MESH)
    for k in range(1, nd):
        pl.semaphore_signal(barrier, inc=1, device_id=doc_peer(k)[1], device_id_type=MESH)

    def col_update(state, t):
        high, total = state
        t = t.reshape(rows // 8, 8, half)
        new = jnp.maximum(high, jnp.max(t, axis=0))
        total = total * jnp.exp2(high - new) + jnp.sum(jnp.exp2(t - new[None]), axis=0)
        return new, total

    state = (jnp.full((8, half), -jnp.inf, F32), jnp.zeros((8, half), F32))

    def first_block(state, slot):
        s = lax.dot_general(
            emb_all[slot], centers[...], (((1,), (1,)), ((), ())), preferred_element_type=F32
        ) * (LOG2E / SMOOTHING)
        scores[slot] = s
        return col_update(state, s)

    def arrive(slot):
        remote(
            emb_all.at[slot], emb_all.at[slot], emb_ss.at[0], emb_rs.at[slot], (partner, c)
        ).wait_recv()

    def clu_peer(k):
        if nc & (nc - 1):
            return lax.rem(c + k, nc)
        bits = [1 << i for i in range(nc.bit_length() - 1)]
        return sum(lax.rem(lax.div(c, b) + k // b, 2) * b for b in bits)

    own_copy.wait()
    cent_copy.wait()
    state = first_block(state, me)
    pl.semaphore_wait(barrier, nb - 1 + nd - 1)

    own = emb_all.at[me]
    for k in reversed(range(1, nc)):
        send(own, own, emb_ss.at[k], emb_rs.at[me], (d, clu_peer(k)))
    send(own, own, emb_ss.at[0], emb_rs.at[me], (partner, c))
    other = 1 - core
    for k in range(1, nc):
        slot = core * nc + clu_peer(k)
        arrive(slot)
        send(emb_all.at[slot], emb_all.at[slot], fwd_ss.at[k], emb_rs.at[slot], (partner, c))
        state = first_block(state, slot)
    for k in range(nc):
        slot = other * nc + clu_peer(k)
        arrive(slot)
        state = first_block(state, slot)

    diagonal = lax.broadcasted_iota(jnp.int32, (rows, rows), 0) == lax.broadcasted_iota(
        jnp.int32, (rows, rows), 1
    )

    def to_lanes(x):
        return jnp.sum(jnp.where(diagonal, x, 0.0), axis=0, keepdims=True)

    def to_sublanes(x):
        return jnp.sum(jnp.where(diagonal, x, 0.0), axis=1, keepdims=True)

    def column_potential(it, state):
        high, total = state
        top = jnp.max(high, axis=0, keepdims=True)
        total = jnp.sum(total * jnp.exp2(high - top), axis=0, keepdims=True)
        colbuf[it, z] = top + jnp.log2(total)
        mine = colbuf.at[it, z]
        for k in range(1, nz):
            send(mine, mine, col_ss.at[it, k], col_rs.at[it, z], z_peer(k)[1])
        for k in range(1, nz):
            peer, device = z_peer(k)
            theirs = colbuf.at[it, peer]
            remote(theirs, theirs, col_ss.at[it, k], col_rs.at[it, peer], device).wait_recv()
        logs = [colbuf[it, s] for s in range(nz)]
        top = functools.reduce(jnp.maximum, logs)
        return -log_clusters - (top + jnp.log2(sum(jnp.exp2(x - top) for x in logs)))

    part = nb // 2

    def row_send(it, h, col_pot):
        def block(b, carry):
            t = scores[h * part + b] + col_pot
            high = jnp.max(t, axis=1, keepdims=True)
            total = jnp.sum(jnp.exp2(t - high), axis=1, keepdims=True)
            rowbuf[it, h, me, pl.ds(b, 1), :] = to_lanes(high + jnp.log2(total))
            return carry

        lax.fori_loop(0, part, block, 0, unroll=4)
        mine = rowbuf.at[it, h, me]
        for k in range(1, nb):
            send(mine, mine, row_ss.at[it, h, k], row_rs.at[it, h, me], block_peer(k)[1])

    def row_receive(it, h):
        for k in range(1, nb):
            peer, device = block_peer(k)
            theirs = rowbuf.at[it, h, peer]
            remote(
                theirs, theirs, row_ss.at[it, h, k], row_rs.at[it, h, peer], device
            ).wait_recv()
        logs = rowbuf[it, h]
        top = jnp.max(logs, axis=0)
        total = jnp.sum(jnp.exp2(logs - top[None]), axis=0)
        rpot[h] = -log_docs - (top + jnp.log2(total))

    for it in range(ITERS):
        if it > 0:
            state = (jnp.full((8, half), -jnp.inf, F32), jnp.zeros((8, half), F32))
            for h in range(2):
                def again(b, state):
                    t = scores[h * part + b] + to_sublanes(rpot[h, pl.ds(b, 1), :])
                    return col_update(state, t)

                row_receive(it - 1, h)
                state = lax.fori_loop(0, part, again, state, unroll=4)
        col_pot = column_potential(it, state)
        for h in range(2):
            row_send(it, h, col_pot)

    mass = jnp.zeros((8, half), F32)
    for h in range(2):
        def plan_block(b, mass):
            t = scores[h * part + b] + to_sublanes(rpot[h, pl.ds(b, 1), :]) + col_pot + log_docs
            p = jnp.exp2(t)
            plan[h, pl.ds(pl.multiple_of(b * rows, rows), rows), :] = p.astype(jnp.bfloat16)
            return mass + jnp.sum(p.reshape(rows // 8, 8, half), axis=0)

        row_receive(ITERS - 1, h)
        mass = lax.fori_loop(0, part, plan_block, mass, unroll=4)
        product = lax.dot_general(
            emb_all[h * part:(h + 1) * part].reshape(part * rows, features), plan[h],
            (((0,), (0,)), ((), ())), preferred_element_type=F32,
        )
        sums[...] = product if h == 0 else sums[...] + product
    massbuf[d] = jnp.sum(mass, axis=0, keepdims=True)
    far = sorted(range(1, nz), key=lambda k: -min(k, nz - k))

    def share(peer):
        return sums.at[pl.ds(pl.multiple_of(peer * 2 * own_f, 2 * own_f), 2 * own_f), :]

    for k in far:
        peer, device = z_peer(k)
        send(share(peer), rsbuf.at[z], sum_ss.at[k], sum_rs.at[z], device)
    for k in range(1, nd):
        send(massbuf.at[d], massbuf.at[d], mass_ss.at[k], mass_rs.at[d], doc_peer(k)[1])
    total = share(z)[...]
    for k in reversed(far):
        peer, device = z_peer(k)
        remote(share(z), rsbuf.at[peer], sum_ss.at[k], sum_rs.at[peer], device).wait_recv()
        total = total + rsbuf[peer]
    tot[...] = total
    sqbuf[d] = jnp.sum(total * total, axis=0, keepdims=True)

    def features_of(which):
        return tot.at[pl.ds(pl.multiple_of(which * own_f, own_f), own_f), :]

    for k in range(1, nd):
        send(sqbuf.at[d], sqbuf.at[d], sq_ss.at[k], sq_rs.at[d], doc_peer(k)[1])
    send(features_of(other), pairbuf, pair_ss, pair_rs, (partner, c))
    for k in range(1, nd):
        peer, device = doc_peer(k)
        theirs = massbuf.at[peer]
        remote(theirs, theirs, mass_ss.at[k], mass_rs.at[peer], device).wait_recv()
        theirs = sqbuf.at[peer]
        remote(theirs, theirs, sq_ss.at[k], sq_rs.at[peer], device).wait_recv()
    remote(features_of(core), pairbuf, pair_ss, pair_rs, (partner, c)).wait_recv()

    def finish(which, block):
        columns = pl.ds(pl.multiple_of(which * half, half), half)
        squares = sum(sqbuf[2 * s + which] for s in range(nz))
        out_ref[:, columns] = block * lax.rsqrt(squares / features + 1e-06)
        mass_ref[:, columns] = sum(massbuf[2 * s + which] for s in range(nz)) * (
            2 * half * nc / (rows * nd * nc)
        )

    finish(core, features_of(core)[...])
    finish(other, pairbuf[...])
    for copy in sends:
        copy.wait_send()


def scattered(nd, nc, embeddings, centroids):
    rows, features = embeddings.shape
    own_cols = centroids.shape[0]
    half, nz, nb = own_cols // 2, nd // 2, 2 * nc
    own_f = features // nd
    dma = pltpu.SemaphoreType.DMA
    out, mass = pl.pallas_call(
        functools.partial(scattered_kernel, nd, nc),
        out_shape=(
            jax.ShapeDtypeStruct((own_f, own_cols), F32),
            jax.ShapeDtypeStruct((1, own_cols), F32),
        ),
        in_specs=[pl.BlockSpec(memory_space=pltpu.HBM)] * 2,
        out_specs=(pl.BlockSpec(memory_space=pltpu.VMEM),) * 2,
        scratch_shapes=[
            pltpu.VMEM((nb, rows, features), jnp.bfloat16),
            pltpu.VMEM((half, features), jnp.bfloat16),
            pltpu.VMEM((nb, rows, half), F32),
            pltpu.VMEM((2, nc * rows, half), jnp.bfloat16),
            pltpu.VMEM((2, nc, rows), F32),
            pltpu.VMEM((ITERS, nz, 1, half), F32),
            pltpu.VMEM((ITERS, 2, nb, nc, rows), F32),
            pltpu.VMEM((nd, 1, half), F32),
            pltpu.VMEM((nd, 1, half), F32),
            pltpu.VMEM((features, half), F32),
            pltpu.VMEM((nz, 2 * own_f, half), F32),
            pltpu.VMEM((2 * own_f, half), F32),
            pltpu.VMEM((own_f, half), F32),
            dma, dma, dma((nc,)), dma((nb,)), dma((nc,)),
            dma((ITERS, nz)), dma((ITERS, nz)), dma((ITERS, 2, nb)), dma((ITERS, 2, nb)),
            dma((nd,)), dma((nd,)), dma((nd,)), dma((nd,)),
            dma((nz,)), dma((nz,)), dma, dma,
        ],
        compiler_params=pltpu.CompilerParams(
            collective_id=0, has_side_effects=True
        ),
    )(embeddings, centroids)
    return out, mass.reshape(own_cols)


def replicated_kernel(
    nd, nc,
    emb_ref, cent_ref, out_ref, mass_ref,
    emb_all, centers, scores, plan, high, total, wide, pots, share, colbuf, rowbuf, sums, finished, pairbuf, pairmass,
    own_sem, cent_sem, own_ss, emb_rs, core_ss, plane_ss, col_ss, col_rs, row_ss, row_rs,
    pot_ss, pot_rs, pair_ss, pair_rs,
):
    nz = nd // 2
    nb = 2 * nc
    rows, features = emb_ref.shape
    half = cent_ref.shape[0] // 2
    own_f = features // nd
    docs, clusters = rows * nd * nc, 2 * half * nc
    log_docs, log_clusters = math.log2(docs), math.log2(clusters)
    d = lax.axis_index("doc")
    c = lax.axis_index("clu")
    core = lax.rem(d, 2)
    other = 1 - core
    z = lax.div(d, 2)
    partner = d + other - core
    me = core * nc + c
    step = min(half, 64)
    tiles = step // 8

    def paired(i, k, n):
        if n & (n - 1):
            return lax.rem(i + k, n)
        bits = [1 << b for b in range(n.bit_length() - 1)]
        return sum(lax.rem(lax.div(i, b) + k // b, 2) * b for b in bits)

    block_peers = [paired(me, k, nb) for k in range(nb)]
    block_peers = [(p, (2 * z + lax.div(p, nc), lax.rem(p, nc))) for p in block_peers]
    clu_peers = [paired(c, k, nc) for k in range(nc)]
    z_peers = [paired(z, k, nz) for k in range(nz)]

    pair_peers = [paired(lax.div(c, 2), k, nc // 2) for k in range(nc // 2)]

    outward = sorted(range(1, nb), key=lambda k: -(2 * (k % nc).bit_count() + k // nc))

    def block_peer(k):
        return block_peers[k]

    def clu_peer(k):
        return clu_peers[k]

    def z_peer(k):
        return z_peers[k]

    def slot_of(plane, side, cluster):
        return plane * nb + side * nc + cluster

    def remote(src, dst, ss, rs, device):
        return pltpu.make_async_remote_copy(
            src_ref=src, dst_ref=dst, send_sem=ss, recv_sem=rs,
            device_id=device, device_id_type=MESH,
        )

    sends = []

    def send(*args):
        copy = remote(*args)
        copy.start()
        sends.append(copy)

    mine = slot_of(z, core, c)
    own = emb_all.at[mine]
    own_copy = pltpu.make_async_copy(emb_ref, own, own_sem)
    cent_copy = pltpu.make_async_copy(
        cent_ref.at[pl.ds(pl.multiple_of(core * half, half), half), :], centers, cent_sem
    )
    barrier = pltpu.get_barrier_semaphore()
    for k in range(1, nb):
        pl.semaphore_signal(barrier, inc=1, device_id=block_peer(k)[1], device_id_type=MESH)
    for k in range(1, nz):
        pl.semaphore_signal(
            barrier, inc=1, device_id=(2 * z_peer(k) + core, c), device_id_type=MESH
        )

    own_copy.start()
    cent_copy.start()

    def score(slot):
        return lax.dot_general(
            centers[...], emb_all[slot], (((1,), (1,)), ((), ())), preferred_element_type=F32
        ) * (LOG2E / SMOOTHING)

    def arrive(slot):
        remote(
            emb_all.at[slot], emb_all.at[slot], own_ss.at[0], emb_rs.at[slot], (partner, c)
        ).wait_recv()

    def to_partner(slot, k):
        send(emb_all.at[slot], emb_all.at[slot], core_ss.at[k], emb_rs.at[slot], (partner, c))

    near = [j for j in range(1, nc) if not j & (j - 1)]
    far = [j for j in range(1, nc) if j & (j - 1)]

    def to_plane(slot, k, which):
        for j in which:
            send(
                emb_all.at[slot], emb_all.at[slot], plane_ss.at[k, j], emb_rs.at[slot],
                (d, clu_peer(j)),
            )

    def pair_scores(k, side, pair):
        slot = slot_of(z_peer(k), side, 2 * pair)
        both = lax.dot_general(
            centers[...], emb_all[pl.ds(slot, 2)].reshape(2 * rows, features),
            (((1,), (1,)), ((), ())), preferred_element_type=F32,
        ) * (LOG2E / SMOOTHING)
        for n in range(2):
            block = both[:, n * rows:(n + 1) * rows]
            scores[slot + n] = block + wide[...] if k else block
        return slot, slot + 1

    def plane_scores(k, first, count):
        for j in range(2 * first, 2 * (first + count)):
            arrive(slot_of(z_peer(k), other, clu_peer(j)))
        for j in range(first, first + count):
            for side in (core, other):
                pair_scores(k, side, pair_peers[j])

    def piece(g):
        return pl.ds(pl.multiple_of(g * step, step), step)

    def column_update(slots, first):
        def body(g, carry):
            at = piece(g)
            ts = [scores[s, at, :] for s in slots]
            old = None if first else high[at, :]
            new = functools.reduce(jnp.maximum, ts if first else ts + [old])
            part = sum(jnp.exp2(t - new) for t in ts)
            total[at, :] = part if first else part + total[at, :] * jnp.exp2(old - new)
            high[at, :] = new
            return carry

        lax.fori_loop(0, half // step, body, 0, unroll=8)

    own_copy.wait()
    pl.semaphore_wait(barrier, nb - 1 + nz - 1)

    to_plane(mine, 0, far + near)
    to_partner(mine, 0)
    for k in range(1, nz):
        send(own, own, own_ss.at[k], emb_rs.at[mine], (2 * z_peer(k) + core, c))
    cent_copy.wait()
    scores[mine] = score(mine)
    column_update([mine], True)
    slot = slot_of(z, core, clu_peer(1))
    arrive(slot)
    to_partner(slot, 1)
    scores[slot] = score(slot)
    column_update([slot], False)
    for j in range(1, nc // 2):
        for k in (2 * j, 2 * j + 1):
            slot = slot_of(z, core, clu_peer(k))
            arrive(slot)
            to_partner(slot, k)
        column_update(pair_scores(0, core, pair_peers[j]), False)

    def from_plane(k):
        slot = slot_of(z_peer(k), core, c)
        arrive(slot)
        to_plane(slot, k, near)
        to_partner(slot, k * nc)

    def across(k, which):
        for j in which:
            slot = slot_of(z_peer(k), core, clu_peer(j))
            arrive(slot)
            to_partner(slot, k * nc + j)

    if nz > 1:
        from_plane(1)
    for j in range(nc // 2):
        for k in (2 * j, 2 * j + 1):
            arrive(slot_of(z, other, clu_peer(k)))
        column_update(pair_scores(0, other, pair_peers[j]), False)

    def spread(x):
        wide[...] = jnp.transpose(jnp.broadcast_to(x, (rows, half)))

    def column_send(it, x):
        colbuf[it, z] = x
        ref = colbuf.at[it, z]
        for k in reversed(range(1, nz)):
            send(ref, ref, col_ss.at[it, k], col_rs.at[it, z], (2 * z_peer(k) + core, c))

    def column_receive(it):
        for k in range(1, nz):
            theirs = colbuf.at[it, z_peer(k)]
            remote(
                theirs, theirs, col_ss.at[it, k], col_rs.at[it, z_peer(k)], (partner, c)
            ).wait_recv()
        return [colbuf[it, s] for s in range(nz)]

    def row_send(it, k):
        ref = rowbuf.at[it, k, me]
        for j in outward:
            send(ref, ref, row_ss.at[it, k, j], row_rs.at[it, k, me], block_peer(j)[1])

    def row_receive(it, k):
        for j in range(1, nb):
            peer, device = block_peer(j)
            theirs = rowbuf.at[it, k, peer]
            remote(
                theirs, theirs, row_ss.at[it, k, j], row_rs.at[it, k, peer], device
            ).wait_recv()
        return [rowbuf[it, k, s] for s in range(nb)]

    def folded(x, op):
        return functools.reduce(op, [x[8 * i:8 * i + 8] for i in range(tiles)])

    def rows_of(parts, op):
        return jnp.concatenate([op(x, axis=0, keepdims=True) for x in parts], axis=0)

    def row_first():
        def shift(g, tops):
            at = piece(g)
            w = wide[at, :]
            new = []
            for b in range(nb):
                t = scores[z * nb + b, at, :] + w
                scores[z * nb + b, at, :] = t
                new.append(jnp.maximum(tops[b], folded(t, jnp.maximum)))
            return tuple(new)

        def add(g, accs):
            at = piece(g)
            return tuple(
                accs[b] + folded(jnp.exp2(scores[z * nb + b, at, :] - top[b:b + 1]), jnp.add)
                for b in range(nb)
            )

        count = half // step
        low = (jnp.full((8, rows), -jnp.inf, F32),) * nb
        top = rows_of(lax.fori_loop(0, count, shift, low, unroll=count), jnp.max)
        zero = (jnp.zeros((8, rows), F32),) * nb
        total = rows_of(lax.fori_loop(0, count, add, zero, unroll=count), jnp.sum)
        rowbuf[0, 0, me] = top + jnp.log2(total)

    def row_next(it, k, last):
        plane = z_peer(k)

        def body(g, accs):
            at = piece(g)
            w = wide[at, :]
            new = []
            for b in range(nb):
                t = scores[plane * nb + b, at, :] + w
                e = jnp.exp2(t + r[b:b + 1])
                scores[plane * nb + b, at, :] = e if last else t
                new.append(accs[b] + folded(e, jnp.add))
            return tuple(new)

        r = pots[plane]
        zero = (jnp.zeros((8, rows), F32),) * nb
        found = lax.fori_loop(0, half // step, body, zero, unroll=half // step)
        rowbuf[it, k, me] = rows_of(found, jnp.sum)

    def column_next(g, carry):
        at = piece(g)
        acc = jnp.zeros((step, rows), F32)
        for b in range(nb):
            acc = acc + jnp.exp2(scores[z * nb + b, at, :] + pots[z, pl.ds(b, 1), :])
        total[at, :] = acc
        return carry

    tops = jnp.transpose(high[...])
    top = jnp.max(tops, axis=0, keepdims=True)
    column_send(
        0,
        top + jnp.log2(
            jnp.sum(jnp.transpose(total[...]) * jnp.exp2(tops - top), axis=0, keepdims=True)
        ),
    )
    for k in range(1, nz):
        for j in far:
            slot = slot_of(z, core, clu_peer(j))
            send(
                emb_all.at[slot], emb_all.at[slot], plane_ss.at[k, j], emb_rs.at[slot],
                (2 * z_peer(k) + core, c),
            )
    for k in range(2, nz):
        from_plane(k)
    logs = column_receive(0)
    top = functools.reduce(jnp.maximum, logs)
    spread(-log_clusters - (top + jnp.log2(sum(jnp.exp2(x - top) for x in logs))))
    row_first()
    row_send(0, 0)
    for k in range(1, nz):
        across(k, near + far if k == 1 else near)
    for k in range(1, nz):
        plane_scores(k, 0, nc // 2 if k == 1 else 1)
    logs = row_receive(0, 0)
    top = functools.reduce(jnp.maximum, logs)
    pots[z] = -log_docs - (top + jnp.log2(sum(jnp.exp2(x - top) for x in logs)))

    for it in range(1, ITERS):
        last = it == ITERS - 1
        if last:
            gone = list(sends)
            sends.clear()
        lax.fori_loop(0, half // step, column_next, 0, unroll=8)
        column_send(it, jnp.sum(jnp.transpose(total[...]), axis=0, keepdims=True))
        if last:
            ref = pots.at[z]
            for k in range(1, nz):
                send(ref, ref, pot_ss.at[k], pot_rs.at[z], (2 * z_peer(k) + core, c))
        if it == 1:
            for k in range(2, nz):
                across(k, far)
            for k in range(2, nz):
                plane_scores(k, 1, nc // 2 - 1)
        change = -log_clusters - jnp.log2(sum(column_receive(it)))
        spread(change)
        for k in range(nz if last else 1):
            if k:
                theirs = pots.at[z_peer(k)]
                remote(
                    theirs, theirs, pot_ss.at[k], pot_rs.at[z_peer(k)], (partner, c)
                ).wait_recv()
            row_next(it, k, last)
            row_send(it, k)
        if not last:
            pots[z] = pots[z] - log_docs - jnp.log2(sum(row_receive(it, 0)))

    for copy in gone:
        copy.wait_send()
    wider = min(half, 256)

    def plane_plan(k):
        plane = z_peer(k)
        share[k] = 1.0 / sum(row_receive(ITERS - 1, k))
        block = emb_all[pl.ds(plane * nb, nb)].reshape(nb * rows, features)
        for g in range(half // wider):
            for i in range(wider // step):
                at = pl.ds(g * wider + i * step, step)
                acc = jnp.zeros((step, rows), F32)
                for b in range(nb):
                    p = scores[plane * nb + b, at, :] * share[k, pl.ds(b, 1), :]
                    plan[at, b * rows:(b + 1) * rows] = p.astype(jnp.bfloat16)
                    acc = acc + p
                total[at, :] = acc + total[at, :] if k else acc
            at = pl.ds(g * wider, wider)
            product = lax.dot_general(
                plan[at, :], block, (((1,), (0,)), ((), ())), preferred_element_type=F32
            )
            sums[at, :] = sums[at, :] + product if k else product

    for k in range(nz):
        plane_plan(k)

    everything = jnp.transpose(sums[...])
    scale = lax.rsqrt(jnp.sum(everything * everything, axis=0, keepdims=True) / features + 1e-06)
    finished[...] = everything * scale
    pairmass[0] = jnp.sum(jnp.transpose(total[...]), axis=0, keepdims=True) * (clusters / docs)

    def features_of(which):
        return finished.at[pl.ds(pl.multiple_of((2 * z + which) * own_f, own_f), own_f), :]

    send(features_of(other), pairbuf, pair_ss.at[0], pair_rs.at[0], (partner, c))
    send(pairmass.at[0], pairmass.at[1], pair_ss.at[1], pair_rs.at[1], (partner, c))
    columns = pl.ds(pl.multiple_of(core * half, half), half)
    out_ref[:, columns] = features_of(core)[...]
    mass_ref[:, columns] = pairmass[0]
    for copy in sends:
        copy.wait_send()
    columns = pl.ds(pl.multiple_of(other * half, half), half)
    remote(pairbuf, pairbuf, pair_ss.at[0], pair_rs.at[0], (partner, c)).wait_recv()
    out_ref[:, columns] = pairbuf[...]
    remote(
        pairmass.at[1], pairmass.at[1], pair_ss.at[1], pair_rs.at[1], (partner, c)
    ).wait_recv()
    mass_ref[:, columns] = pairmass[1]


def store_kernel(part_ref, mass_ref, out_ref, total_ref):
    out_ref[...] = part_ref[...]
    total_ref[...] = mass_ref[...].reshape(total_ref.shape)


def replicated(nd, nc, embeddings, centroids):
    rows, features = embeddings.shape
    own_cols = centroids.shape[0]
    half, nz, nb = own_cols // 2, nd // 2, 2 * nc
    own_f = features // nd
    dma = pltpu.SemaphoreType.DMA
    out, mass = pl.pallas_call(
        functools.partial(replicated_kernel, nd, nc),
        out_shape=(
            jax.ShapeDtypeStruct((own_f, own_cols), F32),
            jax.ShapeDtypeStruct((1, own_cols), F32),
        ),
        in_specs=[pl.BlockSpec(memory_space=pltpu.HBM)] * 2,
        out_specs=(pl.BlockSpec(memory_space=pltpu.VMEM),) * 2,
        scratch_shapes=[
            pltpu.VMEM((nz * nb, rows, features), jnp.bfloat16),
            pltpu.VMEM((half, features), jnp.bfloat16),
            pltpu.VMEM((nz * nb, half, rows), F32),
            pltpu.VMEM((half, nb * rows), jnp.bfloat16),
            pltpu.VMEM((half, rows), F32),
            pltpu.VMEM((half, rows), F32),
            pltpu.VMEM((half, rows), F32),
            pltpu.VMEM((nz, nb, rows), F32),
            pltpu.VMEM((nz, nb, rows), F32),
            pltpu.VMEM((ITERS, nz, 1, half), F32),
            pltpu.VMEM((ITERS, nz, nb, nb, rows), F32),
            pltpu.VMEM((half, features), F32),
            pltpu.VMEM((features, half), F32),
            pltpu.VMEM((own_f, half), F32),
            pltpu.VMEM((2, 1, half), F32),
            dma, dma, dma((nz,)), dma((nz * nb,)), dma((nz * nc,)), dma((nz, nc)),
            dma((ITERS, nz)), dma((ITERS, nz)), dma((ITERS, nz, nb)), dma((ITERS, nz, nb)),
            dma((nz,)), dma((nz,)), dma((2,)), dma((2,)),
        ],
        compiler_params=pltpu.CompilerParams(
            collective_id=0, has_side_effects=True, vmem_limit_bytes=VMEM_BYTES
        ),
    )(*(pltpu.with_memory_space_constraint(a, pltpu.HBM) for a in (embeddings, centroids)))
    return pl.pallas_call(
        store_kernel,
        out_shape=(
            jax.ShapeDtypeStruct((own_f, own_cols), F32),
            jax.ShapeDtypeStruct((own_cols,), F32),
        ),
        in_specs=[pl.BlockSpec(memory_space=pltpu.VMEM)] * 2,
        out_specs=(pl.BlockSpec(memory_space=pltpu.VMEM),) * 2,
        compiler_params=pltpu.CompilerParams(vmem_limit_bytes=4 << 20),
    )(out, mass)


VMEM_BYTES = 48 << 20


def local(nd, nc, embeddings, centroids):
    rows, features = embeddings.shape
    docs = rows * nd * nc
    half = centroids.shape[0] // 2
    held = docs * (2 * features + 4 * half)
    fits = 2 * held <= VMEM_BYTES and nd > 2 and nc > 1 and not nc & (nc - 1)
    form = replicated if fits else scattered
    return form(nd, nc, embeddings, centroids)


def solution(mesh):
    placed = (P(("doc", "clu"), None), P("clu", None))
    body = functools.partial(local, mesh.shape["doc"], mesh.shape["clu"])
    return jax.shard_map(
        body, mesh=mesh, in_specs=placed, out_specs=(P("doc", "clu"), P("clu")), check_vma=False
    )
```

```python
import functools
import math

import jax
import jax.numpy as jnp
from jax import lax
from jax.experimental import pallas as pl
from jax.experimental.pallas import tpu as pltpu
from jax.sharding import PartitionSpec as P

ITERS = 2
SMOOTHING = 0.05
LOG2E = math.log2(math.e)
MESH = pl.DeviceIdType.MESH
F32 = jnp.float32


def scattered_kernel(
    nd, nc,
    emb_ref, cent_ref, out_ref, mass_ref,
    emb_all, centers, scores, plan, rpot, colbuf, rowbuf, massbuf, sqbuf, sums, rsbuf, tot, pairbuf,
    own_sem, cent_sem, emb_ss, emb_rs, fwd_ss, col_ss, col_rs, row_ss, row_rs,
    mass_ss, mass_rs, sq_ss, sq_rs, sum_ss, sum_rs, pair_ss, pair_rs,
):
    nz = nd // 2
    nb = 2 * nc
    rows, features = emb_ref.shape
    half = cent_ref.shape[0] // 2
    own_f = features // nd
    log_docs = math.log2(rows * nd * nc)
    log_clusters = math.log2(2 * half * nc)
    d = lax.axis_index("doc")
    c = lax.axis_index("clu")
    core = lax.rem(d, 2)
    z = lax.div(d, 2)
    partner = d + 1 - 2 * core
    me = core * nc + c

    def block_peer(k):
        peer = lax.rem(me + k, nb)
        return peer, (2 * z + lax.div(peer, nc), lax.rem(peer, nc))

    def z_peer(k):
        peer = lax.rem(z + k, nz)
        return peer, (2 * peer + core, c)

    def doc_peer(k):
        peer = lax.rem(d + k, nd)
        return peer, (peer, c)

    def remote(src, dst, ss, rs, device):
        return pltpu.make_async_remote_copy(
            src_ref=src, dst_ref=dst, send_sem=ss, recv_sem=rs,
            device_id=device, device_id_type=MESH,
        )

    sends = []

    def send(*args):
        copy = remote(*args)
        copy.start()
        sends.append(copy)

    own_copy = pltpu.make_async_copy(emb_ref, emb_all.at[me], own_sem)
    own_copy.start()
    cent_copy = pltpu.make_async_copy(
        cent_ref.at[pl.ds(pl.multiple_of(core * half, half), half), :], centers, cent_sem
    )
    cent_copy.start()
    barrier = pltpu.get_barrier_semaphore()
    for k in range(1, nb):
        pl.semaphore_signal(barrier, inc=1, device_id=block_peer(k)[1], device_id_type=MESH)
    for k in range(1, nd):
        pl.semaphore_signal(barrier, inc=1, device_id=doc_peer(k)[1], device_id_type=MESH)

    def col_update(state, t):
        high, total = state
        t = t.reshape(rows // 8, 8, half)
        new = jnp.maximum(high, jnp.max(t, axis=0))
        total = total * jnp.exp2(high - new) + jnp.sum(jnp.exp2(t - new[None]), axis=0)
        return new, total

    state = (jnp.full((8, half), -jnp.inf, F32), jnp.zeros((8, half), F32))

    def first_block(state, slot):
        s = lax.dot_general(
            emb_all[slot], centers[...], (((1,), (1,)), ((), ())), preferred_element_type=F32
        ) * (LOG2E / SMOOTHING)
        scores[slot] = s
        return col_update(state, s)

    def arrive(slot):
        remote(
            emb_all.at[slot], emb_all.at[slot], emb_ss.at[0], emb_rs.at[slot], (partner, c)
        ).wait_recv()

    def clu_peer(k):
        if nc & (nc - 1):
            return lax.rem(c + k, nc)
        bits = [1 << i for i in range(nc.bit_length() - 1)]
        return sum(lax.rem(lax.div(c, b) + k // b, 2) * b for b in bits)

    own_copy.wait()
    cent_copy.wait()
    state = first_block(state, me)
    pl.semaphore_wait(barrier, nb - 1 + nd - 1)

    own = emb_all.at[me]
    for k in reversed(range(1, nc)):
        send(own, own, emb_ss.at[k], emb_rs.at[me], (d, clu_peer(k)))
    send(own, own, emb_ss.at[0], emb_rs.at[me], (partner, c))
    other = 1 - core
    for k in range(1, nc):
        slot = core * nc + clu_peer(k)
        arrive(slot)
        send(emb_all.at[slot], emb_all.at[slot], fwd_ss.at[k], emb_rs.at[slot], (partner, c))
        state = first_block(state, slot)
    for k in range(nc):
        slot = other * nc + clu_peer(k)
        arrive(slot)
        state = first_block(state, slot)

    diagonal = lax.broadcasted_iota(jnp.int32, (rows, rows), 0) == lax.broadcasted_iota(
        jnp.int32, (rows, rows), 1
    )

    def to_lanes(x):
        return jnp.sum(jnp.where(diagonal, x, 0.0), axis=0, keepdims=True)

    def to_sublanes(x):
        return jnp.sum(jnp.where(diagonal, x, 0.0), axis=1, keepdims=True)

    def column_potential(it, state):
        high, total = state
        top = jnp.max(high, axis=0, keepdims=True)
        total = jnp.sum(total * jnp.exp2(high - top), axis=0, keepdims=True)
        colbuf[it, z] = top + jnp.log2(total)
        mine = colbuf.at[it, z]
        for k in range(1, nz):
            send(mine, mine, col_ss.at[it, k], col_rs.at[it, z], z_peer(k)[1])
        for k in range(1, nz):
            peer, device = z_peer(k)
            theirs = colbuf.at[it, peer]
            remote(theirs, theirs, col_ss.at[it, k], col_rs.at[it, peer], device).wait_recv()
        logs = [colbuf[it, s] for s in range(nz)]
        top = functools.reduce(jnp.maximum, logs)
        return -log_clusters - (top + jnp.log2(sum(jnp.exp2(x - top) for x in logs)))

    part = nb // 2

    def row_send(it, h, col_pot):
        def block(b, carry):
            t = scores[h * part + b] + col_pot
            high = jnp.max(t, axis=1, keepdims=True)
            total = jnp.sum(jnp.exp2(t - high), axis=1, keepdims=True)
            rowbuf[it, h, me, pl.ds(b, 1), :] = to_lanes(high + jnp.log2(total))
            return carry

        lax.fori_loop(0, part, block, 0, unroll=4)
        mine = rowbuf.at[it, h, me]
        for k in range(1, nb):
            send(mine, mine, row_ss.at[it, h, k], row_rs.at[it, h, me], block_peer(k)[1])

    def row_receive(it, h):
        for k in range(1, nb):
            peer, device = block_peer(k)
            theirs = rowbuf.at[it, h, peer]
            remote(
                theirs, theirs, row_ss.at[it, h, k], row_rs.at[it, h, peer], device
            ).wait_recv()
        logs = rowbuf[it, h]
        top = jnp.max(logs, axis=0)
        total = jnp.sum(jnp.exp2(logs - top[None]), axis=0)
        rpot[h] = -log_docs - (top + jnp.log2(total))

    for it in range(ITERS):
        if it > 0:
            state = (jnp.full((8, half), -jnp.inf, F32), jnp.zeros((8, half), F32))
            for h in range(2):
                def again(b, state):
                    t = scores[h * part + b] + to_sublanes(rpot[h, pl.ds(b, 1), :])
                    return col_update(state, t)

                row_receive(it - 1, h)
                state = lax.fori_loop(0, part, again, state, unroll=4)
        col_pot = column_potential(it, state)
        for h in range(2):
            row_send(it, h, col_pot)

    mass = jnp.zeros((8, half), F32)
    for h in range(2):
        def plan_block(b, mass):
            t = scores[h * part + b] + to_sublanes(rpot[h, pl.ds(b, 1), :]) + col_pot + log_docs
            p = jnp.exp2(t)
            plan[h, pl.ds(pl.multiple_of(b * rows, rows), rows), :] = p.astype(jnp.bfloat16)
            return mass + jnp.sum(p.reshape(rows // 8, 8, half), axis=0)

        row_receive(ITERS - 1, h)
        mass = lax.fori_loop(0, part, plan_block, mass, unroll=4)
        product = lax.dot_general(
            emb_all[h * part:(h + 1) * part].reshape(part * rows, features), plan[h],
            (((0,), (0,)), ((), ())), preferred_element_type=F32,
        )
        sums[...] = product if h == 0 else sums[...] + product
    massbuf[d] = jnp.sum(mass, axis=0, keepdims=True)
    far = sorted(range(1, nz), key=lambda k: -min(k, nz - k))

    def share(peer):
        return sums.at[pl.ds(pl.multiple_of(peer * 2 * own_f, 2 * own_f), 2 * own_f), :]

    for k in far:
        peer, device = z_peer(k)
        send(share(peer), rsbuf.at[z], sum_ss.at[k], sum_rs.at[z], device)
    for k in range(1, nd):
        send(massbuf.at[d], massbuf.at[d], mass_ss.at[k], mass_rs.at[d], doc_peer(k)[1])
    total = share(z)[...]
    for k in reversed(far):
        peer, device = z_peer(k)
        remote(share(z), rsbuf.at[peer], sum_ss.at[k], sum_rs.at[peer], device).wait_recv()
        total = total + rsbuf[peer]
    tot[...] = total
    sqbuf[d] = jnp.sum(total * total, axis=0, keepdims=True)

    def features_of(which):
        return tot.at[pl.ds(pl.multiple_of(which * own_f, own_f), own_f), :]

    for k in range(1, nd):
        send(sqbuf.at[d], sqbuf.at[d], sq_ss.at[k], sq_rs.at[d], doc_peer(k)[1])
    send(features_of(other), pairbuf, pair_ss, pair_rs, (partner, c))
    for k in range(1, nd):
        peer, device = doc_peer(k)
        theirs = massbuf.at[peer]
        remote(theirs, theirs, mass_ss.at[k], mass_rs.at[peer], device).wait_recv()
        theirs = sqbuf.at[peer]
        remote(theirs, theirs, sq_ss.at[k], sq_rs.at[peer], device).wait_recv()
    remote(features_of(core), pairbuf, pair_ss, pair_rs, (partner, c)).wait_recv()

    def finish(which, block):
        columns = pl.ds(pl.multiple_of(which * half, half), half)
        squares = sum(sqbuf[2 * s + which] for s in range(nz))
        out_ref[:, columns] = block * lax.rsqrt(squares / features + 1e-06)
        mass_ref[:, columns] = sum(massbuf[2 * s + which] for s in range(nz)) * (
            2 * half * nc / (rows * nd * nc)
        )

    finish(core, features_of(core)[...])
    finish(other, pairbuf[...])
    for copy in sends:
        copy.wait_send()


def scattered(nd, nc, embeddings, centroids):
    rows, features = embeddings.shape
    own_cols = centroids.shape[0]
    half, nz, nb = own_cols // 2, nd // 2, 2 * nc
    own_f = features // nd
    dma = pltpu.SemaphoreType.DMA
    out, mass = pl.pallas_call(
        functools.partial(scattered_kernel, nd, nc),
        out_shape=(
            jax.ShapeDtypeStruct((own_f, own_cols), F32),
            jax.ShapeDtypeStruct((1, own_cols), F32),
        ),
        in_specs=[pl.BlockSpec(memory_space=pltpu.HBM)] * 2,
        out_specs=(pl.BlockSpec(memory_space=pltpu.VMEM),) * 2,
        scratch_shapes=[
            pltpu.VMEM((nb, rows, features), jnp.bfloat16),
            pltpu.VMEM((half, features), jnp.bfloat16),
            pltpu.VMEM((nb, rows, half), F32),
            pltpu.VMEM((2, nc * rows, half), jnp.bfloat16),
            pltpu.VMEM((2, nc, rows), F32),
            pltpu.VMEM((ITERS, nz, 1, half), F32),
            pltpu.VMEM((ITERS, 2, nb, nc, rows), F32),
            pltpu.VMEM((nd, 1, half), F32),
            pltpu.VMEM((nd, 1, half), F32),
            pltpu.VMEM((features, half), F32),
            pltpu.VMEM((nz, 2 * own_f, half), F32),
            pltpu.VMEM((2 * own_f, half), F32),
            pltpu.VMEM((own_f, half), F32),
            dma, dma, dma((nc,)), dma((nb,)), dma((nc,)),
            dma((ITERS, nz)), dma((ITERS, nz)), dma((ITERS, 2, nb)), dma((ITERS, 2, nb)),
            dma((nd,)), dma((nd,)), dma((nd,)), dma((nd,)),
            dma((nz,)), dma((nz,)), dma, dma,
        ],
        compiler_params=pltpu.CompilerParams(
            collective_id=0, has_side_effects=True
        ),
    )(embeddings, centroids)
    return out, mass.reshape(own_cols)


def replicated_kernel(
    nd, nc,
    emb_ref, cent_ref, out_ref, mass_ref,
    emb_all, centers, scores, plan, high, total, wide, pots, share, colbuf, rowbuf, sums, finished, pairbuf, pairmass,
    own_sem, cent_sem, own_ss, emb_rs, core_ss, plane_ss, col_ss, col_rs, row_ss, row_rs,
    pot_ss, pot_rs, pair_ss, pair_rs,
):
    nz = nd // 2
    nb = 2 * nc
    rows, features = emb_ref.shape
    half = cent_ref.shape[0] // 2
    own_f = features // nd
    docs, clusters = rows * nd * nc, 2 * half * nc
    log_docs, log_clusters = math.log2(docs), math.log2(clusters)
    d = lax.axis_index("doc")
    c = lax.axis_index("clu")
    core = lax.rem(d, 2)
    other = 1 - core
    z = lax.div(d, 2)
    partner = d + other - core
    me = core * nc + c
    step = min(half, 64)
    tiles = step // 8

    def paired(i, k, n):
        if n & (n - 1):
            return lax.rem(i + k, n)
        bits = [1 << b for b in range(n.bit_length() - 1)]
        return sum(lax.rem(lax.div(i, b) + k // b, 2) * b for b in bits)

    block_peers = [paired(me, k, nb) for k in range(nb)]
    block_peers = [(p, (2 * z + lax.div(p, nc), lax.rem(p, nc))) for p in block_peers]
    clu_peers = [paired(c, k, nc) for k in range(nc)]
    z_peers = [paired(z, k, nz) for k in range(nz)]

    pair_peers = [paired(lax.div(c, 2), k, nc // 2) for k in range(nc // 2)]

    outward = sorted(range(1, nb), key=lambda k: -(2 * (k % nc).bit_count() + k // nc))

    def block_peer(k):
        return block_peers[k]

    def clu_peer(k):
        return clu_peers[k]

    def z_peer(k):
        return z_peers[k]

    def slot_of(plane, side, cluster):
        return plane * nb + side * nc + cluster

    def remote(src, dst, ss, rs, device):
        return pltpu.make_async_remote_copy(
            src_ref=src, dst_ref=dst, send_sem=ss, recv_sem=rs,
            device_id=device, device_id_type=MESH,
        )

    sends = []

    def send(*args):
        copy = remote(*args)
        copy.start()
        sends.append(copy)

    mine = slot_of(z, core, c)
    own = emb_all.at[mine]
    own_copy = pltpu.make_async_copy(emb_ref, own, own_sem)
    cent_copy = pltpu.make_async_copy(
        cent_ref.at[pl.ds(pl.multiple_of(core * half, half), half), :], centers, cent_sem
    )
    barrier = pltpu.get_barrier_semaphore()
    for k in range(1, nb):
        pl.semaphore_signal(barrier, inc=1, device_id=block_peer(k)[1], device_id_type=MESH)
    for k in range(1, nz):
        pl.semaphore_signal(
            barrier, inc=1, device_id=(2 * z_peer(k) + core, c), device_id_type=MESH
        )

    own_copy.start()
    cent_copy.start()

    def score(slot):
        return lax.dot_general(
            centers[...], emb_all[slot], (((1,), (1,)), ((), ())), preferred_element_type=F32
        ) * (LOG2E / SMOOTHING)

    def arrive(slot):
        remote(
            emb_all.at[slot], emb_all.at[slot], own_ss.at[0], emb_rs.at[slot], (partner, c)
        ).wait_recv()

    def to_partner(slot, k):
        send(emb_all.at[slot], emb_all.at[slot], core_ss.at[k], emb_rs.at[slot], (partner, c))

    near = [j for j in range(1, nc) if not j & (j - 1)]
    far = [j for j in range(1, nc) if j & (j - 1)]

    def to_plane(slot, k, which):
        for j in which:
            send(
                emb_all.at[slot], emb_all.at[slot], plane_ss.at[k, j], emb_rs.at[slot],
                (d, clu_peer(j)),
            )

    def pair_scores(k, side, pair):
        slot = slot_of(z_peer(k), side, 2 * pair)
        both = lax.dot_general(
            centers[...], emb_all[pl.ds(slot, 2)].reshape(2 * rows, features),
            (((1,), (1,)), ((), ())), preferred_element_type=F32,
        ) * (LOG2E / SMOOTHING)
        for n in range(2):
            block = both[:, n * rows:(n + 1) * rows]
            scores[slot + n] = block + wide[...] if k else block
        return slot, slot + 1

    def plane_scores(k, first, count):
        for j in range(2 * first, 2 * (first + count)):
            arrive(slot_of(z_peer(k), other, clu_peer(j)))
        for j in range(first, first + count):
            for side in (core, other):
                pair_scores(k, side, pair_peers[j])

    def piece(g):
        if isinstance(g, int):
            return pl.ds(g * step, step)
        return pl.ds(pl.multiple_of(g * step, step), step)

    def column_update(slots, first):
        def body(g, carry):
            at = piece(g)
            ts = [scores[s, at, :] for s in slots]
            old = None if first else high[at, :]
            new = functools.reduce(jnp.maximum, ts if first else ts + [old])
            part = sum(jnp.exp2(t - new) for t in ts)
            total[at, :] = part if first else part + total[at, :] * jnp.exp2(old - new)
            high[at, :] = new
            return carry

        lax.fori_loop(0, half // step, body, 0, unroll=8)

    own_copy.wait()
    pl.semaphore_wait(barrier, nb - 1 + nz - 1)

    to_plane(mine, 0, far + near)
    to_partner(mine, 0)
    for k in range(1, nz):
        send(own, own, own_ss.at[k], emb_rs.at[mine], (2 * z_peer(k) + core, c))
    cent_copy.wait()
    scores[mine] = score(mine)
    column_update([mine], True)
    slot = slot_of(z, core, clu_peer(1))
    arrive(slot)
    to_partner(slot, 1)
    scores[slot] = score(slot)
    column_update([slot], False)
    for j in range(1, nc // 2):
        for k in (2 * j, 2 * j + 1):
            slot = slot_of(z, core, clu_peer(k))
            arrive(slot)
            to_partner(slot, k)
        column_update(pair_scores(0, core, pair_peers[j]), False)

    def from_plane(k):
        slot = slot_of(z_peer(k), core, c)
        arrive(slot)
        to_plane(slot, k, near)
        to_partner(slot, k * nc)

    def across(k, which):
        for j in which:
            slot = slot_of(z_peer(k), core, clu_peer(j))
            arrive(slot)
            to_partner(slot, k * nc + j)

    if nz > 1:
        from_plane(1)
    for j in range(nc // 2):
        for k in (2 * j, 2 * j + 1):
            arrive(slot_of(z, other, clu_peer(k)))
        column_update(pair_scores(0, other, pair_peers[j]), False)

    def spread(x):
        wide[...] = jnp.transpose(jnp.broadcast_to(x, (rows, half)))

    def column_send(it, x):
        colbuf[it, z] = x
        ref = colbuf.at[it, z]
        for k in reversed(range(1, nz)):
            send(ref, ref, col_ss.at[it, k], col_rs.at[it, z], (2 * z_peer(k) + core, c))

    def column_receive(it):
        for k in range(1, nz):
            theirs = colbuf.at[it, z_peer(k)]
            remote(
                theirs, theirs, col_ss.at[it, k], col_rs.at[it, z_peer(k)], (partner, c)
            ).wait_recv()
        return [colbuf[it, s] for s in range(nz)]

    def row_send(it, k):
        ref = rowbuf.at[it, k, me]
        for j in outward:
            send(ref, ref, row_ss.at[it, k, j], row_rs.at[it, k, me], block_peer(j)[1])

    def row_receive(it, k):
        for j in range(1, nb):
            peer, device = block_peer(j)
            theirs = rowbuf.at[it, k, peer]
            remote(
                theirs, theirs, row_ss.at[it, k, j], row_rs.at[it, k, peer], device
            ).wait_recv()
        return [rowbuf[it, k, s] for s in range(nb)]

    def folded(x, op):
        return functools.reduce(op, [x[8 * i:8 * i + 8] for i in range(tiles)])

    def rows_of(parts, op):
        return jnp.concatenate([op(x, axis=0, keepdims=True) for x in parts], axis=0)

    def row_first():
        def shift(g, tops):
            at = piece(g)
            w = wide[at, :]
            new = []
            for b in range(nb):
                t = scores[z * nb + b, at, :] + w
                scores[z * nb + b, at, :] = t
                new.append(jnp.maximum(tops[b], folded(t, jnp.maximum)))
            return tuple(new)

        def add(g, accs):
            at = piece(g)
            return tuple(
                accs[b] + folded(jnp.exp2(scores[z * nb + b, at, :] - top[b:b + 1]), jnp.add)
                for b in range(nb)
            )

        count = half // step
        low = (jnp.full((8, rows), -jnp.inf, F32),) * nb
        top = rows_of(lax.fori_loop(0, count, shift, low, unroll=count), jnp.max)
        zero = (jnp.zeros((8, rows), F32),) * nb
        total = rows_of(lax.fori_loop(0, count, add, zero, unroll=count), jnp.sum)
        rowbuf[0, 0, me] = top + jnp.log2(total)

    def row_next(it, k, last):
        plane = z_peer(k)

        def body(g, accs):
            at = piece(g)
            w = wide[at, :]
            new = []
            for b in range(nb):
                t = scores[plane * nb + b, at, :] + w
                e = jnp.exp2(t + r[b:b + 1])
                scores[plane * nb + b, at, :] = e if last else t
                new.append(accs[b] + folded(e, jnp.add))
            return tuple(new)

        r = pots[plane]
        zero = (jnp.zeros((8, rows), F32),) * nb
        found = lax.fori_loop(0, half // step, body, zero, unroll=half // step)
        rowbuf[it, k, me] = rows_of(found, jnp.sum)

    def column_next(g, carry):
        at = piece(g)
        acc = jnp.zeros((step, rows), F32)
        for b in range(nb):
            acc = acc + jnp.exp2(scores[z * nb + b, at, :] + pots[z, pl.ds(b, 1), :])
        total[at, :] = acc
        return carry

    tops = jnp.transpose(high[...])
    top = jnp.max(tops, axis=0, keepdims=True)
    column_send(
        0,
        top + jnp.log2(
            jnp.sum(jnp.transpose(total[...]) * jnp.exp2(tops - top), axis=0, keepdims=True)
        ),
    )
    for k in range(1, nz):
        for j in far:
            slot = slot_of(z, core, clu_peer(j))
            send(
                emb_all.at[slot], emb_all.at[slot], plane_ss.at[k, j], emb_rs.at[slot],
                (2 * z_peer(k) + core, c),
            )
    for k in range(2, nz):
        from_plane(k)
    logs = column_receive(0)
    top = functools.reduce(jnp.maximum, logs)
    spread(-log_clusters - (top + jnp.log2(sum(jnp.exp2(x - top) for x in logs))))
    row_first()
    row_send(0, 0)
    for k in range(1, nz):
        across(k, near + far if k == 1 else near)
    if nz > 1:
        plane_scores(1, 0, nc // 2)
    logs = row_receive(0, 0)
    top = functools.reduce(jnp.maximum, logs)
    pots[z] = -log_docs - (top + jnp.log2(sum(jnp.exp2(x - top) for x in logs)))

    for it in range(1, ITERS):
        last = it == ITERS - 1
        if last:
            gone = list(sends)
            sends.clear()
        for g in range(half // step):
            column_next(g, 0)
        column_send(it, jnp.sum(jnp.transpose(total[...]), axis=0, keepdims=True))
        if last:
            ref = pots.at[z]
            for k in range(1, nz):
                send(ref, ref, pot_ss.at[k], pot_rs.at[z], (2 * z_peer(k) + core, c))
        if it == 1:
            for k in range(2, nz):
                across(k, far)
            for k in range(2, nz):
                plane_scores(k, 0, nc // 2)
        change = -log_clusters - jnp.log2(sum(column_receive(it)))
        spread(change)
        for k in range(nz if last else 1):
            if k:
                theirs = pots.at[z_peer(k)]
                remote(
                    theirs, theirs, pot_ss.at[k], pot_rs.at[z_peer(k)], (partner, c)
                ).wait_recv()
            row_next(it, k, last)
            row_send(it, k)
        if not last:
            pots[z] = pots[z] - log_docs - jnp.log2(sum(row_receive(it, 0)))

    for copy in gone:
        copy.wait_send()
    wider = min(half, 256)

    def plane_plan(k):
        plane = z_peer(k)
        share[k] = 1.0 / sum(row_receive(ITERS - 1, k))
        block = emb_all[pl.ds(plane * nb, nb)].reshape(nb * rows, features)
        for g in range(half // wider):
            for i in range(wider // step):
                at = pl.ds(g * wider + i * step, step)
                acc = jnp.zeros((step, rows), F32)
                for b in range(nb):
                    p = scores[plane * nb + b, at, :] * share[k, pl.ds(b, 1), :]
                    plan[at, b * rows:(b + 1) * rows] = p.astype(jnp.bfloat16)
                    acc = acc + p
                total[at, :] = acc + total[at, :] if k else acc
            at = pl.ds(g * wider, wider)
            product = lax.dot_general(
                plan[at, :], block, (((1,), (0,)), ((), ())), preferred_element_type=F32
            )
            sums[at, :] = sums[at, :] + product if k else product

    for k in range(nz):
        plane_plan(k)

    everything = jnp.transpose(sums[...])
    scale = lax.rsqrt(jnp.sum(everything * everything, axis=0, keepdims=True) / features + 1e-06)
    finished[...] = everything * scale
    pairmass[0] = jnp.sum(jnp.transpose(total[...]), axis=0, keepdims=True) * (clusters / docs)

    def features_of(which):
        return finished.at[pl.ds(pl.multiple_of((2 * z + which) * own_f, own_f), own_f), :]

    send(features_of(other), pairbuf, pair_ss.at[0], pair_rs.at[0], (partner, c))
    send(pairmass.at[0], pairmass.at[1], pair_ss.at[1], pair_rs.at[1], (partner, c))
    columns = pl.ds(pl.multiple_of(core * half, half), half)
    out_ref[:, columns] = features_of(core)[...]
    mass_ref[:, columns] = pairmass[0]
    for copy in sends:
        copy.wait_send()
    columns = pl.ds(pl.multiple_of(other * half, half), half)
    remote(pairbuf, pairbuf, pair_ss.at[0], pair_rs.at[0], (partner, c)).wait_recv()
    out_ref[:, columns] = pairbuf[...]
    remote(
        pairmass.at[1], pairmass.at[1], pair_ss.at[1], pair_rs.at[1], (partner, c)
    ).wait_recv()
    mass_ref[:, columns] = pairmass[1]


def store_kernel(part_ref, mass_ref, out_ref, total_ref):
    out_ref[...] = part_ref[...]
    total_ref[...] = mass_ref[...].reshape(total_ref.shape)


def replicated(nd, nc, embeddings, centroids):
    rows, features = embeddings.shape
    own_cols = centroids.shape[0]
    half, nz, nb = own_cols // 2, nd // 2, 2 * nc
    own_f = features // nd
    dma = pltpu.SemaphoreType.DMA
    out, mass = pl.pallas_call(
        functools.partial(replicated_kernel, nd, nc),
        out_shape=(
            jax.ShapeDtypeStruct((own_f, own_cols), F32),
            jax.ShapeDtypeStruct((1, own_cols), F32),
        ),
        in_specs=[pl.BlockSpec(memory_space=pltpu.HBM)] * 2,
        out_specs=(pl.BlockSpec(memory_space=pltpu.VMEM),) * 2,
        scratch_shapes=[
            pltpu.VMEM((nz * nb, rows, features), jnp.bfloat16),
            pltpu.VMEM((half, features), jnp.bfloat16),
            pltpu.VMEM((nz * nb, half, rows), F32),
            pltpu.VMEM((half, nb * rows), jnp.bfloat16),
            pltpu.VMEM((half, rows), F32),
            pltpu.VMEM((half, rows), F32),
            pltpu.VMEM((half, rows), F32),
            pltpu.VMEM((nz, nb, rows), F32),
            pltpu.VMEM((nz, nb, rows), F32),
            pltpu.VMEM((ITERS, nz, 1, half), F32),
            pltpu.VMEM((ITERS, nz, nb, nb, rows), F32),
            pltpu.VMEM((half, features), F32),
            pltpu.VMEM((features, half), F32),
            pltpu.VMEM((own_f, half), F32),
            pltpu.VMEM((2, 1, half), F32),
            dma, dma, dma((nz,)), dma((nz * nb,)), dma((nz * nc,)), dma((nz, nc)),
            dma((ITERS, nz)), dma((ITERS, nz)), dma((ITERS, nz, nb)), dma((ITERS, nz, nb)),
            dma((nz,)), dma((nz,)), dma((2,)), dma((2,)),
        ],
        compiler_params=pltpu.CompilerParams(
            collective_id=0, has_side_effects=True, vmem_limit_bytes=VMEM_BYTES
        ),
    )(*(pltpu.with_memory_space_constraint(a, pltpu.HBM) for a in (embeddings, centroids)))
    return pl.pallas_call(
        store_kernel,
        out_shape=(
            jax.ShapeDtypeStruct((own_f, own_cols), F32),
            jax.ShapeDtypeStruct((own_cols,), F32),
        ),
        in_specs=[pl.BlockSpec(memory_space=pltpu.VMEM)] * 2,
        out_specs=(pl.BlockSpec(memory_space=pltpu.VMEM),) * 2,
        compiler_params=pltpu.CompilerParams(vmem_limit_bytes=4 << 20),
    )(out, mass)


VMEM_BYTES = 48 << 20


def local(nd, nc, embeddings, centroids):
    rows, features = embeddings.shape
    docs = rows * nd * nc
    half = centroids.shape[0] // 2
    held = docs * (2 * features + 4 * half)
    fits = 2 * held <= VMEM_BYTES and nd > 2 and nc > 1 and not nc & (nc - 1)
    form = replicated if fits else scattered
    return form(nd, nc, embeddings, centroids)


def solution(mesh):
    placed = (P(("doc", "clu"), None), P("clu", None))
    body = functools.partial(local, mesh.shape["doc"], mesh.shape["clu"])
    return jax.shard_map(
        body, mesh=mesh, in_specs=placed, out_specs=(P("doc", "clu"), P("clu")), check_vma=False
    )
```
